32 devices in a mesh: gx: 2 (over core), yz: 16 (over z, y, x).
Axes of the slice: x: 2, y: 2, z: 4, core: 2. Of those that a mesh axis runs over, the one named last changes fastest.
Arguments:
- features_in: bfloat16 [16, 32, 24, 144], P('yz', None, 'gx'), may hold values from -6 to 6
- encode_fine_first: bfloat16 [32, 864], replicated, may hold values from -0.3125 to 0.3125
- encode_fine_second: bfloat16 [32, 864], replicated, may hold values from -0.3125 to 0.3125
- reduce_fine: bfloat16 [64, 256], replicated, may hold values from -0.5 to 0.5
- encode_middle_first: bfloat16 [64, 1728], replicated, may hold values from -0.21875 to 0.21875
- encode_middle_second: bfloat16 [64, 1728], replicated, may hold values from -0.21875 to 0.21875
- reduce_middle: bfloat16 [256, 512], replicated, may hold values from -0.375 to 0.375
- bottom_first: bfloat16 [1024, 1728], P('yz'), may hold values from -0.109375 to 0.109375
- bottom_second: bfloat16 [1024, 1728], P('yz'), may hold values from -0.109375 to 0.109375
- expand_middle: bfloat16 [256, 512], replicated, may hold values from -0.5 to 0.5
- decode_middle_first: bfloat16 [64, 1728], replicated, may hold values from -0.21875 to 0.21875
- decode_middle_second: bfloat16 [64, 1728], replicated, may hold values from -0.21875 to 0.21875
- expand_fine: bfloat16 [64, 256], replicated, may hold values from -1 to 1
- decode_fine_first: bfloat16 [32, 864], replicated, may hold values from -0.3125 to 0.3125
- decode_fine_second: bfloat16 [32, 864], replicated, may hold values from -0.3125 to 0.3125
Outputs:
- features_out: bfloat16 [16, 32, 24, 144], P('yz', None, 'gx')
The draws below stay inside these ranges and needn't reach their ends.
All inputs are finite; a program needn't handle non-finite values.
Results may differ from the reference program's by a relative error of at most 0.023.
Values may be sent and summed in bfloat16 or wider, within the bound.
No kernel may reach another device: no remote copies, remote signals or barrier semaphores. Data moves between devices by JAX's collectives and lax.ppermute only.
A program may use at most 128 MiB of HBM per device.

```python
import math
import jax
import jax.numpy as jnp
from jax import lax

C0 = 12
CH0 = 32
CH1 = 64
CB = 256
NX = 24
N_YZ = 16


def level_of(key, shape, split, low, high):
    level, own = 1.0, jax.random.fold_in(key, 6)
    for dim, shards_of in split:
        heights = jnp.exp(jax.random.uniform(jax.random.fold_in(own, dim), (shards_of,), jnp.float32, low / len(split), high / len(split)))
        level = level * jnp.repeat(heights, shape[dim] // shards_of).reshape([-1 if axis == dim else 1 for axis in range(len(shape))])
    return level


def gaussian(rng, shape, scale, limit, pieces=(), kind=jnp.bfloat16):
    array = scale * jax.random.normal(rng, shape, jnp.float32)
    if pieces:
        array = array * level_of(rng, shape, pieces, -0.22, 0.18)
    return jnp.clip(array, -limit, limit).astype(kind)


def setup_inputs(seed: int = 0) -> dict:
    splits = jax.random.split(jax.random.key(seed), 16)
    features_in = gaussian(splits[0], (N_YZ, CH0, NX, C0 * C0), 1.0, 6.0, ((0, 16), (2, 2)))
    encode_fine_first = gaussian(splits[1], (CH0, CH0 * 27), (CH0 * 27 // 2) ** -0.5, 0.3125)
    encode_fine_second = gaussian(splits[2], (CH0, CH0 * 27), (CH0 * 27 // 2) ** -0.5, 0.3125)
    reduce_fine = gaussian(splits[3], (CH1, CH0 * 8), (CH0 * 4) ** -0.5, 0.5)
    encode_middle_first = gaussian(splits[4], (CH1, CH1 * 27), (CH1 * 27 // 2) ** -0.5, 0.21875)
    encode_middle_second = gaussian(splits[5], (CH1, CH1 * 27), (CH1 * 27 // 2) ** -0.5, 0.21875)
    reduce_middle = gaussian(splits[6], (CB, CH1 * 8), (CH1 * 4) ** -0.5, 0.375)
    bottom_first = gaussian(splits[7], (4 * CB, CB * 27 // 4), (CB * 27 // 2) ** -0.5, 0.109375, ((0, 16),))
    bottom_second = gaussian(splits[8], (4 * CB, CB * 27 // 4), (CB * 27 // 2) ** -0.5, 0.109375, ((0, 16),))
    expand_middle = gaussian(splits[9], (CB, CH1 * 8), (CB // 2) ** -0.5, 0.5)
    decode_middle_first = gaussian(splits[10], (CH1, CH1 * 27), (CH1 * 27 // 2) ** -0.5, 0.21875)
    decode_middle_second = gaussian(splits[11], (CH1, CH1 * 27), (CH1 * 27 // 2) ** -0.5, 0.21875)
    expand_fine = gaussian(splits[12], (CH1, CH0 * 8), (CH1 // 2) ** -0.5, 1.0)
    decode_fine_first = gaussian(splits[13], (CH0, CH0 * 27), (CH0 * 27 // 2) ** -0.5, 0.3125)
    decode_fine_second = gaussian(splits[14], (CH0, CH0 * 27), (CH0 * 27 // 2) ** -0.5, 0.3125)
    return {"features_in": features_in, "encode_fine_first": encode_fine_first, "encode_fine_second": encode_fine_second, "reduce_fine": reduce_fine, "encode_middle_first": encode_middle_first, "encode_middle_second": encode_middle_second, "reduce_middle": reduce_middle, "bottom_first": bottom_first, "bottom_second": bottom_second, "expand_middle": expand_middle, "decode_middle_first": decode_middle_first, "decode_middle_second": decode_middle_second, "expand_fine": expand_fine, "decode_fine_first": decode_fine_first, "decode_fine_second": decode_fine_second}


def to_volume(packed, across):
    count, width, extent_x, flat = packed.shape
    extent = math.isqrt(flat)
    shaped = packed.reshape(across, across, width, extent_x, extent, extent)
    return shaped.transpose(2, 3, 0, 4, 1, 5).reshape(width, extent_x, across * extent, across * extent)

def from_volume(volume, across):
    width, extent_x, extent_y, extent_z = volume.shape
    extent = extent_y // across
    shaped = volume.reshape(width, extent_x, across, extent, across, extent)
    return shaped.transpose(2, 4, 0, 1, 3, 5).reshape(across * across, width, extent_x, extent * extent)

def conv_taps(padded, weight, width_in):
    kernel = weight.reshape(weight.shape[0], width_in, 3, 3, 3)
    return lax.conv_general_dilated(padded[None], kernel, (1, 1, 1), 'VALID', dimension_numbers=('NCDHW', 'OIDHW', 'NCDHW'), preferred_element_type=jnp.float32)[0]

def conv_layer(volume, weight):
    padded = jnp.pad(volume, ((0, 0), (1, 1), (1, 1), (1, 1)), mode='wrap')
    return jnp.maximum(conv_taps(padded, weight, volume.shape[0]), 0.0).astype(jnp.bfloat16)

def full_weight(stored):
    width_out = stored.shape[0] // 4
    return stored.reshape(4, width_out, stored.shape[1]).transpose(1, 0, 2).reshape(width_out, 4 * stored.shape[1])

def shrink(volume, weight):
    kernel = weight.reshape(weight.shape[0], volume.shape[0], 2, 2, 2)
    result = lax.conv_general_dilated(volume[None], kernel, (2, 2, 2), 'VALID', dimension_numbers=('NCDHW', 'OIDHW', 'NCDHW'), preferred_element_type=jnp.float32)[0]
    return result.astype(jnp.bfloat16)

def expand(volume, weight, skipped):
    width_in, extent_x, extent_y, extent_z = volume.shape
    width_out = weight.shape[1] // 8
    columns = lax.dot_general(weight, volume.reshape(width_in, -1), (((0,), (0,)), ((), ())), preferred_element_type=jnp.float32)
    spread = columns.reshape(width_out, 2, 2, 2, extent_x, extent_y, extent_z).transpose(0, 4, 1, 5, 2, 6, 3)
    spread = spread.reshape(width_out, 2 * extent_x, 2 * extent_y, 2 * extent_z)
    return (spread + skipped.astype(jnp.float32)).astype(jnp.bfloat16)

def reference(features_in, encode_fine_first, encode_fine_second, reduce_fine, encode_middle_first, encode_middle_second, reduce_middle, bottom_first, bottom_second, expand_middle, decode_middle_first, decode_middle_second, expand_fine, decode_fine_first, decode_fine_second):
    across = math.isqrt(N_YZ)
    volume = to_volume(features_in, across)
    fine_skip = conv_layer(conv_layer(volume, encode_fine_first), encode_fine_second)
    middle = shrink(fine_skip, reduce_fine)
    middle_skip = conv_layer(conv_layer(middle, encode_middle_first), encode_middle_second)
    bottom = shrink(middle_skip, reduce_middle)
    bottom = conv_layer(conv_layer(bottom, full_weight(bottom_first)), full_weight(bottom_second))
    rising = expand(bottom, expand_middle, middle_skip)
    rising = conv_layer(conv_layer(rising, decode_middle_first), decode_middle_second)
    rising = expand(rising, expand_fine, fine_skip)
    rising = conv_layer(conv_layer(rising, decode_fine_first), decode_fine_second)
    return from_volume(rising, across)
```

```python
import functools
import math

import jax
import jax.numpy as jnp
from jax import lax
from jax.experimental import pallas as pl
from jax.experimental.pallas import tpu as pltpu
from jax.sharding import PartitionSpec as P

BF = jnp.bfloat16
F32 = jnp.float32
LANES = 256


def dot(a, b):
    return lax.dot_general(a, b, (((1,), (0,)), ((), ())), preferred_element_type=F32)


def banded(table, weight, count, depth, wide_in, wide_out, cells, target):
    lane = lax.broadcasted_iota(jnp.int32, (wide_in, LANES), 1)
    spread = (
        lax.broadcasted_iota(jnp.int32, (wide_out, LANES), 0)
        == lax.broadcasted_iota(jnp.int32, (wide_out, LANES), 1) % wide_out
    ).astype(BF)
    cell_out = lane // wide_out
    rows = depth * wide_in

    def one(t, carry):
        taps = dot(weight[pl.ds(pl.multiple_of(t * rows, rows), rows), :], spread)
        for cell in range(cells):
            value = jnp.zeros((wide_in, LANES), F32)
            for k in range(depth):
                out = target(cell, k)
                if isinstance(out, int) and not 0 <= out < LANES // wide_out:
                    continue
                if out is None:
                    continue
                value = jnp.where(
                    cell_out == out, taps[k * wide_in : (k + 1) * wide_in], value
                )
            table[t, cell * wide_in : (cell + 1) * wide_in, :] = value.astype(BF)
        return carry

    lax.fori_loop(0, count, one, 0)


def conv_table(table, weight, channels):
    banded(table, weight, 9, 3, channels, channels, 384 // channels, lambda z, k: z - k)


def halved(offset):
    return lambda z, k: (z - offset - k) // 2 if (z - offset - k) % 2 == 0 else None


def doubled(offset):
    return lambda z, k: 2 * (z - offset) + k


def stage(wide, shifted, layers, rows, first):
    width = min(shifted.shape[2], wide.shape[2])
    for y in range(layers):
        for d in range(3):
            shifted[d, y * rows : (y + 1) * rows, :width] = wide[
                y, first + d : first + d + rows, :width
            ].astype(BF)


def convolve(shifted, table, layers, rows, tile, depth=384, width=LANES):
    height = layers * rows
    start = tile * LANES
    left = jnp.concatenate(
        [
            shifted[dx, dy * rows : dy * rows + height, start : start + depth]
            for dy in range(3)
            for dx in range(3)
        ],
        axis=1,
    )
    return dot(left, table[:, :depth, :width].reshape(9 * depth, width))


def rounded_relu(value):
    return jnp.maximum(value, 0.0).astype(BF)


def fine_encoder(low, mid, high, first, second, reduce, skip, small, wide, s1, s2, table, halves):
    layers, across = mid.shape[0], mid.shape[1]
    wide[:, :across, 0:128] = low[...].astype(F32)
    wide[:, :across, 128:512] = mid[...].astype(F32)
    wide[:, :across, 512:640] = high[...].astype(F32)
    stage(wide, s1, layers, 32, 0)
    conv_table(table, first, 32)
    inner = layers - 2
    for tile, depth, width in ((0, 384, 256), (1, 384, 256), (2, 128, 128)):
        value = rounded_relu(convolve(s1, table, inner, 32, tile, depth, width))
        wide[:inner, :32, tile * LANES : tile * LANES + width] = value.astype(F32).reshape(
            inner, 32, width
        )
    stage(wide, s2, inner, 16, 0)
    conv_table(table, second, 32)
    kept = inner - 2
    for tile in range(2):
        value = rounded_relu(convolve(s2, table, kept, 16, tile))
        skip[:, :, tile * LANES : (tile + 1) * LANES] = value.reshape(kept, 16, LANES)
    banded(table, reduce, 4, 2, 32, 64, 12, halved(2))
    count = small.shape[0]
    for tile, depth, width in ((0, 384, 256), (1, 256, 128)):
        for a in range(2):
            total = 0.0
            for b in range(2):
                left = jnp.concatenate(
                    [
                        skip[2 + 2 * y + b, :, tile * LANES : tile * LANES + depth]
                        for y in range(count)
                    ],
                    axis=0,
                )
                total = total + dot(left, table[2 * a + b, :depth, :width])
            for part in range(width // 128):
                halves[2 * a + part] = total[:, 128 * part : 128 * part + 128]
        for y in range(count):
            for part in range(width // 128):
                value = halves[part, pl.ds(16 * y + 2, count, 2), :]
                value = value + halves[2 + part, pl.ds(16 * y + 3, count, 2), :]
                lanes = tile * LANES + 128 * part
                small[y, :, lanes : lanes + 128] = value.astype(BF)


def wrap_rows(wide, layers, count):
    wide[1 : layers + 1, 7:8, :] = wide[1 : layers + 1, 7 + count : 8 + count, :]
    wide[1 : layers + 1, 8 + count : 9 + count, :] = wide[1 : layers + 1, 8:9, :]
    wide[0:1] = wide[layers : layers + 1]
    wide[layers + 1 : layers + 2] = wide[1:2]


def middle(
    where, own, other, first, second, reduce, bottom, window, partial, wide, s, table, whole, halves
):
    across = math.isqrt(own.shape[0])
    side = own.shape[1]
    cells = side * across
    lanes = side * 64
    span = cells * 64
    for i in range(across):
        for place, j in enumerate([across - 1] + list(range(across))):
            start = place * lanes
            size = min(lanes, span + 128 - start)
            for part, gathered in enumerate((own, other)):
                wide[
                    1 + side * i : 1 + side * (i + 1),
                    8 + side * part : 8 + side * (part + 1),
                    start : start + size,
                ] = gathered[i * across + j, :, :, :size].astype(F32)
    wrap_rows(wide, cells, 2 * side)
    stage(wide, s, cells + 2, 16, 7)
    conv_table(table, first, 64)
    for tile in range(span // LANES):
        value = rounded_relu(convolve(s, table, cells, 16, tile))
        wide[1 : cells + 1, 8:24, tile * LANES : (tile + 1) * LANES] = value.astype(F32).reshape(
            cells, 16, LANES
        )
    wide[:, :, span : span + 128] = wide[:, :, 0:128]
    wrap_rows(wide, cells, 2 * side)
    stage(wide, s, cells + 2, 16, 7)
    conv_table(table, second, 64)
    for tile in range(span // LANES):
        value = rounded_relu(convolve(s, table, cells, 16, tile))
        whole[3 : cells + 3, :, tile * LANES : (tile + 1) * LANES] = value.reshape(
            cells, 16, LANES
        )
    whole[0:3] = whole[cells : cells + 3]
    whole[cells + 3 : cells + 6] = whole[3:6]
    whole[:, :, span : span + 512] = whole[:, :, 0:512]
    row, column = where[0], where[1]
    window[...] = whole[
        pl.ds(row * side, window.shape[0]),
        :,
        pl.ds(pl.multiple_of(column * lanes, 128), window.shape[2]),
    ]
    half = cells // 2
    shrunk = half * 64
    banded(table, reduce, 4, 2, 64, 64, 6, halved(0))
    for tile in range(shrunk // LANES):
        for a in range(2):
            total = 0.0
            for b in range(2):
                left = jnp.concatenate(
                    [
                        whole[3 + 2 * y + b, :, tile * 512 : tile * 512 + 512]
                        for y in range(half)
                    ],
                    axis=0,
                )
                narrow = table[2 * a + b, :256, :128]
                total = total + jnp.concatenate(
                    [dot(left[:, :256], narrow), dot(left[:, 256:], narrow)], axis=1
                )
            for part in range(2):
                halves[2 * a + part] = total[:, 128 * part : 128 * part + 128]
        for y in range(half):
            for part in range(2):
                value = halves[part, pl.ds(16 * y, side, 2), :]
                value = value + halves[2 + part, pl.ds(16 * y + 1, side, 2), :]
                put = tile * LANES + 128 * part
                wide[1 + y, 8 : 8 + side, put : put + 128] = value.astype(BF).astype(F32)
    wide[1 : half + 1, 8 : 8 + side, shrunk : shrunk + 128] = wide[
        1 : half + 1, 8 : 8 + side, 0:128
    ]
    wrap_rows(wide, half, side)
    stage(wide, s, half + 2, 16, 7)
    conv_table(table, bottom, 64)
    for tile in range(shrunk // LANES):
        value = convolve(s, table, half, 16, tile).astype(BF).reshape(half, 16, LANES)
        partial[:, :, tile * LANES : (tile + 1) * LANES] = value[:, :8]


def bottom_second_kernel(p0, p1, p2, p3, weight, out, wide, s, table, whole):
    cells, _, span = p0.shape
    side = cells // 2
    across = math.isqrt(out.shape[0])
    total = p0[...].astype(F32) + p1[...].astype(F32) + p2[...].astype(F32) + p3[...].astype(F32)
    wide[1 : cells + 1, 8:16, :span] = jnp.maximum(total, 0.0).astype(BF).astype(F32)
    wide[1 : cells + 1, 8:16, span : span + 128] = wide[1 : cells + 1, 8:16, 0:128]
    wrap_rows(wide, cells, side)
    stage(wide, s, cells + 2, 16, 7)
    conv_table(table, weight, 64)
    for tile in range(span // LANES):
        value = convolve(s, table, cells, 16, tile).reshape(cells, 16, LANES)
        for part in range(2):
            put = tile * LANES + 128 * part + 128
            whole[2 : cells + 2, :, put : put + 128] = value[:, :8, 128 * part : 128 * part + 128]
    whole[0:2] = whole[cells : cells + 2]
    whole[cells + 2 : cells + 5] = whole[2:5]
    whole[:, :, 0:128] = whole[:, :, span : span + 128]
    whole[:, :, span + 128 : span + 512] = whole[:, :, 128:512]
    block = cells // across
    for i in range(across):
        for j in range(across):
            start = (block * j - block * j % 2) * 64
            out[i * across + j] = whole[
                block * i : block * i + out.shape[1], :, start : start + out.shape[3]
            ].astype(BF)


def decoder(
    where,
    parts,
    window,
    skip,
    up,
    m1,
    m2,
    up_fine,
    f1,
    f2,
    out,
    wide,
    s,
    table,
    up_table,
    columns,
    spread,
):
    across = math.isqrt(parts.shape[0])
    layers = parts.shape[1]
    odd = where[1] % 2
    banded(up_table, up, 16, 2, 64, 64, 4, doubled(odd))
    groups = []
    for group in range(across):
        total = 0.0
        for k in range(across):
            total = total + parts[k * across + group].astype(F32)
        columns[:layers, :8, :512] = jnp.maximum(total, 0.0)
        groups.append(columns[:layers, :, :512].astype(BF).reshape(layers * 16, 512))
    for tile, depth in ((0, 256), (1, 256), (2, 256), (3, 128)):
        for a in range(2):
            for b in range(2):
                left = jnp.concatenate(
                    [g[:, tile * 128 : tile * 128 + depth] for g in groups], axis=1
                )
                right = jnp.concatenate(
                    [up_table[4 * g + 2 * a + b, :depth, :] for g in range(across)], axis=0
                )
                value = dot(left, right)
                columns[:layers, :, :LANES] = value.reshape(layers, 16, LANES)
                for y in range(layers):
                    for part in range(2):
                        spread[2 * tile + part, 2 * y + b, pl.ds(8 + a, 6, 2), :] = columns[
                            y, 0:6, 128 * part : 128 * part + 128
                        ]
    span = window.shape[2]
    count = window.shape[0]
    for lanes in range(0, span, 128):
        total = spread[lanes // 128, 1 : count + 1, 8:24, :]
        total = total + window[:, :, lanes : lanes + 128].astype(F32)
        wide[1 : count + 1, 8:24, lanes : lanes + 128] = total.astype(BF).astype(F32)
    wide[:, 7:8, :] = wide[:, 19:20, :]
    wide[:, 20:21, :] = wide[:, 8:9, :]
    for y in range(count):
        for d in range(3):
            s[d, y * 16 : (y + 1) * 16, :span] = wide[y + 1, 7 + d : 23 + d, :span].astype(BF)
    conv_table(table, m1, 64)
    count = count - 2
    for tile in range(3):
        value = rounded_relu(convolve(s, table, count, 16, tile))
        wide[:count, 8:24, tile * LANES : (tile + 1) * LANES] = value.astype(F32).reshape(
            count, 16, LANES
        )
    wide[:, 7:8, :] = wide[:, 19:20, :]
    wide[:, 20:21, :] = wide[:, 8:9, :]
    stage(wide, s, count, 16, 7)
    conv_table(table, m2, 64)
    count = count - 2
    risen = []
    for tile, depth in ((0, 384), (1, 384), (2, 256)):
        risen.append(rounded_relu(convolve(s, table, count, 16, tile, depth)))
    risen = jnp.concatenate(risen, axis=1)
    banded(table, up_fine, 4, 2, 64, 32, 6, doubled(1))
    for tile in range(2):
        for a in range(2):
            for b in range(2):
                value = dot(risen[:, tile * LANES : tile * LANES + 384], table[2 * a + b])
                columns[:count, :, :LANES] = value.reshape(count, 16, LANES)
                for y in range(count):
                    for part in range(2):
                        group = 2 * tile + part
                        lanes = slice(128 * part, 128 * part + 128)
                        spread[group, 2 * y + b, pl.ds(2 + a, 7, 2), :] = columns[y, 0:7, lanes]
                        spread[group, 2 * y + b, a : a + 1, :] = columns[y, 11:12, lanes]
    count = 2 * count
    for lanes in range(0, skip.shape[2], 128):
        total = spread[lanes // 128, :count, 0:16, :]
        total = total + skip[:, :, lanes : lanes + 128].astype(F32)
        wide[:count, 0:16, lanes : lanes + 128] = total.astype(BF).astype(F32)
    for y in range(count):
        for d in range(3):
            s[d, y * 16 : (y + 1) * 16, 0:512] = wide[y, d : d + 16, 0:512].astype(BF)
    conv_table(table, f1, 32)
    count = count - 2
    for tile, depth in ((0, 384), (1, 256)):
        value = rounded_relu(convolve(s, table, count, 16, tile, depth))
        wide[:count, 0:16, tile * LANES : (tile + 1) * LANES] = value.astype(F32).reshape(
            count, 16, LANES
        )
    for y in range(count):
        for d in range(3):
            s[d, y * 16 : (y + 1) * 16, 0:512] = wide[y, d : d + 16, 0:512].astype(BF)
    conv_table(table, f2, 32)
    count = count - 2
    for tile, depth, width in ((0, 384, 256), (1, 256, 128)):
        value = rounded_relu(convolve(s, table, count, 16, tile, depth, width))
        out[:, :, tile * LANES : tile * LANES + width] = value.reshape(count, 16, width)


def conv_rows(weight, channels):
    split = weight.reshape(weight.shape[0], channels, 3, 3, 3)
    return split.transpose(3, 2, 4, 1, 0).reshape(27 * channels, weight.shape[0])


def call(kernel, outs, scratch, *args, scalars=0):
    spaces = [pltpu.SMEM] * scalars + [pltpu.VMEM] * (len(args) - scalars)
    return pl.pallas_call(
        kernel,
        out_shape=outs,
        in_specs=[pl.BlockSpec(memory_space=space) for space in spaces],
        out_specs=jax.tree.map(lambda _: pl.BlockSpec(memory_space=pltpu.VMEM), outs),
        scratch_shapes=scratch,
        name=kernel.__name__,
    )(*args)


def exchange(head, tail, axis, route):
    ahead = [(source, route(source, 1)) for source in range(lax.axis_size(axis))]
    back = [(source, route(source, -1)) for source in range(lax.axis_size(axis))]
    return lax.ppermute(tail, axis, ahead), lax.ppermute(head, axis, back)


def gathered_body(
    features_in,
    encode_fine_first,
    encode_fine_second,
    reduce_fine,
    encode_middle_first,
    encode_middle_second,
    reduce_middle,
    bottom_first,
    bottom_second,
    expand_middle,
    decode_middle_first,
    decode_middle_second,
    expand_fine,
    decode_fine_first,
    decode_fine_second,
):
    devices = lax.axis_size("yz")
    across = math.isqrt(devices)
    place = lax.axis_index("yz")
    row, column = place // across, place % across
    where = jnp.stack([row, column]).astype(jnp.int32)
    fine, ext = features_in.shape[1], features_in.shape[2]
    mid = encode_middle_first.shape[0]
    halo = 4

    def around(source, step):
        return (source + step) % lax.axis_size("gx")

    def along_y(source, step):
        return (source + step * across) % devices

    def along_z(source, step):
        return source // across * across + (source % across + step) % across

    cells = features_in.reshape(fine, ext, ext, ext).transpose(2, 1, 3, 0)
    cells = cells.reshape(ext, ext, ext * fine)
    low, high = exchange(cells[:, :halo], cells[:, ext - halo :], "gx", around)
    cells = jnp.concatenate([low, cells, high], axis=1)
    low, high = exchange(cells[:halo], cells[ext - halo :], "yz", along_y)
    cells = jnp.concatenate([low, cells, high], axis=0)
    edge = halo * fine
    low, high = exchange(cells[:, :, :edge], cells[:, :, -edge:], "yz", along_z)

    seen = ext + 2 * halo
    side = ext // 2
    skip, small = call(
        fine_encoder,
        (
            jax.ShapeDtypeStruct((ext + 4, ext + 4, (ext + 4) * fine), BF),
            jax.ShapeDtypeStruct((side, side, side * mid), BF),
        ),
        [
            pltpu.VMEM((seen, 40, 640), F32),
            pltpu.VMEM((3, seen * 32, 640), BF),
            pltpu.VMEM((3, (seen - 2) * 16, 640), BF),
            pltpu.VMEM((9, 384, LANES), BF),
            pltpu.VMEM((4, side * 16, 128), F32),
        ],
        low,
        cells,
        high,
        conv_rows(encode_fine_first, fine),
        conv_rows(encode_fine_second, fine),
        reduce_fine.reshape(mid, fine, 8).transpose(2, 1, 0).reshape(8 * fine, mid),
    )

    own = lax.all_to_all(jnp.broadcast_to(small[None], (devices, *small.shape)), "yz", 0, 0)
    other = lax.ppermute(own, "gx", [(s, around(s, 1)) for s in range(lax.axis_size("gx"))])

    total = side * across
    half = total // 2
    quarter = lax.dynamic_slice_in_dim(reduce_middle, row * mid, mid, 0)
    window, partial = call(
        middle,
        (
            jax.ShapeDtypeStruct((12, 16, 14 * mid), BF),
            jax.ShapeDtypeStruct((half, 8, half * mid), BF),
        ),
        [
            pltpu.VMEM((total + 2, 32, total * mid + 128), F32),
            pltpu.VMEM((3, (total + 2) * 16, total * mid + 128), BF),
            pltpu.VMEM((9, 384, LANES), BF),
            pltpu.VMEM((total + 6, 16, total * mid + 512), BF),
            pltpu.VMEM((4, half * 16, 128), F32),
        ],
        where,
        own,
        other,
        conv_rows(encode_middle_first, mid),
        conv_rows(encode_middle_second, mid),
        quarter.reshape(mid, mid, 8).transpose(2, 1, 0).reshape(8 * mid, mid),
        conv_rows(bottom_first, mid),
        scalars=1,
    )

    pieces = [
        lax.ppermute(
            partial,
            "yz",
            [
                (s, (s % across) * across + (s // across + turn) % across)
                for s in range(devices)
            ],
        )
        for turn in range(across)
    ]
    sent = call(
        bottom_second_kernel,
        jax.ShapeDtypeStruct((devices, 7, 8, 512), BF),
        [
            pltpu.VMEM((half + 2, 32, half * mid + 128), F32),
            pltpu.VMEM((3, (half + 2) * 16, half * mid + 128), BF),
            pltpu.VMEM((9, 384, LANES), BF),
            pltpu.VMEM((half + 5, 8, half * mid + 512), F32),
        ],
        *pieces,
        conv_rows(bottom_second, mid),
    )
    parts = lax.all_to_all(sent, "yz", 0, 0)

    up = expand_middle.reshape(across, mid, mid, 8).transpose(0, 3, 1, 2).reshape(-1, mid)
    up_fine = expand_fine.reshape(mid, fine, 8).transpose(2, 0, 1).reshape(8 * mid, fine)
    risen = call(
        decoder,
        jax.ShapeDtypeStruct((ext, 16, ext * fine), BF),
        [
            pltpu.VMEM((16, 32, 1024), F32),
            pltpu.VMEM((3, 256, 1024), BF),
            pltpu.VMEM((9, 384, LANES), BF),
            pltpu.VMEM((4 * across, LANES, LANES), BF),
            pltpu.VMEM((8, 16, 512), F32),
            pltpu.VMEM((8, 16, 32, 128), F32),
        ],
        where,
        parts,
        window,
        skip,
        up,
        conv_rows(decode_middle_first, mid),
        conv_rows(decode_middle_second, mid),
        up_fine,
        conv_rows(decode_fine_first, fine),
        conv_rows(decode_fine_second, fine),
        scalars=1,
    )
    risen = risen[:, :ext].reshape(ext, ext, ext, fine).transpose(3, 1, 0, 2)
    return risen.reshape(1, fine, ext, ext * ext)


def with_halo(cells, sides, width):
    for axis, dim in sides:
        count = lax.axis_size(axis)
        head = lax.slice_in_dim(cells, 0, width, axis=dim)
        tail = lax.slice_in_dim(cells, cells.shape[dim] - width, cells.shape[dim], axis=dim)
        cells = jnp.concatenate(
            [
                lax.ppermute(tail, axis, [(i, (i + 1) % count) for i in range(count)]),
                cells,
                lax.ppermute(head, axis, [((i + 1) % count, i) for i in range(count)]),
            ],
            axis=dim,
        )
    return cells


def shortened(x):
    return jax.tree.map(lambda a: a.astype(jnp.bfloat16) if a.dtype == jnp.float32 else a, x)


def from_behind(block, axis, distance):
    devices = range(lax.axis_size(axis))
    route = [((i - distance) % len(devices), i) for i in devices]
    return lax.ppermute(block, axis, route)


def conv_taps(padded, weight, width_in):
    kernel = weight.reshape(weight.shape[0], width_in, 3, 3, 3)
    return lax.conv_general_dilated(
        padded[None],
        kernel,
        (1, 1, 1),
        "VALID",
        dimension_numbers=("NCDHW", "OIDHW", "NCDHW"),
        preferred_element_type=jnp.float32,
    )[0]


def rectify(running):
    return jnp.maximum(running, 0.0).astype(jnp.bfloat16)


def shrink(region, weight):
    kernel = weight.reshape(weight.shape[0], region.shape[0], 2, 2, 2)
    result = lax.conv_general_dilated(
        region[None],
        kernel,
        (2, 2, 2),
        "VALID",
        dimension_numbers=("NCDHW", "OIDHW", "NCDHW"),
        preferred_element_type=jnp.float32,
    )[0]
    return result.astype(jnp.bfloat16)


def expand(region, weight, skipped):
    width_in, extent_x, extent_y, extent_z = region.shape
    width_out = weight.shape[1] // 8
    columns = lax.dot_general(
        weight,
        region.reshape(width_in, -1),
        (((0,), (0,)), ((), ())),
        preferred_element_type=jnp.float32,
    )
    spread = columns.reshape(width_out, 2, 2, 2, extent_x, extent_y, extent_z).transpose(
        0, 4, 1, 5, 2, 6, 3
    )
    spread = spread.reshape(width_out, 2 * extent_x, 2 * extent_y, 2 * extent_z)
    return (spread + skipped.astype(jnp.float32)).astype(jnp.bfloat16)


def x_margins(region):
    return with_halo(region, (("gx", 1),), 1)


def from_peer(plane, offset):
    return from_behind(shortened(plane), "yz", offset).astype(plane.dtype)


def pad_block(region, across):
    extended = x_margins(region)
    below_face = from_peer(extended[:, :, -1:, :], across)
    above_face = from_peer(extended[:, :, :1, :], -across)
    extended = jnp.concatenate([below_face, extended, above_face], axis=2)
    column = lax.axis_index("yz") % across
    last_plane = extended[:, :, :, -1:]
    first_plane = extended[:, :, :, :1]
    behind = jnp.where(column == 0, from_peer(last_plane, 1 - across), from_peer(last_plane, 1))
    ahead = jnp.where(
        column == across - 1, from_peer(first_plane, across - 1), from_peer(first_plane, -1)
    )
    return jnp.concatenate([behind, extended, ahead], axis=3)


def conv_layer(region, weight, across):
    return rectify(conv_taps(pad_block(region, across), weight, region.shape[0]))


def assemble(stored):
    width_out = stored.shape[0] // 4
    return (
        stored.reshape(4, width_out, stored.shape[1])
        .transpose(1, 0, 2)
        .reshape(width_out, 4 * stored.shape[1])
    )


def bottom_layer(region, weight, across):
    width_in = region.shape[0]
    padded = pad_block(region, across)
    gathered = lax.all_gather(weight, "yz", axis=0, tiled=True)
    return rectify(conv_taps(padded, assemble(gathered), width_in))


def body(
    features_in,
    encode_fine_first,
    encode_fine_second,
    reduce_fine,
    encode_middle_first,
    encode_middle_second,
    reduce_middle,
    bottom_first,
    bottom_second,
    expand_middle,
    decode_middle_first,
    decode_middle_second,
    expand_fine,
    decode_fine_first,
    decode_fine_second,
):
    across = math.isqrt(lax.axis_size("yz"))
    width_fine, extent = (features_in.shape[1], features_in.shape[2])
    region = features_in.reshape(width_fine, extent, extent, extent)
    fine_skip = conv_layer(
        conv_layer(region, encode_fine_first, across), encode_fine_second, across
    )
    middle = shrink(fine_skip, reduce_fine)
    middle_skip = conv_layer(
        conv_layer(middle, encode_middle_first, across), encode_middle_second, across
    )
    bottom = shrink(middle_skip, reduce_middle)
    bottom = bottom_layer(bottom_layer(bottom, bottom_first, across), bottom_second, across)
    rising = expand(bottom, expand_middle, middle_skip)
    rising = conv_layer(
        conv_layer(rising, decode_middle_first, across), decode_middle_second, across
    )
    rising = expand(rising, expand_fine, fine_skip)
    rising = conv_layer(conv_layer(rising, decode_fine_first, across), decode_fine_second, across)
    return rising.reshape(1, width_fine, extent, extent * extent)


def solution(mesh):
    placed = (
        P("yz", None, "gx", None),
        P(),
        P(),
        P(),
        P(),
        P(),
        P(),
        P("yz", None),
        P("yz", None),
        P(),
        P(),
        P(),
        P(),
        P(),
        P(),
    )

    def chosen(*args):
        across = math.isqrt(lax.axis_size("yz"))
        stored, channels = args[7].shape[0], args[4].shape[0]
        gathered = lax.axis_size("gx") == 2 and stored == channels and across * channels == args[6].shape[0]
        return (gathered_body if gathered else body)(*args)

    return jax.shard_map(
        chosen, mesh=mesh, in_specs=placed, out_specs=P("yz", None, "gx", None), check_vma=False
    )
```

```python
import math

import jax
import jax.numpy as jnp
from jax import lax
from jax.experimental import pallas as pl
from jax.experimental.pallas import tpu as pltpu
from jax.sharding import PartitionSpec as P

BF = jnp.bfloat16
F32 = jnp.float32
LANES = 128
DEPTH = 256


def dot(a, b):
    return lax.dot_general(a, b, (((1,), (0,)), ((), ())), preferred_element_type=F32)


def lane_group(rows, width):
    return lax.broadcasted_iota(jnp.int32, (rows, LANES), 1) // width


def transposed(flat, weight):
    columns = weight.shape[1]
    copies = jnp.concatenate([weight.astype(F32)] * (LANES // weight.shape[0]), axis=0)
    for start in range(0, columns, LANES):
        stop = min(start + LANES, columns)
        flat[start:stop, :] = copies[:, start:stop].T


def blocks(taps, cells, wide_in, wide_out, target):
    group = lane_group(wide_in, wide_out)
    for cell in range(cells):
        value = jnp.zeros((wide_in, LANES), F32)
        for k, tap in enumerate(taps):
            out = target(cell, k)
            if out is not None and 0 <= out < LANES // wide_out:
                value = jnp.where(group == out, tap, value)
        yield cell * wide_in, value.astype(BF)


def conv_table(table, flat, weight, channels):
    transposed(flat, weight)
    for dy in range(3):
        for dx in range(3):
            taps = [flat[pl.ds(9 * dx + 3 * dy + dz, channels, 27), :] for dz in range(3)]
            for row, block in blocks(
                taps, DEPTH // channels, channels, channels, lambda z, k: z - k
            ):
                table[3 * dy + dx, row : row + channels, :] = block


def shrink_table(table, flat, weight, channels, offset):
    transposed(flat, weight)

    def target(z, k):
        return (z - offset - k) // 2 if (z - offset - k) % 2 == 0 else None

    for dx in range(2):
        for dy in range(2):
            taps = [flat[pl.ds(4 * dx + 2 * dy + dz, channels, 8), :] for dz in range(2)]
            for row, block in blocks(
                taps, DEPTH // channels, channels, weight.shape[0], target
            ):
                row += DEPTH * dy
                table[row : row + channels, LANES * dx : LANES * (dx + 1)] = block


def picked(weight, dx, dy, channels):
    rows = weight.shape[1]
    lane = lax.broadcasted_iota(jnp.int32, (rows, LANES), 1) % (2 * channels)
    row = lax.broadcasted_iota(jnp.int32, (rows, LANES), 0)
    wanted = 8 * (lane % channels) + 4 * dx + 2 * dy + lane // channels
    return dot(weight, (row == wanted).astype(BF))


def stage(wide, shifted, layers, rows, first, width, base=0):
    for y in range(layers):
        for d in range(3):
            shifted[d, y * rows : (y + 1) * rows, :width] = wide[
                base + y, first + d : first + d + rows, :width
            ].astype(BF)


def convolve(shifted, table, layers, rows, tile, depth=DEPTH):
    height = layers * rows
    start = tile * LANES
    left = jnp.concatenate(
        [
            shifted[dx, dy * rows : dy * rows + height, start : start + depth]
            for dy in range(3)
            for dx in range(3)
        ],
        axis=1,
    )
    return dot(left, table[:, :depth, :].reshape(9 * depth, LANES))


def rounded_relu(value):
    return jnp.maximum(value, 0.0).astype(BF)


def span_of(tile):
    return slice(tile * LANES, (tile + 1) * LANES)


def fine_encoder(
    low, mid, high, first, second, reduce, skip, small, wide, s1, s2, table, flat, down, halves, flats
):
    layers, width = mid.shape[0], mid.shape[2]
    start = 0
    for piece in (low, mid, high):
        wide[:, start : start + piece.shape[1], :] = piece[...].astype(F32)
        start += piece.shape[1]
    stage(wide, s1, layers, 32, 0, width)
    conv_table(table, flat, first[...], 32)
    inner = layers - 2
    tiles = width // LANES
    for tile in range(tiles):
        depth = DEPTH if tile + 1 < tiles else LANES
        value = rounded_relu(convolve(s1, table, inner, 32, tile, depth))
        wide[:inner, :32, span_of(tile)] = value.astype(F32).reshape(inner, 32, LANES)
    stage(wide, s2, inner, 16, 0, width)
    conv_table(table, flat, second[...], 32)
    kept = inner - 2
    for tile in range(tiles - 1):
        value = rounded_relu(convolve(s2, table, kept, 16, tile))
        skip[:, :, span_of(tile)] = value.reshape(kept, 16, LANES)
    shrink_table(down, flat, reduce[...], 32, 2)
    count = (kept - 4) // 2
    for tile in range(count // 2):
        left = jnp.concatenate(
            [
                jnp.concatenate(
                    [
                        skip[2 + 2 * y + dy, :, tile * LANES : tile * LANES + DEPTH]
                        for y in range(count)
                    ],
                    axis=0,
                )
                for dy in range(2)
            ],
            axis=1,
        )
        total = dot(left, down[...])
        halves[0] = total[:, :LANES]
        halves[1] = total[:, LANES:]
        for y in range(count):
            value = halves[0, pl.ds(16 * y + 2, count, 2), :]
            value = value + halves[1, pl.ds(16 * y + 3, count, 2), :]
            flats[count * y : count * (y + 1), span_of(tile)] = value
    result = flats[...].astype(BF)
    for copy in range(small.shape[0]):
        small[copy] = result


def wrap_rows(wide, layers, count):
    wide[1 : layers + 1, 7:8, :] = wide[1 : layers + 1, 7 + count : 8 + count, :]
    wide[1 : layers + 1, 8 + count : 9 + count, :] = wide[1 : layers + 1, 8:9, :]
    wide[0:1] = wide[layers : layers + 1]
    wide[layers + 1 : layers + 2] = wide[1:2]


def middle(
    where,
    own,
    other,
    first,
    second,
    reduce,
    turned,
    swapped,
    window,
    partial,
    wide,
    s,
    table,
    flat,
    down,
    whole,
    halves,
    flats,
):
    across = math.isqrt(own.shape[0])
    side = math.isqrt(own.shape[1])
    cells = side * across
    lanes = side * 64
    span = cells * 64
    row, column = where[0], where[1]
    for i in range(across):
        for place, j in enumerate([across - 1] + list(range(across))):
            start = place * lanes
            size = min(lanes, span + LANES - start)
            for part, gathered in enumerate((own, other)):
                block = gathered[i * across + j, :, :size].astype(F32)
                for y in range(side):
                    wide[
                        1 + side * i + y,
                        8 + side * part : 8 + side * (part + 1),
                        start : start + size,
                    ] = block[side * y : side * (y + 1)]
    wrap_rows(wide, cells, 2 * side)
    stage(wide, s, cells + 2, 16, 7, span + LANES)
    conv_table(table, flat, first[...], 64)
    for tile in range(span // LANES):
        value = rounded_relu(convolve(s, table, cells, 16, tile))
        wide[1 : cells + 1, 8:24, span_of(tile)] = value.astype(F32).reshape(cells, 16, LANES)
    wide[:, :, span : span + LANES] = wide[:, :, 0:LANES]
    wrap_rows(wide, cells, 2 * side)
    stage(wide, s, cells + 2, 16, 7, span + LANES)
    conv_table(table, flat, second[...], 64)
    for tile in range(span // LANES):
        value = rounded_relu(convolve(s, table, cells, 16, tile))
        whole[3 : cells + 3, :, span_of(tile)] = value.reshape(cells, 16, LANES)
    whole[0:3] = whole[cells : cells + 3]
    whole[cells + 3 : cells + 6] = whole[3:6]
    whole[:, :, span : span + 512] = whole[:, :, 0:512]
    window[...] = whole[
        pl.ds(row * side, window.shape[0]),
        :,
        pl.ds(pl.multiple_of(column * lanes, LANES), window.shape[2]),
    ]
    half = cells // 2
    shrunk = half * 64
    quarter = reduce[pl.ds(pl.multiple_of(column * 64, 64), 64), :]
    shrink_table(down, flat, quarter, 64, 0)
    for tile in range(shrunk // LANES):
        left = jnp.concatenate(
            [
                jnp.concatenate(
                    [
                        whole[3 + 2 * y + dy, :, tile * DEPTH : (tile + 1) * DEPTH]
                        for y in range(half)
                    ],
                    axis=0,
                )
                for dy in range(2)
            ],
            axis=1,
        )
        total = dot(left, down[...])
        halves[0] = total[:, :LANES]
        halves[1] = total[:, LANES:]
        for y in range(half):
            value = halves[0, pl.ds(16 * y, side, 2), :]
            value = value + halves[1, pl.ds(16 * y + 1, side, 2), :]
            wide[1 + y, 8 : 8 + side, span_of(tile)] = value.astype(BF).astype(F32)
    wide[1 : half + 1, 8 : 8 + side, shrunk : shrunk + LANES] = wide[
        1 : half + 1, 8 : 8 + side, 0:LANES
    ]
    wrap_rows(wide, half, side)
    stage(wide, s, half + 2, 16, 7, shrunk + LANES)
    mine, theirs = turned[...].astype(F32), swapped[...].astype(F32)
    is_first = where[2] == 0
    stored = jnp.concatenate(
        [jnp.where(is_first, mine, theirs), jnp.where(is_first, theirs, mine)], axis=0
    )
    conv_table(table, flat, stored, 64)
    for tile in range(shrunk // LANES):
        value = convolve(s, table, half, 16, tile)
        for y in range(half):
            flats[side * y : side * (y + 1), span_of(tile)] = value[16 * y : 16 * y + side]
    partial[...] = flats[...].astype(BF)


def bottom(*refs):
    *pieces, weight, out, wide, s, table, flat, whole, flats = refs
    span = pieces[0].shape[1]
    cells = span // 64
    side = cells // 2
    across = math.isqrt(out.shape[0])
    total = 0.0
    for piece in pieces:
        total = total + piece[...].astype(F32)
    total = jnp.maximum(total, 0.0).astype(BF).astype(F32)
    for y in range(cells):
        wide[1 + y, 8 : 8 + side, :span] = total[side * y : side * (y + 1)]
    wide[1 : cells + 1, 8 : 8 + side, span : span + LANES] = wide[
        1 : cells + 1, 8 : 8 + side, 0:LANES
    ]
    wrap_rows(wide, cells, side)
    stage(wide, s, cells + 2, 16, 7, span + LANES)
    conv_table(table, flat, weight[...], 64)
    for tile in range(span // LANES):
        value = convolve(s, table, cells, 16, tile).reshape(cells, 16, LANES)
        whole[2 : cells + 2, :, span_of(tile + 1)] = value[:, :8]
    whole[0:2] = whole[cells : cells + 2]
    whole[cells + 2 : cells + 5] = whole[2:5]
    whole[:, :, 0:LANES] = whole[:, :, span : span + LANES]
    whole[:, :, span + LANES : span + 512] = whole[:, :, LANES:512]
    block = cells // across
    kept = side // 2
    layers = out.shape[1] // kept
    for i in range(across):
        for j in range(across):
            start = (block * j - block * j % 2) * 64
            for y in range(layers):
                flats[kept * y : kept * (y + 1), :] = whole[
                    block * i + y, 0:kept, start : start + out.shape[2]
                ]
            out[i * across + j] = flats[...].astype(BF)


def decoder(
    where,
    near,
    far,
    window,
    skip,
    up,
    m1,
    m2,
    up_fine,
    f1,
    f2,
    out,
    wide,
    s,
    table,
    flat,
    lift,
    columns,
    spread,
):
    across = math.isqrt(near.shape[0])
    kept = window.shape[0] // 4
    layers = near.shape[1] // kept
    odd = where[1] % 2
    for dx in range(2):
        for dy in range(2):
            pair = picked(up[...], dx, dy, 64)
            blank = jnp.zeros((64, LANES), BF)
            for group in range(across):
                value = pair[64 * group : 64 * (group + 1)]
                for cell in range(4):
                    for half in range(2):
                        block = blank
                        if cell - half in (0, 1):
                            block = jnp.where(odd == cell - half, value, 0.0).astype(BF)
                        row = DEPTH * group + 64 * cell
                        lift[2 * dx + dy, row : row + 64, span_of(half)] = block
    groups = []
    for group in range(across):
        for part, parts in enumerate((near, far)):
            total = 0.0
            for k in range(across):
                total = total + parts[k * across + group].astype(F32)
            total = jnp.maximum(total, 0.0)
            for y in range(layers):
                columns[y, kept * part : kept * (part + 1), :512] = total[
                    kept * y : kept * (y + 1)
                ]
        groups.append(
            jnp.concatenate(
                [
                    columns[:layers, :, :512].astype(BF).reshape(layers * 16, 512),
                    jnp.zeros((layers * 16, LANES), BF),
                ],
                axis=1,
            )
        )
    for tile in range(4):
        left = jnp.concatenate(
            [g[:, tile * LANES : tile * LANES + DEPTH] for g in groups], axis=1
        )
        for dx in range(2):
            for dy in range(2):
                value = dot(left, lift[2 * dx + dy])
                for y in range(layers):
                    for half in range(2):
                        spread[2 * tile + half, 2 * y + dy, pl.ds(8 + dx, 2 * kept, 2), :] = value[
                            16 * y : 16 * y + 2 * kept, span_of(half)
                        ]
    count = window.shape[0]
    for tile in range(window.shape[2] // LANES):
        total = spread[tile, 1 : count + 1, 8:24, :] + window[:, :, span_of(tile)].astype(F32)
        wide[:count, 8:24, span_of(tile)] = total.astype(BF).astype(F32)
    ends = 8 + count
    wide[:, 7:8, :] = wide[:, ends - 1 : ends, :]
    wide[:, ends : ends + 1, :] = wide[:, 8:9, :]
    stage(wide, s, count, 16, 7, window.shape[2])
    conv_table(table, flat, m1[...], 64)
    count = count - 2
    for tile in range(6):
        value = rounded_relu(convolve(s, table, count, 16, tile))
        wide[:count, 8:24, span_of(tile)] = value.astype(F32).reshape(count, 16, LANES)
    wide[:, 7:8, :] = wide[:, ends - 1 : ends, :]
    wide[:, ends : ends + 1, :] = wide[:, 8:9, :]
    stage(wide, s, count, 16, 7, 6 * LANES)
    conv_table(table, flat, m2[...], 64)
    count = count - 2
    risen = jnp.concatenate(
        [rounded_relu(convolve(s, table, count, 16, tile)) for tile in range(5)], axis=1
    )
    second_half = lane_group(64, 64) == 1
    zeros = jnp.zeros((64, LANES), F32)
    for dx in range(2):
        for dy in range(2):
            value = picked(up_fine[...], dx, dy, 32)
            for cell, block in enumerate(
                (
                    zeros,
                    jnp.where(second_half, 0.0, value),
                    jnp.where(second_half, value, 0.0),
                    zeros,
                )
            ):
                lift[0, 64 * cell : 64 * (cell + 1), span_of(0)] = block.astype(BF)
            for tile in range(4):
                left = risen[:, tile * LANES : tile * LANES + DEPTH]
                rise = dot(left, lift[0, :DEPTH, :LANES])
                for y in range(count):
                    part = rise[16 * y : 16 * (y + 1)]
                    spread[tile, 2 * y + dy, pl.ds(2 + dx, 7, 2), :] = part[0:7]
                    spread[tile, 2 * y + dy, dx : dx + 1, :] = part[ends - 9 : ends - 8]
    count = 2 * count
    for tile in range(skip.shape[2] // LANES):
        total = spread[tile, :count, 0:16, :] + skip[:, :, span_of(tile)].astype(F32)
        wide[:count, 0:16, span_of(tile)] = total.astype(BF).astype(F32)
    stage(wide, s, count, 16, 0, 4 * LANES)
    conv_table(table, flat, f1[...], 32)
    count = count - 2
    for tile in range(4):
        value = rounded_relu(convolve(s, table, count, 16, tile, DEPTH if tile < 3 else LANES))
        wide[:count, 0:16, span_of(tile)] = value.astype(F32).reshape(count, 16, LANES)
    stage(wide, s, count, 16, 0, 4 * LANES)
    conv_table(table, flat, f2[...], 32)
    count = count - 2
    for tile in range(3):
        value = rounded_relu(convolve(s, table, count, 16, tile))
        out[:, :, span_of(tile)] = value.reshape(count, 16, LANES)


def call(kernel, outs, scratch, *args, scalars=0):
    spaces = [pltpu.SMEM] * scalars + [pltpu.VMEM] * (len(args) - scalars)
    return pl.pallas_call(
        kernel,
        out_shape=outs,
        in_specs=[pl.BlockSpec(memory_space=space) for space in spaces],
        out_specs=jax.tree.map(lambda _: pl.BlockSpec(memory_space=pltpu.VMEM), outs),
        scratch_shapes=scratch,
        name=kernel.__name__,
    )(*args)


def exchange(head, tail, axis, route):
    ahead = [(source, route(source, 1)) for source in range(lax.axis_size(axis))]
    back = [(source, route(source, -1)) for source in range(lax.axis_size(axis))]
    return lax.ppermute(tail, axis, ahead), lax.ppermute(head, axis, back)


def gathered_body(
    features_in,
    encode_fine_first,
    encode_fine_second,
    reduce_fine,
    encode_middle_first,
    encode_middle_second,
    reduce_middle,
    bottom_first,
    bottom_second,
    expand_middle,
    decode_middle_first,
    decode_middle_second,
    expand_fine,
    decode_fine_first,
    decode_fine_second,
):
    devices = lax.axis_size("yz")
    across = math.isqrt(devices)
    place = lax.axis_index("yz")
    where = jnp.stack([place // across, place % across, lax.axis_index("gx")]).astype(jnp.int32)
    fine, ext = features_in.shape[1], features_in.shape[2]
    mid = encode_middle_first.shape[0]
    halo = 4

    def around(source, step):
        return (source + step) % lax.axis_size("gx")

    def along_y(source, step):
        return (source + step * across) % devices

    def along_z(source, step):
        return source // across * across + (source % across + step) % across

    cores = lax.axis_size("gx")
    size = bottom_first.shape[0] // cores
    mine = lax.dynamic_slice_in_dim(bottom_first, lax.axis_index("gx") * size, size, 0)
    turned = lax.ppermute(
        mine, "yz", [(s, s % across * across + s // across) for s in range(devices)]
    )

    cells = features_in.reshape(fine, ext, ext, ext).transpose(2, 1, 3, 0)
    cells = cells.reshape(ext, ext, ext * fine)
    low, high = exchange(cells[:halo], cells[ext - halo :], "yz", along_y)
    cells = jnp.concatenate([low, cells, high], axis=0)
    edge = halo * fine
    low, high = exchange(cells[:, :, :edge], cells[:, :, -edge:], "yz", along_z)
    cells = jnp.concatenate([low, cells, high], axis=2)
    low, high = exchange(cells[:, :halo], cells[:, ext - halo :], "gx", around)

    seen = ext + 2 * halo
    side = ext // 2
    flat = pltpu.VMEM((27 * mid, LANES), F32)
    table = pltpu.VMEM((9, DEPTH, LANES), BF)
    down = pltpu.VMEM((2 * DEPTH, 2 * LANES), BF)
    skip, small = call(
        fine_encoder,
        (
            jax.ShapeDtypeStruct((ext + 4, ext + 4, (ext + 4) * fine), BF),
            jax.ShapeDtypeStruct((devices, side * side, side * mid), BF),
        ),
        [
            pltpu.VMEM((seen, 40, seen * fine), F32),
            pltpu.VMEM((3, seen * 32, seen * fine), BF),
            pltpu.VMEM((3, (seen - 2) * 16, seen * fine), BF),
            table,
            flat,
            down,
            pltpu.VMEM((2, side * 16, LANES), F32),
            pltpu.VMEM((side * side, side * mid), F32),
        ],
        low,
        cells,
        high,
        encode_fine_first,
        encode_fine_second,
        reduce_fine,
    )

    small, turned = lax.optimization_barrier((small, turned))
    swap = [(s, around(s, 1)) for s in range(cores)]
    own = lax.all_to_all(small, "yz", 0, 0)
    other = lax.ppermute(own, "gx", swap)
    swapped = lax.ppermute(turned, "gx", swap)

    total = side * across
    half = total // 2
    window, partial = call(
        middle,
        (
            jax.ShapeDtypeStruct((12, 16, 14 * mid), BF),
            jax.ShapeDtypeStruct((half * side, half * mid), BF),
        ),
        [
            pltpu.VMEM((total + 2, 32, total * mid + LANES), F32),
            pltpu.VMEM((3, (total + 2) * 16, total * mid + LANES), BF),
            table,
            flat,
            down,
            pltpu.VMEM((total + 6, 16, total * mid + 512), BF),
            pltpu.VMEM((2, half * 16, LANES), F32),
            pltpu.VMEM((half * side, half * mid), F32),
        ],
        where,
        own,
        other,
        encode_middle_first,
        encode_middle_second,
        reduce_middle,
        turned,
        swapped,
        scalars=1,
    )

    pieces = [partial] + [
        lax.ppermute(partial, "yz", [(s, s ^ turn) for s in range(devices)])
        for turn in range(1, across)
    ]
    sent = call(
        bottom,
        jax.ShapeDtypeStruct((devices, 7 * side // 2, 8 * mid), BF),
        [
            pltpu.VMEM((half + 2, 32, half * mid + LANES), F32),
            pltpu.VMEM((3, (half + 2) * 16, half * mid + LANES), BF),
            table,
            flat,
            pltpu.VMEM((half + 5, 8, half * mid + 512), F32),
            pltpu.VMEM((7 * side // 2, 8 * mid), F32),
        ],
        *pieces,
        bottom_second,
    )
    near = lax.all_to_all(sent, "yz", 0, 0)
    far = lax.ppermute(near, "gx", swap)

    risen = call(
        decoder,
        jax.ShapeDtypeStruct((ext, 16, ext * fine), BF),
        [
            pltpu.VMEM((16, 32, 1024), F32),
            pltpu.VMEM((3, 256, 1024), BF),
            table,
            flat,
            pltpu.VMEM((4, across * DEPTH, 2 * LANES), BF),
            pltpu.VMEM((8, 16, 512), F32),
            pltpu.VMEM((8, 16, 32, LANES), F32),
        ],
        where,
        near,
        far,
        window,
        skip,
        expand_middle,
        decode_middle_first,
        decode_middle_second,
        expand_fine,
        decode_fine_first,
        decode_fine_second,
        scalars=1,
    )
    risen = risen[:, :ext].reshape(ext, ext, ext, fine).transpose(3, 1, 0, 2)
    return risen.reshape(1, fine, ext, ext * ext)


def with_halo(cells, sides, width):
    for axis, dim in sides:
        count = lax.axis_size(axis)
        head = lax.slice_in_dim(cells, 0, width, axis=dim)
        tail = lax.slice_in_dim(cells, cells.shape[dim] - width, cells.shape[dim], axis=dim)
        cells = jnp.concatenate(
            [
                lax.ppermute(tail, axis, [(i, (i + 1) % count) for i in range(count)]),
                cells,
                lax.ppermute(head, axis, [((i + 1) % count, i) for i in range(count)]),
            ],
            axis=dim,
        )
    return cells


def shortened(x):
    return jax.tree.map(lambda a: a.astype(jnp.bfloat16) if a.dtype == jnp.float32 else a, x)


def from_behind(block, axis, distance):
    devices = range(lax.axis_size(axis))
    route = [((i - distance) % len(devices), i) for i in devices]
    return lax.ppermute(block, axis, route)


def conv_taps(padded, weight, width_in):
    kernel = weight.reshape(weight.shape[0], width_in, 3, 3, 3)
    return lax.conv_general_dilated(
        padded[None],
        kernel,
        (1, 1, 1),
        "VALID",
        dimension_numbers=("NCDHW", "OIDHW", "NCDHW"),
        preferred_element_type=jnp.float32,
    )[0]


def rectify(running):
    return jnp.maximum(running, 0.0).astype(jnp.bfloat16)


def shrink(region, weight):
    kernel = weight.reshape(weight.shape[0], region.shape[0], 2, 2, 2)
    result = lax.conv_general_dilated(
        region[None],
        kernel,
        (2, 2, 2),
        "VALID",
        dimension_numbers=("NCDHW", "OIDHW", "NCDHW"),
        preferred_element_type=jnp.float32,
    )[0]
    return result.astype(jnp.bfloat16)


def expand(region, weight, skipped):
    width_in, extent_x, extent_y, extent_z = region.shape
    width_out = weight.shape[1] // 8
    columns = lax.dot_general(
        weight,
        region.reshape(width_in, -1),
        (((0,), (0,)), ((), ())),
        preferred_element_type=jnp.float32,
    )
    spread = columns.reshape(width_out, 2, 2, 2, extent_x, extent_y, extent_z).transpose(
        0, 4, 1, 5, 2, 6, 3
    )
    spread = spread.reshape(width_out, 2 * extent_x, 2 * extent_y, 2 * extent_z)
    return (spread + skipped.astype(jnp.float32)).astype(jnp.bfloat16)


def x_margins(region):
    return with_halo(region, (("gx", 1),), 1)


def from_peer(plane, offset):
    return from_behind(shortened(plane), "yz", offset).astype(plane.dtype)


def pad_block(region, across):
    extended = x_margins(region)
    below_face = from_peer(extended[:, :, -1:, :], across)
    above_face = from_peer(extended[:, :, :1, :], -across)
    extended = jnp.concatenate([below_face, extended, above_face], axis=2)
    column = lax.axis_index("yz") % across
    last_plane = extended[:, :, :, -1:]
    first_plane = extended[:, :, :, :1]
    behind = jnp.where(column == 0, from_peer(last_plane, 1 - across), from_peer(last_plane, 1))
    ahead = jnp.where(
        column == across - 1, from_peer(first_plane, across - 1), from_peer(first_plane, -1)
    )
    return jnp.concatenate([behind, extended, ahead], axis=3)


def conv_layer(region, weight, across):
    return rectify(conv_taps(pad_block(region, across), weight, region.shape[0]))


def assemble(stored):
    width_out = stored.shape[0] // 4
    return (
        stored.reshape(4, width_out, stored.shape[1])
        .transpose(1, 0, 2)
        .reshape(width_out, 4 * stored.shape[1])
    )


def bottom_layer(region, weight, across):
    width_in = region.shape[0]
    padded = pad_block(region, across)
    gathered = lax.all_gather(weight, "yz", axis=0, tiled=True)
    return rectify(conv_taps(padded, assemble(gathered), width_in))


def body(
    features_in,
    encode_fine_first,
    encode_fine_second,
    reduce_fine,
    encode_middle_first,
    encode_middle_second,
    reduce_middle,
    bottom_first,
    bottom_second,
    expand_middle,
    decode_middle_first,
    decode_middle_second,
    expand_fine,
    decode_fine_first,
    decode_fine_second,
):
    across = math.isqrt(lax.axis_size("yz"))
    width_fine, extent = (features_in.shape[1], features_in.shape[2])
    region = features_in.reshape(width_fine, extent, extent, extent)
    fine_skip = conv_layer(
        conv_layer(region, encode_fine_first, across), encode_fine_second, across
    )
    middle = shrink(fine_skip, reduce_fine)
    middle_skip = conv_layer(
        conv_layer(middle, encode_middle_first, across), encode_middle_second, across
    )
    bottom = shrink(middle_skip, reduce_middle)
    bottom = bottom_layer(bottom_layer(bottom, bottom_first, across), bottom_second, across)
    rising = expand(bottom, expand_middle, middle_skip)
    rising = conv_layer(
        conv_layer(rising, decode_middle_first, across), decode_middle_second, across
    )
    rising = expand(rising, expand_fine, fine_skip)
    rising = conv_layer(conv_layer(rising, decode_fine_first, across), decode_fine_second, across)
    return rising.reshape(1, width_fine, extent, extent * extent)


def solution(mesh):
    placed = (
        P("yz", None, "gx", None),
        P(),
        P(),
        P(),
        P(),
        P(),
        P(),
        P("yz", None),
        P("yz", None),
        P(),
        P(),
        P(),
        P(),
        P(),
        P(),
    )

    def chosen(*args):
        across = math.isqrt(lax.axis_size("yz"))
        stored, channels = args[7].shape[0], args[4].shape[0]
        gathered = lax.axis_size("gx") == 2 and stored == channels
        gathered = gathered and across == 4 and across * channels == args[6].shape[0]
        return (gathered_body if gathered else body)(*args)

    return jax.shard_map(
        chosen, mesh=mesh, in_specs=placed, out_specs=P("yz", None, "gx", None), check_vma=False
    )
```

```python
import math

import jax
import jax.numpy as jnp
from jax import lax
from jax.experimental import pallas as pl
from jax.experimental.pallas import tpu as pltpu
from jax.sharding import PartitionSpec as P

BF = jnp.bfloat16
F32 = jnp.float32
LANES = 128
DEPTH = 256


def dot(a, b):
    return lax.dot_general(a, b, (((1,), (0,)), ((), ())), preferred_element_type=F32)


def lane_group(rows, width):
    return lax.broadcasted_iota(jnp.int32, (rows, LANES), 1) // width


def transposed(flat, weight):
    columns = weight.shape[1]
    copies = jnp.concatenate([weight.astype(F32)] * (LANES // weight.shape[0]), axis=0)
    for start in range(0, columns, LANES):
        stop = min(start + LANES, columns)
        flat[start:stop, :] = copies[:, start:stop].T


def blocks(taps, cells, wide_in, wide_out, target):
    group = lane_group(wide_in, wide_out)
    for cell in range(cells):
        value = jnp.zeros((wide_in, LANES), F32)
        for k, tap in enumerate(taps):
            out = target(cell, k)
            if out is not None and 0 <= out < LANES // wide_out:
                value = jnp.where(group == out, tap, value)
        yield cell * wide_in, value.astype(BF)


def conv_table(table, flat, weight, channels):
    transposed(flat, weight)
    for dy in range(3):
        for dx in range(3):
            taps = [flat[pl.ds(9 * dx + 3 * dy + dz, channels, 27), :] for dz in range(3)]
            for row, block in blocks(
                taps, DEPTH // channels, channels, channels, lambda z, k: z - k
            ):
                table[3 * dy + dx, row : row + channels, :] = block


def shrink_table(table, flat, weight, channels, offset):
    transposed(flat, weight)

    def target(z, k):
        return (z - offset - k) // 2 if (z - offset - k) % 2 == 0 else None

    for dx in range(2):
        for dy in range(2):
            taps = [flat[pl.ds(4 * dx + 2 * dy + dz, channels, 8), :] for dz in range(2)]
            for row, block in blocks(
                taps, DEPTH // channels, channels, weight.shape[0], target
            ):
                row += DEPTH * dy
                table[row : row + channels, LANES * dx : LANES * (dx + 1)] = block


def picked(weight, dx, dy, channels):
    rows = weight.shape[1]
    lane = lax.broadcasted_iota(jnp.int32, (rows, LANES), 1) % (2 * channels)
    row = lax.broadcasted_iota(jnp.int32, (rows, LANES), 0)
    wanted = 8 * (lane % channels) + 4 * dx + 2 * dy + lane // channels
    return dot(weight, (row == wanted).astype(BF))


def stage(wide, shifted, layers, rows, first, width, base=0):
    for y in range(layers):
        for d in range(3):
            shifted[d, y * rows : (y + 1) * rows, :width] = wide[
                base + y, first + d : first + d + rows, :width
            ].astype(BF)


def convolve(shifted, table, layers, rows, tile, depth=DEPTH):
    height = layers * rows
    start = tile * LANES
    left = jnp.concatenate(
        [
            shifted[dx, dy * rows : dy * rows + height, start : start + depth]
            for dy in range(3)
            for dx in range(3)
        ],
        axis=1,
    )
    return dot(left, table[:, :depth, :].reshape(9 * depth, LANES))


def rounded_relu(value):
    return jnp.maximum(value, 0.0).astype(BF)


def span_of(tile):
    return slice(tile * LANES, (tile + 1) * LANES)


def fine_encoder(
    low, mid, high, first, second, reduce, skip, small, wide, s1, s2, table, flat, down, halves, flats
):
    layers, width = mid.shape[0], mid.shape[2]
    start = 0
    for piece in (low, mid, high):
        wide[:, start : start + piece.shape[1], :] = piece[...].astype(F32)
        start += piece.shape[1]
    stage(wide, s1, layers, 32, 0, width)
    conv_table(table, flat, first[...], 32)
    inner = layers - 2
    tiles = width // LANES
    for tile in range(tiles):
        depth = DEPTH if tile + 1 < tiles else LANES
        value = rounded_relu(convolve(s1, table, inner, 32, tile, depth))
        wide[:inner, :32, span_of(tile)] = value.astype(F32).reshape(inner, 32, LANES)
    stage(wide, s2, inner, 16, 0, width)
    conv_table(table, flat, second[...], 32)
    kept = inner - 2
    for tile in range(tiles - 1):
        value = rounded_relu(convolve(s2, table, kept, 16, tile))
        skip[:, :, span_of(tile)] = value.reshape(kept, 16, LANES)
    shrink_table(down, flat, reduce[...], 32, 2)
    count = (kept - 4) // 2
    for tile in range(count // 2):
        left = jnp.concatenate(
            [
                jnp.concatenate(
                    [
                        skip[2 + 2 * y + dy, :, tile * LANES : tile * LANES + DEPTH]
                        for y in range(count)
                    ],
                    axis=0,
                )
                for dy in range(2)
            ],
            axis=1,
        )
        total = dot(left, down[...])
        halves[0] = total[:, :LANES]
        halves[1] = total[:, LANES:]
        for y in range(count):
            value = halves[0, pl.ds(16 * y + 2, count, 2), :]
            value = value + halves[1, pl.ds(16 * y + 3, count, 2), :]
            flats[count * y : count * (y + 1), span_of(tile)] = value
    small[...] = flats[...].astype(BF)


def wrap_rows(wide, layers, count):
    wide[1 : layers + 1, 7:8, :] = wide[1 : layers + 1, 7 + count : 8 + count, :]
    wide[1 : layers + 1, 8 + count : 9 + count, :] = wide[1 : layers + 1, 8:9, :]
    wide[0:1] = wide[layers : layers + 1]
    wide[layers + 1 : layers + 2] = wide[1:2]


def middle(
    own, other, first, second, reduce, window, sent, wide, s, table, flat, down, whole, halves, flats
):
    span = own.shape[1]
    side = span // 3 // 64
    reach = side - 1
    layers = side + 2 * reach
    near, far = own[...].astype(F32), other[...].astype(F32)
    for y in range(layers):
        start = side * y
        wide[y, 0:reach, :span] = far[start + 1 : start + side]
        wide[y, reach : reach + side, :span] = near[start : start + side]
        wide[y, reach + side : 2 * reach + side, :span] = far[start : start + reach]
    stage(wide, s, layers, 16, 0, span)
    conv_table(table, flat, first[...], 64)
    layers -= 2
    tiles = span // LANES - 1
    for tile in range(tiles):
        value = rounded_relu(convolve(s, table, layers, 16, tile))
        wide[:layers, 0:16, span_of(tile)] = value.astype(F32).reshape(layers, 16, LANES)
    stage(wide, s, layers, 16, 0, tiles * LANES)
    conv_table(table, flat, second[...], 64)
    layers -= 2
    for tile in range(tiles - 1):
        value = rounded_relu(convolve(s, table, layers, 16, tile)).reshape(layers, 16, LANES)
        whole[:, :, span_of(tile)] = value
        wide[:layers, 0:16, span_of(tile)] = value.astype(F32)
    width = window.shape[2]
    skipped = layers - side - 3
    wide[:layers, 16 : 16 + layers - 3, :width] = wide[:layers, 3:layers, :width]
    wide[:layers, 13 + layers : 16 + layers, :width] = wide[:layers, 0:3, :width]
    window[...] = wide[:layers, 16:32, :width].astype(BF)
    half = side // 2
    lefts = [
        jnp.concatenate(
            [
                jnp.concatenate(
                    [
                        whole[skipped + 2 * y + dy, :, (tile + 1) * DEPTH : (tile + 2) * DEPTH]
                        for y in range(half)
                    ],
                    axis=0,
                )
                for dy in range(2)
            ],
            axis=1,
        )
        for tile in range(2)
    ]
    across = reduce.shape[0] // 64
    for quarter in range(across):
        shrink_table(down, flat, reduce[64 * quarter : 64 * (quarter + 1), :], 64, 0)
        for tile, left in enumerate(lefts):
            total = dot(left, down[...])
            halves[0] = total[:, :LANES]
            halves[1] = total[:, LANES:]
            for y in range(half):
                value = halves[0, pl.ds(16 * y + 3, half, 2), :]
                value = value + halves[1, pl.ds(16 * y + 4, half, 2), :]
                row = half * (half * tile + y)
                flats[row : row + half, :] = value
        count = half * half
        fold = (count + 1) // 2
        last = flats[count : count + 16, :]
        turn = pltpu.roll(last, 64, 1)
        flats[count : count + fold, :] = jnp.where(
            lane_group(fold, 64) == 0, last[:fold], turn[fold : 2 * fold]
        )
        result = flats[0 : sent.shape[1], :].astype(BF)
        for target in range(quarter, sent.shape[0], across):
            sent[target] = result


def bottom_start(gathered, turned, swapped, partial, wide, s, table, flat, flats):
    span = partial.shape[1]
    cells = span // 64
    side = cells // 2
    core = lax.axis_index("gx")
    devices = gathered.shape[0] // 2
    across = math.isqrt(devices)
    half = cells // across
    count = half * half
    fold = (count + 1) // 2
    low = lane_group(count, 64) == 0
    for part in range(2):
        base = (core if part == 0 else 1 - core) * devices
        for i in range(across):
            for j in range(0, across, 2):
                here = gathered[base + across * i + j].astype(F32)
                after = gathered[base + across * i + j + 1].astype(F32)
                here_turn, after_turn = pltpu.roll(here, 64, 1), pltpu.roll(after, 64, 1)

                def unfold(one, two):
                    return jnp.concatenate([one[count : count + fold], two[count : 2 * count - fold]])

                pieces = (
                    here[:count],
                    jnp.where(low, unfold(here, here_turn), after_turn[:count]),
                    jnp.where(low, after_turn[:count], unfold(after_turn, after)),
                )
                for turn, piece in enumerate(pieces):
                    tile = half * (j // 2) + turn
                    for y in range(half):
                        wide[
                            1 + half * i + y,
                            8 + half * part : 8 + half * (part + 1),
                            span_of(tile),
                        ] = piece[half * y : half * (y + 1)]
    wide[1 : cells + 1, 8 : 8 + side, span : span + LANES] = wide[
        1 : cells + 1, 8 : 8 + side, 0:LANES
    ]
    wrap_rows(wide, cells, side)
    stage(wide, s, cells + 2, 16, 7, span + LANES)
    mine, theirs = turned[...].astype(F32), swapped[...].astype(F32)
    is_first = core == 0
    stored = jnp.concatenate(
        [jnp.where(is_first, mine, theirs), jnp.where(is_first, theirs, mine)], axis=0
    )
    conv_table(table, flat, stored, 64)
    for tile in range(span // LANES):
        value = convolve(s, table, cells, 16, tile)
        for y in range(cells):
            flats[side * y : side * (y + 1), span_of(tile)] = value[16 * y : 16 * y + side]
    partial[...] = flats[...].astype(BF)


def bottom(*refs):
    *pieces, weight, out, wide, s, table, flat, whole, flats = refs
    span = pieces[0].shape[1]
    cells = span // 64
    side = cells // 2
    across = math.isqrt(out.shape[0])
    total = 0.0
    for piece in pieces:
        total = total + piece[...].astype(F32)
    total = jnp.maximum(total, 0.0).astype(BF).astype(F32)
    for y in range(cells):
        wide[1 + y, 8 : 8 + side, :span] = total[side * y : side * (y + 1)]
    wide[1 : cells + 1, 8 : 8 + side, span : span + LANES] = wide[
        1 : cells + 1, 8 : 8 + side, 0:LANES
    ]
    wrap_rows(wide, cells, side)
    stage(wide, s, cells + 2, 16, 7, span + LANES)
    conv_table(table, flat, weight[...], 64)
    for tile in range(span // LANES):
        value = convolve(s, table, cells, 16, tile).reshape(cells, 16, LANES)
        whole[2 : cells + 2, :, span_of(tile + 2)] = value[:, :8]
    whole[0:2] = whole[cells : cells + 2]
    whole[cells + 2 : cells + 5] = whole[2:5]
    whole[:, :, 0 : 2 * LANES] = whole[:, :, span : span + 2 * LANES]
    block = cells // across
    kept = side // 2
    layers = block + 4
    for i in range(across):
        for j in range(across):
            start = (block * j - block * j % 2) * 64
            for tile in range(4):
                for y in range(layers):
                    row = kept * (layers * tile + y)
                    flats[row : row + kept, :] = whole[
                        block * i + y,
                        0:kept,
                        start + tile * LANES : start + (tile + 1) * LANES,
                    ]
            out[i * across + j] = flats[...].astype(BF)


def decoder(
    near,
    far,
    window,
    skip,
    up,
    m1,
    m2,
    up_fine,
    f1,
    f2,
    out,
    wide,
    s,
    table,
    flat,
    lift,
    columns,
    spread,
):
    across = math.isqrt(near.shape[0])
    kept = window.shape[0] // 4
    layers = kept + 4
    odd = lax.axis_index("yz") % across % 2
    for dx in range(2):
        for dy in range(2):
            pair = picked(up[...], dx, dy, 64)
            blank = jnp.zeros((64, LANES), BF)
            for group in range(across):
                value = pair[64 * group : 64 * (group + 1)]
                for cell in range(4):
                    for half in range(2):
                        block = blank
                        if cell - half in (0, 1):
                            block = jnp.where(odd == cell - half, value, 0.0).astype(BF)
                        row = DEPTH * group + 64 * cell
                        lift[2 * dx + dy, row : row + 64, span_of(half)] = block
    groups = []
    for group in range(across):
        for part, parts in enumerate((near, far)):
            total = 0.0
            for k in range(across):
                total = total + parts[k * across + group].astype(F32)
            total = jnp.maximum(total, 0.0)
            for tile in range(4):
                for y in range(layers):
                    row = kept * (layers * tile + y)
                    columns[y, kept * part : kept * (part + 1), span_of(tile)] = total[
                        row : row + kept
                    ]
        groups.append(
            jnp.concatenate(
                [
                    columns[:layers, :, :512].astype(BF).reshape(layers * 16, 512),
                    jnp.zeros((layers * 16, LANES), BF),
                ],
                axis=1,
            )
        )
    for tile in range(4):
        left = jnp.concatenate(
            [g[:, tile * LANES : tile * LANES + DEPTH] for g in groups], axis=1
        )
        for dx in range(2):
            for dy in range(2):
                value = dot(left, lift[2 * dx + dy])
                for y in range(layers):
                    for half in range(2):
                        spread[2 * tile + half, 2 * y + dy, pl.ds(8 + dx, 2 * kept, 2), :] = value[
                            16 * y : 16 * y + 2 * kept, span_of(half)
                        ]
    count = window.shape[0]
    for tile in range(window.shape[2] // LANES):
        total = spread[tile, 1 : count + 1, 8:24, :] + window[:, :, span_of(tile)].astype(F32)
        wide[:count, 8:24, span_of(tile)] = total.astype(BF).astype(F32)
    ends = 8 + count
    wide[:, 7:8, :] = wide[:, ends - 1 : ends, :]
    wide[:, ends : ends + 1, :] = wide[:, 8:9, :]
    stage(wide, s, count, 16, 7, window.shape[2])
    conv_table(table, flat, m1[...], 64)
    count = count - 2
    for tile in range(6):
        value = rounded_relu(convolve(s, table, count, 16, tile))
        wide[:count, 8:24, span_of(tile)] = value.astype(F32).reshape(count, 16, LANES)
    wide[:, 7:8, :] = wide[:, ends - 1 : ends, :]
    wide[:, ends : ends + 1, :] = wide[:, 8:9, :]
    stage(wide, s, count, 16, 7, 6 * LANES)
    conv_table(table, flat, m2[...], 64)
    count = count - 2
    risen = jnp.concatenate(
        [rounded_relu(convolve(s, table, count, 16, tile)) for tile in range(5)], axis=1
    )
    second_half = lane_group(64, 64) == 1
    zeros = jnp.zeros((64, LANES), F32)
    for dx in range(2):
        for dy in range(2):
            value = picked(up_fine[...], dx, dy, 32)
            for cell, block in enumerate(
                (
                    zeros,
                    jnp.where(second_half, 0.0, value),
                    jnp.where(second_half, value, 0.0),
                    zeros,
                )
            ):
                lift[0, 64 * cell : 64 * (cell + 1), span_of(0)] = block.astype(BF)
            for tile in range(4):
                left = risen[:, tile * LANES : tile * LANES + DEPTH]
                rise = dot(left, lift[0, :DEPTH, :LANES])
                for y in range(count):
                    part = rise[16 * y : 16 * (y + 1)]
                    spread[tile, 2 * y + dy, pl.ds(2 + dx, 7, 2), :] = part[0:7]
                    spread[tile, 2 * y + dy, dx : dx + 1, :] = part[ends - 9 : ends - 8]
    count = 2 * count
    for tile in range(skip.shape[2] // LANES):
        total = spread[tile, :count, 0:16, :] + skip[:, :, span_of(tile)].astype(F32)
        wide[:count, 0:16, span_of(tile)] = total.astype(BF).astype(F32)
    stage(wide, s, count, 16, 0, 4 * LANES)
    conv_table(table, flat, f1[...], 32)
    count = count - 2
    for tile in range(4):
        value = rounded_relu(convolve(s, table, count, 16, tile, DEPTH if tile < 3 else LANES))
        wide[:count, 0:16, span_of(tile)] = value.astype(F32).reshape(count, 16, LANES)
    stage(wide, s, count, 16, 0, 4 * LANES)
    conv_table(table, flat, f2[...], 32)
    count = count - 2
    for tile in range(3):
        value = rounded_relu(convolve(s, table, count, 16, tile))
        out[:, :, span_of(tile)] = value.reshape(count, 16, LANES)


def call(kernel, outs, scratch, *args):
    return pl.pallas_call(
        kernel,
        out_shape=jax.tree.map(lambda out: pltpu.VMEM(out.shape, out.dtype), outs),
        in_specs=[pl.BlockSpec(memory_space=pltpu.VMEM)] * len(args),
        out_specs=jax.tree.map(lambda _: pl.BlockSpec(memory_space=pltpu.VMEM), outs),
        scratch_shapes=scratch,
        name=kernel.__name__,
    )(*[near_by(arg) for arg in args])


def near_by(arg):
    return pltpu.with_memory_space_constraint(arg, pltpu.MemorySpace.VMEM)


def exchange(head, tail, axis, route):
    ahead = [(source, route(source, 1)) for source in range(lax.axis_size(axis))]
    back = [(source, route(source, -1)) for source in range(lax.axis_size(axis))]
    return lax.ppermute(tail, axis, ahead), lax.ppermute(head, axis, back)


def gathered_body(
    features_in,
    encode_fine_first,
    encode_fine_second,
    reduce_fine,
    encode_middle_first,
    encode_middle_second,
    reduce_middle,
    bottom_first,
    bottom_second,
    expand_middle,
    decode_middle_first,
    decode_middle_second,
    expand_fine,
    decode_fine_first,
    decode_fine_second,
):
    devices = lax.axis_size("yz")
    across = math.isqrt(devices)
    fine, ext = features_in.shape[1], features_in.shape[2]
    mid = encode_middle_first.shape[0]
    halo = 4

    def around(source, step):
        return (source + step) % lax.axis_size("gx")

    def along_y(source, step):
        return (source + step * across) % devices

    def along_z(source, step):
        return source // across * across + (source % across + step) % across

    cores = lax.axis_size("gx")
    size = bottom_first.shape[0] // cores
    mine = lax.dynamic_slice_in_dim(bottom_first, lax.axis_index("gx") * size, size, 0)
    turned = lax.ppermute(
        mine, "yz", [(s, s % across * across + s // across) for s in range(devices)]
    )

    cells = features_in.reshape(fine, ext, ext, ext).transpose(2, 1, 3, 0)
    cells = cells.reshape(ext, ext, ext * fine)
    low, high = exchange(cells[:halo], cells[ext - halo :], "yz", along_y)
    cells = jnp.concatenate([low, cells, high], axis=0)
    edge = halo * fine
    low, high = exchange(cells[:, :, :edge], cells[:, :, -edge:], "yz", along_z)
    cells = jnp.concatenate([low, cells, high], axis=2)
    low, high = exchange(cells[:, :halo], cells[:, ext - halo :], "gx", around)

    seen = ext + 2 * halo
    side = ext // 2
    flat = pltpu.VMEM((27 * mid, LANES), F32)
    table = pltpu.VMEM((9, DEPTH, LANES), BF)
    down = pltpu.VMEM((2 * DEPTH, 2 * LANES), BF)
    skip, small = call(
        fine_encoder,
        (
            jax.ShapeDtypeStruct((ext + 4, ext + 4, (ext + 4) * fine), BF),
            jax.ShapeDtypeStruct((side * side, side * mid), BF),
        ),
        [
            pltpu.VMEM((seen, 40, seen * fine), F32),
            pltpu.VMEM((3, seen * 32, seen * fine), BF),
            pltpu.VMEM((3, (seen - 2) * 16, seen * fine), BF),
            table,
            flat,
            down,
            pltpu.VMEM((2, side * 16, LANES), F32),
            pltpu.VMEM((side * side, side * mid), F32),
        ],
        low,
        cells,
        high,
        encode_fine_first,
        encode_fine_second,
        reduce_fine,
    )

    small, turned = lax.optimization_barrier((small, turned))
    swap = [(s, around(s, 1)) for s in range(cores)]
    swapped = lax.ppermute(turned, "gx", swap)
    reach = (side - 1) * side
    low, high = exchange(small[:reach], small[side:], "yz", along_y)
    small = jnp.concatenate([low, small, high], axis=0)
    low, high = exchange(small, small, "yz", along_z)
    own = jnp.concatenate([low, small, high], axis=1)
    other = lax.ppermute(own, "gx", swap)

    total = side * across
    half = total // 2
    layers, span = 3 * side - 2, 3 * side * mid
    window, sent = call(
        middle,
        (
            jax.ShapeDtypeStruct((layers - 4, 16, 14 * mid), BF),
            jax.ShapeDtypeStruct((devices * cores, 16, LANES), BF),
        ),
        [
            pltpu.VMEM((layers, 32, span), F32),
            pltpu.VMEM((3, layers * 16, span), BF),
            table,
            flat,
            down,
            pltpu.VMEM((layers - 4, 16, 14 * mid), BF),
            pltpu.VMEM((2, side * 8, LANES), F32),
            pltpu.VMEM((32, LANES), F32),
        ],
        own,
        other,
        encode_middle_first,
        encode_middle_second,
        reduce_middle,
    )
    sent, swapped = lax.optimization_barrier((sent, swapped))
    gathered = lax.all_to_all(sent, ("gx", "yz"), 0, 0)
    partial = call(
        bottom_start,
        jax.ShapeDtypeStruct((half * side, half * mid), BF),
        [
            pltpu.VMEM((half + 2, 32, half * mid + LANES), F32),
            pltpu.VMEM((3, (half + 2) * 16, half * mid + LANES), BF),
            table,
            flat,
            pltpu.VMEM((half * side, half * mid), F32),
        ],
        gathered,
        turned,
        swapped,
    )

    pieces = [partial] + [
        lax.ppermute(partial, "yz", [(s, s ^ turn) for s in range(devices)])
        for turn in range(1, across)
    ]
    sent = call(
        bottom,
        jax.ShapeDtypeStruct((devices, 88, LANES), BF),
        [
            pltpu.VMEM((half + 2, 32, half * mid + LANES), F32),
            pltpu.VMEM((3, (half + 2) * 16, half * mid + LANES), BF),
            table,
            flat,
            pltpu.VMEM((half + 5, 8, half * mid + 2 * LANES), F32),
            pltpu.VMEM((88, LANES), F32),
        ],
        *pieces,
        bottom_second,
    )
    near = lax.all_to_all(sent, "yz", 0, 0)
    far = lax.ppermute(near, "gx", swap)

    risen = call(
        decoder,
        jax.ShapeDtypeStruct((ext, 16, ext * fine), BF),
        [
            pltpu.VMEM((16, 32, 1024), F32),
            pltpu.VMEM((3, 256, 1024), BF),
            table,
            flat,
            pltpu.VMEM((4, across * DEPTH, 2 * LANES), BF),
            pltpu.VMEM((8, 16, 512), F32),
            pltpu.VMEM((8, 16, 32, LANES), F32),
        ],
        near,
        far,
        window,
        skip,
        expand_middle,
        decode_middle_first,
        decode_middle_second,
        expand_fine,
        decode_fine_first,
        decode_fine_second,
    )
    risen = risen[:, :ext].reshape(ext, ext, ext, fine).transpose(3, 1, 0, 2)
    return risen.reshape(1, fine, ext, ext * ext)


def with_halo(cells, sides, width):
    for axis, dim in sides:
        count = lax.axis_size(axis)
        head = lax.slice_in_dim(cells, 0, width, axis=dim)
        tail = lax.slice_in_dim(cells, cells.shape[dim] - width, cells.shape[dim], axis=dim)
        cells = jnp.concatenate(
            [
                lax.ppermute(tail, axis, [(i, (i + 1) % count) for i in range(count)]),
                cells,
                lax.ppermute(head, axis, [((i + 1) % count, i) for i in range(count)]),
            ],
            axis=dim,
        )
    return cells


def shortened(x):
    return jax.tree.map(lambda a: a.astype(jnp.bfloat16) if a.dtype == jnp.float32 else a, x)


def from_behind(block, axis, distance):
    devices = range(lax.axis_size(axis))
    route = [((i - distance) % len(devices), i) for i in devices]
    return lax.ppermute(block, axis, route)


def conv_taps(padded, weight, width_in):
    kernel = weight.reshape(weight.shape[0], width_in, 3, 3, 3)
    return lax.conv_general_dilated(
        padded[None],
        kernel,
        (1, 1, 1),
        "VALID",
        dimension_numbers=("NCDHW", "OIDHW", "NCDHW"),
        preferred_element_type=jnp.float32,
    )[0]


def rectify(running):
    return jnp.maximum(running, 0.0).astype(jnp.bfloat16)


def shrink(region, weight):
    kernel = weight.reshape(weight.shape[0], region.shape[0], 2, 2, 2)
    result = lax.conv_general_dilated(
        region[None],
        kernel,
        (2, 2, 2),
        "VALID",
        dimension_numbers=("NCDHW", "OIDHW", "NCDHW"),
        preferred_element_type=jnp.float32,
    )[0]
    return result.astype(jnp.bfloat16)


def expand(region, weight, skipped):
    width_in, extent_x, extent_y, extent_z = region.shape
    width_out = weight.shape[1] // 8
    columns = lax.dot_general(
        weight,
        region.reshape(width_in, -1),
        (((0,), (0,)), ((), ())),
        preferred_element_type=jnp.float32,
    )
    spread = columns.reshape(width_out, 2, 2, 2, extent_x, extent_y, extent_z).transpose(
        0, 4, 1, 5, 2, 6, 3
    )
    spread = spread.reshape(width_out, 2 * extent_x, 2 * extent_y, 2 * extent_z)
    return (spread + skipped.astype(jnp.float32)).astype(jnp.bfloat16)


def x_margins(region):
    return with_halo(region, (("gx", 1),), 1)


def from_peer(plane, offset):
    return from_behind(shortened(plane), "yz", offset).astype(plane.dtype)


def pad_block(region, across):
    extended = x_margins(region)
    below_face = from_peer(extended[:, :, -1:, :], across)
    above_face = from_peer(extended[:, :, :1, :], -across)
    extended = jnp.concatenate([below_face, extended, above_face], axis=2)
    column = lax.axis_index("yz") % across
    last_plane = extended[:, :, :, -1:]
    first_plane = extended[:, :, :, :1]
    behind = jnp.where(column == 0, from_peer(last_plane, 1 - across), from_peer(last_plane, 1))
    ahead = jnp.where(
        column == across - 1, from_peer(first_plane, across - 1), from_peer(first_plane, -1)
    )
    return jnp.concatenate([behind, extended, ahead], axis=3)


def conv_layer(region, weight, across):
    return rectify(conv_taps(pad_block(region, across), weight, region.shape[0]))


def assemble(stored):
    width_out = stored.shape[0] // 4
    return (
        stored.reshape(4, width_out, stored.shape[1])
        .transpose(1, 0, 2)
        .reshape(width_out, 4 * stored.shape[1])
    )


def bottom_layer(region, weight, across):
    width_in = region.shape[0]
    padded = pad_block(region, across)
    gathered = lax.all_gather(weight, "yz", axis=0, tiled=True)
    return rectify(conv_taps(padded, assemble(gathered), width_in))


def body(
    features_in,
    encode_fine_first,
    encode_fine_second,
    reduce_fine,
    encode_middle_first,
    encode_middle_second,
    reduce_middle,
    bottom_first,
    bottom_second,
    expand_middle,
    decode_middle_first,
    decode_middle_second,
    expand_fine,
    decode_fine_first,
    decode_fine_second,
):
    across = math.isqrt(lax.axis_size("yz"))
    width_fine, extent = (features_in.shape[1], features_in.shape[2])
    region = features_in.reshape(width_fine, extent, extent, extent)
    fine_skip = conv_layer(
        conv_layer(region, encode_fine_first, across), encode_fine_second, across
    )
    middle = shrink(fine_skip, reduce_fine)
    middle_skip = conv_layer(
        conv_layer(middle, encode_middle_first, across), encode_middle_second, across
    )
    bottom = shrink(middle_skip, reduce_middle)
    bottom = bottom_layer(bottom_layer(bottom, bottom_first, across), bottom_second, across)
    rising = expand(bottom, expand_middle, middle_skip)
    rising = conv_layer(
        conv_layer(rising, decode_middle_first, across), decode_middle_second, across
    )
    rising = expand(rising, expand_fine, fine_skip)
    rising = conv_layer(conv_layer(rising, decode_fine_first, across), decode_fine_second, across)
    return rising.reshape(1, width_fine, extent, extent * extent)


def solution(mesh):
    placed = (
        P("yz", None, "gx", None),
        P(),
        P(),
        P(),
        P(),
        P(),
        P(),
        P("yz", None),
        P("yz", None),
        P(),
        P(),
        P(),
        P(),
        P(),
        P(),
    )

    def chosen(*args):
        across = math.isqrt(lax.axis_size("yz"))
        stored, channels = args[7].shape[0], args[4].shape[0]
        gathered = lax.axis_size("gx") == 2 and stored == channels
        gathered = gathered and across == 4 and across * channels == args[6].shape[0]
        return (gathered_body if gathered else body)(*args)

    return jax.shard_map(
        chosen, mesh=mesh, in_specs=placed, out_specs=P("yz", None, "gx", None), check_vma=False
    )
```

```python
import math

import jax
import jax.numpy as jnp
from jax import lax
from jax.experimental import pallas as pl
from jax.experimental.pallas import tpu as pltpu
from jax.sharding import PartitionSpec as P

BF = jnp.bfloat16
F32 = jnp.float32
LANES = 128
DEPTH = 256


def dot(a, b):
    return lax.dot_general(a, b, (((1,), (0,)), ((), ())), preferred_element_type=F32)


def lane_group(rows, width):
    return lax.broadcasted_iota(jnp.int32, (rows, LANES), 1) // width


def transposed(flat, weight):
    columns = weight.shape[1]
    copies = jnp.concatenate([weight.astype(F32)] * (LANES // weight.shape[0]), axis=0)
    for start in range(0, columns, LANES):
        stop = min(start + LANES, columns)
        flat[start:stop, :] = copies[:, start:stop].T


def blocks(taps, cells, wide_in, wide_out, target):
    group = lane_group(wide_in, wide_out)
    for cell in range(cells):
        value = jnp.zeros((wide_in, LANES), F32)
        for k, tap in enumerate(taps):
            out = target(cell, k)
            if out is not None and 0 <= out < LANES // wide_out:
                value = jnp.where(group == out, tap, value)
        yield cell * wide_in, value.astype(BF)


def conv_table(table, flat, weight, channels):
    transposed(flat, weight)
    for dy in range(3):
        for dx in range(3):
            taps = [flat[pl.ds(9 * dx + 3 * dy + dz, channels, 27), :] for dz in range(3)]
            for row, block in blocks(
                taps, DEPTH // channels, channels, channels, lambda z, k: z - k
            ):
                row += DEPTH * dx
                table[row : row + channels, span_of(dy)] = block


def shrink_table(table, flat, weight, channels, offset):
    transposed(flat, weight)

    def target(z, k):
        return (z - offset - k) // 2 if (z - offset - k) % 2 == 0 else None

    for dx in range(2):
        for dy in range(2):
            taps = [flat[pl.ds(4 * dx + 2 * dy + dz, channels, 8), :] for dz in range(2)]
            for row, block in blocks(
                taps, DEPTH // channels, channels, weight.shape[0], target
            ):
                row += DEPTH * dy
                table[row : row + channels, LANES * dx : LANES * (dx + 1)] = block


def picked(weight, dx, dy, channels):
    rows = weight.shape[1]
    lane = lax.broadcasted_iota(jnp.int32, (rows, LANES), 1) % (2 * channels)
    row = lax.broadcasted_iota(jnp.int32, (rows, LANES), 0)
    wanted = 8 * (lane % channels) + 4 * dx + 2 * dy + lane // channels
    return dot(weight, (row == wanted).astype(BF))


def stage(wide, shifted, layers, rows, first, width, base=0):
    for y in range(layers):
        for d in range(3):
            shifted[d, y * rows : (y + 1) * rows, :width] = wide[
                base + y, first + d : first + d + rows, :width
            ].astype(BF)


def convolve(shifted, table, layers, rows, tile, depth=DEPTH):
    height = layers * rows
    start = tile * LANES
    left = jnp.concatenate(
        [shifted[dx, 0 : height + 2 * rows, start : start + depth] for dx in range(3)], axis=1
    )
    right = jnp.concatenate([table[DEPTH * dx : DEPTH * dx + depth, :] for dx in range(3)], axis=0)
    pair = dot(left[: height + rows], right[:, : 2 * LANES])
    last = dot(left[2 * rows :], right[:, 2 * LANES :])
    return pair[:height, :LANES] + pair[rows:, LANES:] + last


def rounded_relu(value):
    return jnp.maximum(value, 0.0).astype(BF)


def span_of(tile):
    return slice(tile * LANES, (tile + 1) * LANES)


def fine_encoder(
    low, mid, high, first, second, reduce, skip, small, wide, s1, s2, table, flat, down, halves, flats
):
    layers, width = mid.shape[0], mid.shape[2]
    start = 0
    for piece in (low, mid, high):
        wide[:, start : start + piece.shape[1], :] = piece[...].astype(F32)
        start += piece.shape[1]
    stage(wide, s1, layers, 32, 0, width)
    conv_table(table, flat, first[...], 32)
    inner = layers - 2
    tiles = width // LANES
    for tile in range(tiles):
        depth = DEPTH if tile + 1 < tiles else LANES
        value = rounded_relu(convolve(s1, table, inner, 32, tile, depth))
        wide[:inner, :32, span_of(tile)] = value.astype(F32).reshape(inner, 32, LANES)
    stage(wide, s2, inner, 16, 0, width)
    conv_table(table, flat, second[...], 32)
    kept = inner - 2
    for tile in range(tiles - 1):
        value = rounded_relu(convolve(s2, table, kept, 16, tile))
        skip[:, :, span_of(tile)] = value.reshape(kept, 16, LANES)
    shrink_table(down, flat, reduce[...], 32, 2)
    count = (kept - 4) // 2
    for tile in range(count // 2):
        left = jnp.concatenate(
            [
                jnp.concatenate(
                    [
                        skip[2 + 2 * y + dy, :, tile * LANES : tile * LANES + DEPTH]
                        for y in range(count)
                    ],
                    axis=0,
                )
                for dy in range(2)
            ],
            axis=1,
        )
        total = dot(left, down[...])
        halves[0] = total[:, :LANES]
        halves[1] = total[:, LANES:]
        for y in range(count):
            value = halves[0, pl.ds(16 * y + 2, count, 2), :]
            value = value + halves[1, pl.ds(16 * y + 3, count, 2), :]
            flats[count * y : count * (y + 1), span_of(tile)] = value
    small[...] = flats[...].astype(BF)


def wrap_rows(wide, layers, count):
    wide[1 : layers + 1, 7:8, :] = wide[1 : layers + 1, 7 + count : 8 + count, :]
    wide[1 : layers + 1, 8 + count : 9 + count, :] = wide[1 : layers + 1, 8:9, :]
    wide[0:1] = wide[layers : layers + 1]
    wide[layers + 1 : layers + 2] = wide[1:2]


def middle(
    own, other, first, second, reduce, window, sent, wide, s, table, flat, down, whole, halves, flats
):
    span = own.shape[1]
    side = span // 3 // 64
    reach = side - 1
    layers = side + 2 * reach
    near, far = own[...].astype(F32), other[...].astype(F32)
    for y in range(layers):
        start = side * y
        wide[y, 0:reach, :span] = far[start + 1 : start + side]
        wide[y, reach : reach + side, :span] = near[start : start + side]
        wide[y, reach + side : 2 * reach + side, :span] = far[start : start + reach]
    stage(wide, s, layers, 16, 0, span)
    conv_table(table, flat, first[...], 64)
    layers -= 2
    tiles = span // LANES - 1
    for tile in range(tiles):
        value = rounded_relu(convolve(s, table, layers, 16, tile))
        wide[:layers, 0:16, span_of(tile)] = value.astype(F32).reshape(layers, 16, LANES)
    stage(wide, s, layers, 16, 0, tiles * LANES)
    conv_table(table, flat, second[...], 64)
    layers -= 2
    for tile in range(tiles - 1):
        value = rounded_relu(convolve(s, table, layers, 16, tile)).reshape(layers, 16, LANES)
        whole[:, :, span_of(tile)] = value
        wide[:layers, 0:16, span_of(tile)] = value.astype(F32)
    width = window.shape[2]
    skipped = layers - side - 3
    wide[:layers, 16 : 16 + layers - 3, :width] = wide[:layers, 3:layers, :width]
    wide[:layers, 13 + layers : 16 + layers, :width] = wide[:layers, 0:3, :width]
    window[...] = wide[:layers, 16:32, :width].astype(BF)
    half = side // 2
    lefts = [
        jnp.concatenate(
            [
                jnp.concatenate(
                    [
                        whole[skipped + 2 * y + dy, :, (tile + 1) * DEPTH : (tile + 2) * DEPTH]
                        for y in range(half)
                    ],
                    axis=0,
                )
                for dy in range(2)
            ],
            axis=1,
        )
        for tile in range(2)
    ]
    across = reduce.shape[0] // 64
    for quarter in range(across):
        shrink_table(down, flat, reduce[64 * quarter : 64 * (quarter + 1), :], 64, 0)
        for tile, left in enumerate(lefts):
            total = dot(left, down[...])
            halves[0] = total[:, :LANES]
            halves[1] = total[:, LANES:]
            for y in range(half):
                value = halves[0, pl.ds(16 * y + 3, half, 2), :]
                value = value + halves[1, pl.ds(16 * y + 4, half, 2), :]
                row = half * (half * tile + y)
                flats[row : row + half, :] = value
        count = half * half
        fold = (count + 1) // 2
        last = flats[count : count + 16, :]
        turn = pltpu.roll(last, 64, 1)
        flats[count : count + fold, :] = jnp.where(
            lane_group(fold, 64) == 0, last[:fold], turn[fold : 2 * fold]
        )
        result = flats[0 : sent.shape[1], :].astype(BF)
        for target in range(quarter, sent.shape[0], across):
            sent[target] = result


def bottom_start(gathered, turned, swapped, partial, wide, s, table, flat, flats):
    span = partial.shape[1]
    cells = span // 64
    side = cells // 2
    core = lax.axis_index("gx")
    devices = gathered.shape[0] // 2
    across = math.isqrt(devices)
    half = cells // across
    count = half * half
    fold = (count + 1) // 2
    low = lane_group(count, 64) == 0
    for part in range(2):
        base = (core if part == 0 else 1 - core) * devices
        for i in range(across):
            for j in range(0, across, 2):
                here = gathered[base + across * i + j].astype(F32)
                after = gathered[base + across * i + j + 1].astype(F32)
                here_turn, after_turn = pltpu.roll(here, 64, 1), pltpu.roll(after, 64, 1)

                def unfold(one, two):
                    return jnp.concatenate([one[count : count + fold], two[count : 2 * count - fold]])

                pieces = (
                    here[:count],
                    jnp.where(low, unfold(here, here_turn), after_turn[:count]),
                    jnp.where(low, after_turn[:count], unfold(after_turn, after)),
                )
                for turn, piece in enumerate(pieces):
                    tile = half * (j // 2) + turn
                    for y in range(half):
                        wide[
                            1 + half * i + y,
                            8 + half * part : 8 + half * (part + 1),
                            span_of(tile),
                        ] = piece[half * y : half * (y + 1)]
    wide[1 : cells + 1, 8 : 8 + side, span : span + LANES] = wide[
        1 : cells + 1, 8 : 8 + side, 0:LANES
    ]
    wrap_rows(wide, cells, side)
    stage(wide, s, cells + 2, 16, 7, span + LANES)
    mine, theirs = turned[...].astype(F32), swapped[...].astype(F32)
    is_first = core == 0
    stored = jnp.concatenate(
        [jnp.where(is_first, mine, theirs), jnp.where(is_first, theirs, mine)], axis=0
    )
    conv_table(table, flat, stored, 64)
    for tile in range(span // LANES):
        value = convolve(s, table, cells, 16, tile)
        for y in range(cells):
            flats[side * y : side * (y + 1), span_of(tile)] = value[16 * y : 16 * y + side]
    partial[...] = flats[...].astype(BF)


def bottom(*refs):
    *pieces, weight, out, wide, s, table, flat, whole, flats = refs
    span = pieces[0].shape[1]
    cells = span // 64
    side = cells // 2
    across = math.isqrt(out.shape[0])
    total = 0.0
    for piece in pieces:
        total = total + piece[...].astype(F32)
    total = jnp.maximum(total, 0.0).astype(BF).astype(F32)
    for y in range(cells):
        wide[1 + y, 8 : 8 + side, :span] = total[side * y : side * (y + 1)]
    wide[1 : cells + 1, 8 : 8 + side, span : span + LANES] = wide[
        1 : cells + 1, 8 : 8 + side, 0:LANES
    ]
    wrap_rows(wide, cells, side)
    stage(wide, s, cells + 2, 16, 7, span + LANES)
    conv_table(table, flat, weight[...], 64)
    for tile in range(span // LANES):
        value = convolve(s, table, cells, 16, tile).reshape(cells, 16, LANES)
        whole[2 : cells + 2, :, span_of(tile + 2)] = value[:, :8]
    whole[0:2] = whole[cells : cells + 2]
    whole[cells + 2 : cells + 5] = whole[2:5]
    whole[:, :, 0 : 2 * LANES] = whole[:, :, span : span + 2 * LANES]
    block = cells // across
    kept = side // 2
    layers = block + 4
    for i in range(across):
        for j in range(across):
            start = (block * j - block * j % 2) * 64
            for tile in range(4):
                for y in range(layers):
                    row = kept * (layers * tile + y)
                    flats[row : row + kept, :] = whole[
                        block * i + y,
                        0:kept,
                        start + tile * LANES : start + (tile + 1) * LANES,
                    ]
            out[i * across + j] = flats[...].astype(BF)


def decoder(
    near,
    far,
    window,
    skip,
    up,
    m1,
    m2,
    up_fine,
    f1,
    f2,
    out,
    wide,
    s,
    table,
    flat,
    lift,
    columns,
    spread,
):
    across = math.isqrt(near.shape[0])
    kept = window.shape[0] // 4
    layers = kept + 4
    odd = lax.axis_index("yz") % across % 2
    for dx in range(2):
        for dy in range(2):
            pair = picked(up[...], dx, dy, 64)
            blank = jnp.zeros((64, LANES), BF)
            for group in range(across):
                value = pair[64 * group : 64 * (group + 1)]
                for cell in range(4):
                    for half in range(2):
                        block = blank
                        if cell - half in (0, 1):
                            block = jnp.where(odd == cell - half, value, 0.0).astype(BF)
                        row = DEPTH * group + 64 * cell
                        lift[2 * dx + dy, row : row + 64, span_of(half)] = block
    groups = []
    for group in range(across):
        for part, parts in enumerate((near, far)):
            total = 0.0
            for k in range(across):
                total = total + parts[k * across + group].astype(F32)
            total = jnp.maximum(total, 0.0)
            for tile in range(4):
                for y in range(layers):
                    row = kept * (layers * tile + y)
                    columns[y, kept * part : kept * (part + 1), span_of(tile)] = total[
                        row : row + kept
                    ]
        groups.append(
            jnp.concatenate(
                [
                    columns[:layers, :, :512].astype(BF).reshape(layers * 16, 512),
                    jnp.zeros((layers * 16, LANES), BF),
                ],
                axis=1,
            )
        )
    for tile in range(4):
        left = jnp.concatenate(
            [g[:, tile * LANES : tile * LANES + DEPTH] for g in groups], axis=1
        )
        for dx in range(2):
            for dy in range(2):
                value = dot(left, lift[2 * dx + dy])
                for y in range(layers):
                    for half in range(2):
                        spread[2 * tile + half, 2 * y + dy, pl.ds(8 + dx, 2 * kept, 2), :] = value[
                            16 * y : 16 * y + 2 * kept, span_of(half)
                        ]
    count = window.shape[0]
    for tile in range(window.shape[2] // LANES):
        total = spread[tile, 1 : count + 1, 8:24, :] + window[:, :, span_of(tile)].astype(F32)
        wide[:count, 8:24, span_of(tile)] = total.astype(BF).astype(F32)
    ends = 8 + count
    wide[:, 7:8, :] = wide[:, ends - 1 : ends, :]
    wide[:, ends : ends + 1, :] = wide[:, 8:9, :]
    stage(wide, s, count, 16, 7, window.shape[2])
    conv_table(table, flat, m1[...], 64)
    count = count - 2
    for tile in range(6):
        value = rounded_relu(convolve(s, table, count, 16, tile))
        wide[:count, 8:24, span_of(tile)] = value.astype(F32).reshape(count, 16, LANES)
    wide[:, 7:8, :] = wide[:, ends - 1 : ends, :]
    wide[:, ends : ends + 1, :] = wide[:, 8:9, :]
    stage(wide, s, count, 16, 7, 6 * LANES)
    conv_table(table, flat, m2[...], 64)
    count = count - 2
    risen = jnp.concatenate(
        [rounded_relu(convolve(s, table, count, 16, tile)) for tile in range(5)], axis=1
    )
    second_half = lane_group(64, 64) == 1
    zeros = jnp.zeros((64, LANES), F32)
    for dx in range(2):
        for dy in range(2):
            value = picked(up_fine[...], dx, dy, 32)
            for cell, block in enumerate(
                (
                    zeros,
                    jnp.where(second_half, 0.0, value),
                    jnp.where(second_half, value, 0.0),
                    zeros,
                )
            ):
                lift[0, 64 * cell : 64 * (cell + 1), span_of(0)] = block.astype(BF)
            for tile in range(4):
                left = risen[:, tile * LANES : tile * LANES + DEPTH]
                rise = dot(left, lift[0, :DEPTH, :LANES])
                for y in range(count):
                    part = rise[16 * y : 16 * (y + 1)]
                    spread[tile, 2 * y + dy, pl.ds(2 + dx, 7, 2), :] = part[0:7]
                    spread[tile, 2 * y + dy, dx : dx + 1, :] = part[ends - 9 : ends - 8]
    count = 2 * count
    for tile in range(skip.shape[2] // LANES):
        total = spread[tile, :count, 0:16, :] + skip[:, :, span_of(tile)].astype(F32)
        wide[:count, 0:16, span_of(tile)] = total.astype(BF).astype(F32)
    stage(wide, s, count, 16, 0, 4 * LANES)
    conv_table(table, flat, f1[...], 32)
    count = count - 2
    for tile in range(4):
        value = rounded_relu(convolve(s, table, count, 16, tile, DEPTH if tile < 3 else LANES))
        wide[:count, 0:16, span_of(tile)] = value.astype(F32).reshape(count, 16, LANES)
    stage(wide, s, count, 16, 0, 4 * LANES)
    conv_table(table, flat, f2[...], 32)
    count = count - 2
    for tile in range(3):
        value = rounded_relu(convolve(s, table, count, 16, tile))
        out[:, :, span_of(tile)] = value.reshape(count, 16, LANES)


def call(kernel, outs, scratch, *args):
    return pl.pallas_call(
        kernel,
        out_shape=jax.tree.map(lambda out: pltpu.VMEM(out.shape, out.dtype), outs),
        in_specs=[pl.BlockSpec(memory_space=pltpu.VMEM)] * len(args),
        out_specs=jax.tree.map(lambda _: pl.BlockSpec(memory_space=pltpu.VMEM), outs),
        scratch_shapes=scratch,
        name=kernel.__name__,
    )(*[near_by(arg) for arg in args])


def near_by(arg):
    return pltpu.with_memory_space_constraint(arg, pltpu.MemorySpace.VMEM)


def exchange(head, tail, axis, route):
    ahead = [(source, route(source, 1)) for source in range(lax.axis_size(axis))]
    back = [(source, route(source, -1)) for source in range(lax.axis_size(axis))]
    return lax.ppermute(tail, axis, ahead), lax.ppermute(head, axis, back)


def gathered_body(
    features_in,
    encode_fine_first,
    encode_fine_second,
    reduce_fine,
    encode_middle_first,
    encode_middle_second,
    reduce_middle,
    bottom_first,
    bottom_second,
    expand_middle,
    decode_middle_first,
    decode_middle_second,
    expand_fine,
    decode_fine_first,
    decode_fine_second,
):
    devices = lax.axis_size("yz")
    across = math.isqrt(devices)
    fine, ext = features_in.shape[1], features_in.shape[2]
    mid = encode_middle_first.shape[0]
    halo = 4

    def around(source, step):
        return (source + step) % lax.axis_size("gx")

    def along_y(source, step):
        return (source + step * across) % devices

    def along_z(source, step):
        return source // across * across + (source % across + step) % across

    cores = lax.axis_size("gx")
    size = bottom_first.shape[0] // cores
    mine = lax.dynamic_slice_in_dim(bottom_first, lax.axis_index("gx") * size, size, 0)
    turned = lax.ppermute(
        mine, "yz", [(s, s % across * across + s // across) for s in range(devices)]
    )

    cells = features_in.reshape(fine, ext, ext, ext).transpose(2, 1, 3, 0)
    cells = cells.reshape(ext, ext, ext * fine)
    low, high = exchange(cells[:halo], cells[ext - halo :], "yz", along_y)
    cells = jnp.concatenate([low, cells, high], axis=0)
    edge = halo * fine
    low, high = exchange(cells[:, :, :edge], cells[:, :, -edge:], "yz", along_z)
    cells = jnp.concatenate([low, cells, high], axis=2)
    low, high = exchange(cells[:, :halo], cells[:, ext - halo :], "gx", around)

    seen = ext + 2 * halo
    side = ext // 2
    flat = pltpu.VMEM((27 * mid, LANES), F32)
    table = pltpu.VMEM((3 * DEPTH, 3 * LANES), BF)
    down = pltpu.VMEM((2 * DEPTH, 2 * LANES), BF)
    skip, small = call(
        fine_encoder,
        (
            jax.ShapeDtypeStruct((ext + 4, ext + 4, (ext + 4) * fine), BF),
            jax.ShapeDtypeStruct((side * side, side * mid), BF),
        ),
        [
            pltpu.VMEM((seen, 40, seen * fine), F32),
            pltpu.VMEM((3, seen * 32, seen * fine), BF),
            pltpu.VMEM((3, (seen - 2) * 16, seen * fine), BF),
            table,
            flat,
            down,
            pltpu.VMEM((2, side * 16, LANES), F32),
            pltpu.VMEM((side * side, side * mid), F32),
        ],
        low,
        cells,
        high,
        encode_fine_first,
        encode_fine_second,
        reduce_fine,
    )

    small, turned = lax.optimization_barrier((small, turned))
    swap = [(s, around(s, 1)) for s in range(cores)]
    swapped = lax.ppermute(turned, "gx", swap)
    reach = (side - 1) * side
    low, high = exchange(small[:reach], small[side:], "yz", along_y)
    small = jnp.concatenate([low, small, high], axis=0)
    low, high = exchange(small, small, "yz", along_z)
    own = jnp.concatenate([low, small, high], axis=1)
    other = lax.ppermute(own, "gx", swap)

    total = side * across
    half = total // 2
    layers, span = 3 * side - 2, 3 * side * mid
    window, sent = call(
        middle,
        (
            jax.ShapeDtypeStruct((layers - 4, 16, 14 * mid), BF),
            jax.ShapeDtypeStruct((devices * cores, 16, LANES), BF),
        ),
        [
            pltpu.VMEM((layers, 32, span), F32),
            pltpu.VMEM((3, layers * 16, span), BF),
            table,
            flat,
            down,
            pltpu.VMEM((layers - 4, 16, 14 * mid), BF),
            pltpu.VMEM((2, side * 8, LANES), F32),
            pltpu.VMEM((32, LANES), F32),
        ],
        own,
        other,
        encode_middle_first,
        encode_middle_second,
        reduce_middle,
    )
    sent, swapped = lax.optimization_barrier((sent, swapped))
    gathered = lax.all_to_all(sent, ("gx", "yz"), 0, 0)
    partial = call(
        bottom_start,
        jax.ShapeDtypeStruct((half * side, half * mid), BF),
        [
            pltpu.VMEM((half + 2, 32, half * mid + LANES), F32),
            pltpu.VMEM((3, (half + 2) * 16, half * mid + LANES), BF),
            table,
            flat,
            pltpu.VMEM((half * side, half * mid), F32),
        ],
        gathered,
        turned,
        swapped,
    )

    pieces = [partial] + [
        lax.ppermute(partial, "yz", [(s, s ^ turn) for s in range(devices)])
        for turn in range(1, across)
    ]
    sent = call(
        bottom,
        jax.ShapeDtypeStruct((devices, 88, LANES), BF),
        [
            pltpu.VMEM((half + 2, 32, half * mid + LANES), F32),
            pltpu.VMEM((3, (half + 2) * 16, half * mid + LANES), BF),
            table,
            flat,
            pltpu.VMEM((half + 5, 8, half * mid + 2 * LANES), F32),
            pltpu.VMEM((88, LANES), F32),
        ],
        *pieces,
        bottom_second,
    )
    near = lax.all_to_all(sent, "yz", 0, 0)
    far = lax.ppermute(near, "gx", swap)

    risen = call(
        decoder,
        jax.ShapeDtypeStruct((ext, 16, ext * fine), BF),
        [
            pltpu.VMEM((16, 32, 1024), F32),
            pltpu.VMEM((3, 256, 1024), BF),
            table,
            flat,
            pltpu.VMEM((4, across * DEPTH, 2 * LANES), BF),
            pltpu.VMEM((8, 16, 512), F32),
            pltpu.VMEM((8, 16, 32, LANES), F32),
        ],
        near,
        far,
        window,
        skip,
        expand_middle,
        decode_middle_first,
        decode_middle_second,
        expand_fine,
        decode_fine_first,
        decode_fine_second,
    )
    risen = risen[:, :ext].reshape(ext, ext, ext, fine).transpose(3, 1, 0, 2)
    return risen.reshape(1, fine, ext, ext * ext)


def with_halo(cells, sides, width):
    for axis, dim in sides:
        count = lax.axis_size(axis)
        head = lax.slice_in_dim(cells, 0, width, axis=dim)
        tail = lax.slice_in_dim(cells, cells.shape[dim] - width, cells.shape[dim], axis=dim)
        cells = jnp.concatenate(
            [
                lax.ppermute(tail, axis, [(i, (i + 1) % count) for i in range(count)]),
                cells,
                lax.ppermute(head, axis, [((i + 1) % count, i) for i in range(count)]),
            ],
            axis=dim,
        )
    return cells


def shortened(x):
    return jax.tree.map(lambda a: a.astype(jnp.bfloat16) if a.dtype == jnp.float32 else a, x)


def from_behind(block, axis, distance):
    devices = range(lax.axis_size(axis))
    route = [((i - distance) % len(devices), i) for i in devices]
    return lax.ppermute(block, axis, route)


def conv_taps(padded, weight, width_in):
    kernel = weight.reshape(weight.shape[0], width_in, 3, 3, 3)
    return lax.conv_general_dilated(
        padded[None],
        kernel,
        (1, 1, 1),
        "VALID",
        dimension_numbers=("NCDHW", "OIDHW", "NCDHW"),
        preferred_element_type=jnp.float32,
    )[0]


def rectify(running):
    return jnp.maximum(running, 0.0).astype(jnp.bfloat16)


def shrink(region, weight):
    kernel = weight.reshape(weight.shape[0], region.shape[0], 2, 2, 2)
    result = lax.conv_general_dilated(
        region[None],
        kernel,
        (2, 2, 2),
        "VALID",
        dimension_numbers=("NCDHW", "OIDHW", "NCDHW"),
        preferred_element_type=jnp.float32,
    )[0]
    return result.astype(jnp.bfloat16)


def expand(region, weight, skipped):
    width_in, extent_x, extent_y, extent_z = region.shape
    width_out = weight.shape[1] // 8
    columns = lax.dot_general(
        weight,
        region.reshape(width_in, -1),
        (((0,), (0,)), ((), ())),
        preferred_element_type=jnp.float32,
    )
    spread = columns.reshape(width_out, 2, 2, 2, extent_x, extent_y, extent_z).transpose(
        0, 4, 1, 5, 2, 6, 3
    )
    spread = spread.reshape(width_out, 2 * extent_x, 2 * extent_y, 2 * extent_z)
    return (spread + skipped.astype(jnp.float32)).astype(jnp.bfloat16)


def x_margins(region):
    return with_halo(region, (("gx", 1),), 1)


def from_peer(plane, offset):
    return from_behind(shortened(plane), "yz", offset).astype(plane.dtype)


def pad_block(region, across):
    extended = x_margins(region)
    below_face = from_peer(extended[:, :, -1:, :], across)
    above_face = from_peer(extended[:, :, :1, :], -across)
    extended = jnp.concatenate([below_face, extended, above_face], axis=2)
    column = lax.axis_index("yz") % across
    last_plane = extended[:, :, :, -1:]
    first_plane = extended[:, :, :, :1]
    behind = jnp.where(column == 0, from_peer(last_plane, 1 - across), from_peer(last_plane, 1))
    ahead = jnp.where(
        column == across - 1, from_peer(first_plane, across - 1), from_peer(first_plane, -1)
    )
    return jnp.concatenate([behind, extended, ahead], axis=3)


def conv_layer(region, weight, across):
    return rectify(conv_taps(pad_block(region, across), weight, region.shape[0]))


def assemble(stored):
    width_out = stored.shape[0] // 4
    return (
        stored.reshape(4, width_out, stored.shape[1])
        .transpose(1, 0, 2)
        .reshape(width_out, 4 * stored.shape[1])
    )


def bottom_layer(region, weight, across):
    width_in = region.shape[0]
    padded = pad_block(region, across)
    gathered = lax.all_gather(weight, "yz", axis=0, tiled=True)
    return rectify(conv_taps(padded, assemble(gathered), width_in))


def body(
    features_in,
    encode_fine_first,
    encode_fine_second,
    reduce_fine,
    encode_middle_first,
    encode_middle_second,
    reduce_middle,
    bottom_first,
    bottom_second,
    expand_middle,
    decode_middle_first,
    decode_middle_second,
    expand_fine,
    decode_fine_first,
    decode_fine_second,
):
    across = math.isqrt(lax.axis_size("yz"))
    width_fine, extent = (features_in.shape[1], features_in.shape[2])
    region = features_in.reshape(width_fine, extent, extent, extent)
    fine_skip = conv_layer(
        conv_layer(region, encode_fine_first, across), encode_fine_second, across
    )
    middle = shrink(fine_skip, reduce_fine)
    middle_skip = conv_layer(
        conv_layer(middle, encode_middle_first, across), encode_middle_second, across
    )
    bottom = shrink(middle_skip, reduce_middle)
    bottom = bottom_layer(bottom_layer(bottom, bottom_first, across), bottom_second, across)
    rising = expand(bottom, expand_middle, middle_skip)
    rising = conv_layer(
        conv_layer(rising, decode_middle_first, across), decode_middle_second, across
    )
    rising = expand(rising, expand_fine, fine_skip)
    rising = conv_layer(conv_layer(rising, decode_fine_first, across), decode_fine_second, across)
    return rising.reshape(1, width_fine, extent, extent * extent)


def solution(mesh):
    placed = (
        P("yz", None, "gx", None),
        P(),
        P(),
        P(),
        P(),
        P(),
        P(),
        P("yz", None),
        P("yz", None),
        P(),
        P(),
        P(),
        P(),
        P(),
        P(),
    )

    def chosen(*args):
        across = math.isqrt(lax.axis_size("yz"))
        stored, channels = args[7].shape[0], args[4].shape[0]
        gathered = lax.axis_size("gx") == 2 and stored == channels
        gathered = gathered and across == 4 and across * channels == args[6].shape[0]
        return (gathered_body if gathered else body)(*args)

    return jax.shard_map(
        chosen, mesh=mesh, in_specs=placed, out_specs=P("yz", None, "gx", None), check_vma=False
    )
```

```python
import math

import jax
import jax.numpy as jnp
from jax import lax
from jax.experimental import pallas as pl
from jax.experimental.pallas import tpu as pltpu
from jax.sharding import PartitionSpec as P

BF = jnp.bfloat16
F32 = jnp.float32
LANES = 128
DEPTH = 256
GRANT = 24 << 20


def dot(a, b):
    return lax.dot_general(a, b, (((1,), (0,)), ((), ())), preferred_element_type=F32)


def lane_group(rows, width):
    return lax.broadcasted_iota(jnp.int32, (rows, LANES), 1) // width


def transposed(flat, weight):
    columns = weight.shape[1]
    copies = jnp.concatenate([weight.astype(F32)] * (LANES // weight.shape[0]), axis=0)
    for start in range(0, columns, LANES):
        stop = min(start + LANES, columns)
        flat[start:stop, :] = copies[:, start:stop].T


def blocks(taps, cells, wide_in, wide_out, target):
    group = lane_group(wide_in, wide_out)
    for cell in range(cells):
        value = jnp.zeros((wide_in, LANES), F32)
        for k, tap in enumerate(taps):
            out = target(cell, k)
            if out is not None and 0 <= out < LANES // wide_out:
                value = jnp.where(group == out, tap, value)
        yield cell * wide_in, value.astype(BF)


def conv_table(table, flat, weight, channels):
    transposed(flat, weight)
    for dy in range(3):
        for dx in range(3):
            taps = [flat[pl.ds(9 * dx + 3 * dy + dz, channels, 27), :] for dz in range(3)]
            for row, block in blocks(
                taps, DEPTH // channels, channels, channels, lambda z, k: z - k
            ):
                row += DEPTH * dx
                table[row : row + channels, span_of(dy)] = block


def shrink_table(table, flat, weight, channels, offset):
    transposed(flat, weight)

    def target(z, k):
        return (z - offset - k) // 2 if (z - offset - k) % 2 == 0 else None

    for dx in range(2):
        for dy in range(2):
            taps = [flat[pl.ds(4 * dx + 2 * dy + dz, channels, 8), :] for dz in range(2)]
            for row, block in blocks(
                taps, DEPTH // channels, channels, weight.shape[0], target
            ):
                row += DEPTH * dy
                table[row : row + channels, LANES * dx : LANES * (dx + 1)] = block


def picked(weight, dx, dy, channels):
    rows = weight.shape[1]
    lane = lax.broadcasted_iota(jnp.int32, (rows, LANES), 1) % (2 * channels)
    row = lax.broadcasted_iota(jnp.int32, (rows, LANES), 0)
    wanted = 8 * (lane % channels) + 4 * dx + 2 * dy + lane // channels
    return dot(weight, (row == wanted).astype(BF))


def stage(wide, shifted, layers, rows, first, width, base=0):
    for y in range(layers):
        for d in range(3):
            shifted[d, y * rows : (y + 1) * rows, :width] = wide[
                base + y, first + d : first + d + rows, :width
            ].astype(BF)


def convolve(shifted, table, layers, rows, tile, depth=DEPTH):
    height = layers * rows
    start = tile * LANES
    left = jnp.concatenate(
        [shifted[dx, 0 : height + 2 * rows, start : start + depth] for dx in range(3)], axis=1
    )
    right = jnp.concatenate([table[DEPTH * dx : DEPTH * dx + depth, :] for dx in range(3)], axis=0)
    pair = dot(left[: height + rows], right[:, : 2 * LANES])
    last = dot(left[2 * rows :], right[:, 2 * LANES :])
    return pair[:height, :LANES] + pair[rows:, LANES:] + last


def rounded_relu(value):
    return jnp.maximum(value, 0.0).astype(BF)


def span_of(tile):
    return slice(tile * LANES, (tile + 1) * LANES)


def fine_tables(first, second, reduce, first_table, second_table, down, flat):
    conv_table(first_table, flat, first[...], 32)
    conv_table(second_table, flat, second[...], 32)
    shrink_table(down, flat, reduce[...], 32, 2)


def middle_tables(first, second, reduce, first_table, second_table, downs, flat):
    conv_table(first_table, flat, first[...], 64)
    conv_table(second_table, flat, second[...], 64)
    for quarter in range(downs.shape[0]):
        rows = reduce[64 * quarter : 64 * (quarter + 1), :]
        shrink_table(downs.at[quarter], flat, rows, 64, 0)


def decoder_tables(bottom, up, m1, m2, up_fine, f1, f2, *refs):
    bottom_table, lift, m1_table, m2_table, lift_fine, f1_table, f2_table, flat = refs
    conv_table(bottom_table, flat, bottom[...], 64)
    conv_table(m1_table, flat, m1[...], 64)
    conv_table(m2_table, flat, m2[...], 64)
    conv_table(f1_table, flat, f1[...], 32)
    conv_table(f2_table, flat, f2[...], 32)
    across = lift.shape[1] // DEPTH
    odd = lax.axis_index("yz") % across % 2
    blank = jnp.zeros((64, LANES), BF)
    second_half = lane_group(64, 64) == 1
    for dx in range(2):
        for dy in range(2):
            pair = picked(up[...], dx, dy, 64)
            for group in range(across):
                value = pair[64 * group : 64 * (group + 1)]
                for cell in range(4):
                    for half in range(2):
                        block = blank
                        if cell - half in (0, 1):
                            block = jnp.where(odd == cell - half, value, 0.0).astype(BF)
                        row = DEPTH * group + 64 * cell
                        lift[2 * dx + dy, row : row + 64, span_of(half)] = block
            value = picked(up_fine[...], dx, dy, 32)
            for cell, block in enumerate(
                (
                    blank,
                    jnp.where(second_half, 0.0, value).astype(BF),
                    jnp.where(second_half, value, 0.0).astype(BF),
                    blank,
                )
            ):
                lift_fine[2 * dx + dy, 64 * cell : 64 * (cell + 1), :] = block


def fine_encoder(
    low, mid, high, first_table, second_table, down, skip, small, wide, s1, s2, halves, flats
):
    layers, width = mid.shape[0], mid.shape[2]
    start = 0
    for piece in (low, mid, high):
        wide[:, start : start + piece.shape[1], :] = piece[...].astype(F32)
        start += piece.shape[1]
    stage(wide, s1, layers, 32, 0, width)
    inner = layers - 2
    tiles = width // LANES
    for tile in range(tiles):
        depth = DEPTH if tile + 1 < tiles else LANES
        value = rounded_relu(convolve(s1, first_table, inner, 32, tile, depth))
        wide[:inner, :32, span_of(tile)] = value.astype(F32).reshape(inner, 32, LANES)
    stage(wide, s2, inner, 16, 0, width)
    kept = inner - 2
    for tile in range(tiles - 1):
        value = rounded_relu(convolve(s2, second_table, kept, 16, tile))
        skip[:, :, span_of(tile)] = value.reshape(kept, 16, LANES)
    count = (kept - 4) // 2
    for tile in range(count // 2):
        left = jnp.concatenate(
            [
                jnp.concatenate(
                    [
                        skip[2 + 2 * y + dy, :, tile * LANES : tile * LANES + DEPTH]
                        for y in range(count)
                    ],
                    axis=0,
                )
                for dy in range(2)
            ],
            axis=1,
        )
        total = dot(left, down[...])
        halves[0] = total[:, :LANES]
        halves[1] = total[:, LANES:]
        for y in range(count):
            value = halves[0, pl.ds(16 * y + 2, count, 2), :]
            value = value + halves[1, pl.ds(16 * y + 3, count, 2), :]
            flats[count * y : count * (y + 1), span_of(tile)] = value
    small[...] = flats[...].astype(BF)


def wrap_rows(wide, layers, count):
    wide[1 : layers + 1, 7:8, :] = wide[1 : layers + 1, 7 + count : 8 + count, :]
    wide[1 : layers + 1, 8 + count : 9 + count, :] = wide[1 : layers + 1, 8:9, :]
    wide[0:1] = wide[layers : layers + 1]
    wide[layers + 1 : layers + 2] = wide[1:2]


def middle(
    own, other, first_table, second_table, downs, window, sent, wide, s, whole, halves, flats
):
    span = own.shape[1]
    side = span // 3 // 64
    reach = side - 1
    layers = side + 2 * reach
    near, far = own[...].astype(F32), other[...].astype(F32)
    for y in range(layers):
        start = side * y
        wide[y, 0:reach, :span] = far[start + 1 : start + side]
        wide[y, reach : reach + side, :span] = near[start : start + side]
        wide[y, reach + side : 2 * reach + side, :span] = far[start : start + reach]
    stage(wide, s, layers, 16, 0, span)
    layers -= 2
    tiles = span // LANES - 1
    for tile in range(tiles):
        value = rounded_relu(convolve(s, first_table, layers, 16, tile))
        wide[:layers, 0:16, span_of(tile)] = value.astype(F32).reshape(layers, 16, LANES)
    stage(wide, s, layers, 16, 0, tiles * LANES)
    layers -= 2
    for tile in range(tiles - 1):
        value = rounded_relu(convolve(s, second_table, layers, 16, tile)).reshape(layers, 16, LANES)
        whole[:, :, span_of(tile)] = value
        wide[:layers, 0:16, span_of(tile)] = value.astype(F32)
    width = window.shape[2]
    skipped = layers - side - 3
    wide[:layers, 16 : 16 + layers - 3, :width] = wide[:layers, 3:layers, :width]
    wide[:layers, 13 + layers : 16 + layers, :width] = wide[:layers, 0:3, :width]
    window[...] = wide[:layers, 16:32, :width].astype(BF)
    half = side // 2
    lefts = [
        jnp.concatenate(
            [
                jnp.concatenate(
                    [
                        whole[skipped + 2 * y + dy, :, (tile + 1) * DEPTH : (tile + 2) * DEPTH]
                        for y in range(half)
                    ],
                    axis=0,
                )
                for dy in range(2)
            ],
            axis=1,
        )
        for tile in range(2)
    ]
    across = downs.shape[0]
    for quarter in range(across):
        for tile, left in enumerate(lefts):
            total = dot(left, downs[quarter])
            halves[0] = total[:, :LANES]
            halves[1] = total[:, LANES:]
            for y in range(half):
                value = halves[0, pl.ds(16 * y + 3, half, 2), :]
                value = value + halves[1, pl.ds(16 * y + 4, half, 2), :]
                row = half * (half * tile + y)
                flats[row : row + half, :] = value
        count = half * half
        fold = (count + 1) // 2
        last = flats[count : count + 16, :]
        turn = pltpu.roll(last, 64, 1)
        flats[count : count + fold, :] = jnp.where(
            lane_group(fold, 64) == 0, last[:fold], turn[fold : 2 * fold]
        )
        result = flats[0 : sent.shape[1], :].astype(BF)
        for target in range(quarter, sent.shape[0], across):
            sent[target] = result


def bottom_start(gathered, turned, swapped, partial, wide, s, table, flat, flats):
    span = partial.shape[1]
    cells = span // 64
    side = cells // 2
    core = lax.axis_index("gx")
    devices = gathered.shape[0] // 2
    across = math.isqrt(devices)
    half = cells // across
    count = half * half
    fold = (count + 1) // 2
    low = lane_group(count, 64) == 0
    for part in range(2):
        base = (core if part == 0 else 1 - core) * devices
        for i in range(across):
            for j in range(0, across, 2):
                here = gathered[base + across * i + j].astype(F32)
                after = gathered[base + across * i + j + 1].astype(F32)
                here_turn, after_turn = pltpu.roll(here, 64, 1), pltpu.roll(after, 64, 1)

                def unfold(one, two):
                    return jnp.concatenate([one[count : count + fold], two[count : 2 * count - fold]])

                pieces = (
                    here[:count],
                    jnp.where(low, unfold(here, here_turn), after_turn[:count]),
                    jnp.where(low, after_turn[:count], unfold(after_turn, after)),
                )
                for turn, piece in enumerate(pieces):
                    tile = half * (j // 2) + turn
                    for y in range(half):
                        wide[
                            1 + half * i + y,
                            8 + half * part : 8 + half * (part + 1),
                            span_of(tile),
                        ] = piece[half * y : half * (y + 1)]
    wide[1 : cells + 1, 8 : 8 + side, span : span + LANES] = wide[
        1 : cells + 1, 8 : 8 + side, 0:LANES
    ]
    wrap_rows(wide, cells, side)
    stage(wide, s, cells + 2, 16, 7, span + LANES)
    mine, theirs = turned[...].astype(F32), swapped[...].astype(F32)
    is_first = core == 0
    stored = jnp.concatenate(
        [jnp.where(is_first, mine, theirs), jnp.where(is_first, theirs, mine)], axis=0
    )
    conv_table(table, flat, stored, 64)
    for tile in range(span // LANES):
        value = convolve(s, table, cells, 16, tile)
        for y in range(cells):
            flats[side * y : side * (y + 1), span_of(tile)] = value[16 * y : 16 * y + side]
    partial[...] = flats[...].astype(BF)


def bottom(*refs):
    *pieces, table, out, wide, s, whole, flats = refs
    span = pieces[0].shape[1]
    cells = span // 64
    side = cells // 2
    across = math.isqrt(out.shape[0])
    total = 0.0
    for piece in pieces:
        total = total + piece[...].astype(F32)
    total = jnp.maximum(total, 0.0).astype(BF).astype(F32)
    for y in range(cells):
        wide[1 + y, 8 : 8 + side, :span] = total[side * y : side * (y + 1)]
    wide[1 : cells + 1, 8 : 8 + side, span : span + LANES] = wide[
        1 : cells + 1, 8 : 8 + side, 0:LANES
    ]
    wrap_rows(wide, cells, side)
    stage(wide, s, cells + 2, 16, 7, span + LANES)
    for tile in range(span // LANES):
        value = convolve(s, table, cells, 16, tile).reshape(cells, 16, LANES)
        whole[2 : cells + 2, :, span_of(tile + 2)] = value[:, :8]
    whole[0:2] = whole[cells : cells + 2]
    whole[cells + 2 : cells + 5] = whole[2:5]
    whole[:, :, 0 : 2 * LANES] = whole[:, :, span : span + 2 * LANES]
    block = cells // across
    kept = side // 2
    layers = block + 4
    for i in range(across):
        for j in range(across):
            start = (block * j - block * j % 2) * 64
            for tile in range(4):
                for y in range(layers):
                    row = kept * (layers * tile + y)
                    flats[row : row + kept, :] = whole[
                        block * i + y,
                        0:kept,
                        start + tile * LANES : start + (tile + 1) * LANES,
                    ]
            out[i * across + j] = flats[...].astype(BF)


def decoder(
    near,
    far,
    window,
    skip,
    lift,
    m1_table,
    m2_table,
    lift_fine,
    f1_table,
    f2_table,
    out,
    wide,
    s,
    columns,
    spread,
):
    across = math.isqrt(near.shape[0])
    kept = window.shape[0] // 4
    layers = kept + 4
    groups = []
    for group in range(across):
        for part, parts in enumerate((near, far)):
            total = 0.0
            for k in range(across):
                total = total + parts[k * across + group].astype(F32)
            total = jnp.maximum(total, 0.0)
            for tile in range(4):
                for y in range(layers):
                    row = kept * (layers * tile + y)
                    columns[y, kept * part : kept * (part + 1), span_of(tile)] = total[
                        row : row + kept
                    ]
        groups.append(
            jnp.concatenate(
                [
                    columns[:layers, :, :512].astype(BF).reshape(layers * 16, 512),
                    jnp.zeros((layers * 16, LANES), BF),
                ],
                axis=1,
            )
        )
    for tile in range(4):
        left = jnp.concatenate(
            [g[:, tile * LANES : tile * LANES + DEPTH] for g in groups], axis=1
        )
        for dx in range(2):
            for dy in range(2):
                value = dot(left, lift[2 * dx + dy])
                for y in range(layers):
                    for half in range(2):
                        spread[2 * tile + half, 2 * y + dy, pl.ds(8 + dx, 2 * kept, 2), :] = value[
                            16 * y : 16 * y + 2 * kept, span_of(half)
                        ]
    count = window.shape[0]
    for tile in range(window.shape[2] // LANES):
        total = spread[tile, 1 : count + 1, 8:24, :] + window[:, :, span_of(tile)].astype(F32)
        wide[:count, 8:24, span_of(tile)] = total.astype(BF).astype(F32)
    ends = 8 + count
    wide[:, 7:8, :] = wide[:, ends - 1 : ends, :]
    wide[:, ends : ends + 1, :] = wide[:, 8:9, :]
    stage(wide, s, count, 16, 7, window.shape[2])
    count = count - 2
    for tile in range(6):
        value = rounded_relu(convolve(s, m1_table, count, 16, tile))
        wide[:count, 8:24, span_of(tile)] = value.astype(F32).reshape(count, 16, LANES)
    wide[:, 7:8, :] = wide[:, ends - 1 : ends, :]
    wide[:, ends : ends + 1, :] = wide[:, 8:9, :]
    stage(wide, s, count, 16, 7, 6 * LANES)
    count = count - 2
    risen = jnp.concatenate(
        [rounded_relu(convolve(s, m2_table, count, 16, tile)) for tile in range(5)], axis=1
    )
    for dx in range(2):
        for dy in range(2):
            for tile in range(4):
                left = risen[:, tile * LANES : tile * LANES + DEPTH]
                rise = dot(left, lift_fine[2 * dx + dy])
                for y in range(count):
                    part = rise[16 * y : 16 * (y + 1)]
                    spread[tile, 2 * y + dy, pl.ds(2 + dx, 7, 2), :] = part[0:7]
                    spread[tile, 2 * y + dy, dx : dx + 1, :] = part[ends - 9 : ends - 8]
    count = 2 * count
    for tile in range(skip.shape[2] // LANES):
        total = spread[tile, :count, 0:16, :] + skip[:, :, span_of(tile)].astype(F32)
        wide[:count, 0:16, span_of(tile)] = total.astype(BF).astype(F32)
    stage(wide, s, count, 16, 0, 4 * LANES)
    count = count - 2
    for tile in range(4):
        value = rounded_relu(convolve(s, f1_table, count, 16, tile, DEPTH if tile < 3 else LANES))
        wide[:count, 0:16, span_of(tile)] = value.astype(F32).reshape(count, 16, LANES)
    stage(wide, s, count, 16, 0, 4 * LANES)
    count = count - 2
    for tile in range(3):
        value = rounded_relu(convolve(s, f2_table, count, 16, tile))
        out[:, :, span_of(tile)] = value.reshape(count, 16, LANES)


def call(kernel, outs, scratch, *args):
    return pl.pallas_call(
        kernel,
        out_shape=jax.tree.map(lambda out: pltpu.VMEM(out.shape, out.dtype), outs),
        in_specs=[pl.BlockSpec(memory_space=pltpu.VMEM)] * len(args),
        out_specs=jax.tree.map(lambda _: pl.BlockSpec(memory_space=pltpu.VMEM), outs),
        scratch_shapes=scratch,
        compiler_params=pltpu.CompilerParams(vmem_limit_bytes=GRANT),
        name=kernel.__name__,
    )(*[near_by(arg) for arg in args])


def near_by(arg):
    return pltpu.with_memory_space_constraint(arg, pltpu.MemorySpace.VMEM)


def exchange(head, tail, axis, route):
    ahead = [(source, route(source, 1)) for source in range(lax.axis_size(axis))]
    back = [(source, route(source, -1)) for source in range(lax.axis_size(axis))]
    return lax.ppermute(tail, axis, ahead), lax.ppermute(head, axis, back)


def gathered_body(
    features_in,
    encode_fine_first,
    encode_fine_second,
    reduce_fine,
    encode_middle_first,
    encode_middle_second,
    reduce_middle,
    bottom_first,
    bottom_second,
    expand_middle,
    decode_middle_first,
    decode_middle_second,
    expand_fine,
    decode_fine_first,
    decode_fine_second,
):
    devices = lax.axis_size("yz")
    across = math.isqrt(devices)
    fine, ext = features_in.shape[1], features_in.shape[2]
    mid = encode_middle_first.shape[0]
    halo = 4

    def around(source, step):
        return (source + step) % lax.axis_size("gx")

    def along_y(source, step):
        return (source + step * across) % devices

    def along_z(source, step):
        return source // across * across + (source % across + step) % across

    seen = ext + 2 * halo
    side = ext // 2
    flat = pltpu.VMEM((27 * mid, LANES), F32)
    table = jax.ShapeDtypeStruct((3 * DEPTH, 3 * LANES), BF)
    down = jax.ShapeDtypeStruct((2 * DEPTH, 2 * LANES), BF)
    fine_tabs = call(
        fine_tables,
        (table, table, down),
        [flat],
        encode_fine_first,
        encode_fine_second,
        reduce_fine,
    )
    middle_tabs = call(
        middle_tables,
        (table, table, jax.ShapeDtypeStruct((across, *down.shape), BF)),
        [flat],
        encode_middle_first,
        encode_middle_second,
        reduce_middle,
    )
    bottom_tab, *decoder_tabs = call(
        decoder_tables,
        (
            table,
            jax.ShapeDtypeStruct((4, across * DEPTH, 2 * LANES), BF),
            table,
            table,
            jax.ShapeDtypeStruct((4, DEPTH, LANES), BF),
            table,
            table,
        ),
        [flat],
        bottom_second,
        expand_middle,
        decode_middle_first,
        decode_middle_second,
        expand_fine,
        decode_fine_first,
        decode_fine_second,
    )

    cores = lax.axis_size("gx")
    size = bottom_first.shape[0] // cores
    mine = lax.dynamic_slice_in_dim(bottom_first, lax.axis_index("gx") * size, size, 0)
    turned = lax.ppermute(
        mine, "yz", [(s, s % across * across + s // across) for s in range(devices)]
    )

    cells = features_in.reshape(fine, ext, ext, ext).transpose(2, 1, 3, 0)
    cells = cells.reshape(ext, ext, ext * fine)
    low, high = exchange(cells[:halo], cells[ext - halo :], "yz", along_y)
    cells = jnp.concatenate([low, cells, high], axis=0)
    edge = halo * fine
    low, high = exchange(cells[:, :, :edge], cells[:, :, -edge:], "yz", along_z)
    cells = jnp.concatenate([low, cells, high], axis=2)
    low, high = exchange(cells[:, :halo], cells[:, ext - halo :], "gx", around)

    skip, small = call(
        fine_encoder,
        (
            jax.ShapeDtypeStruct((ext + 4, ext + 4, (ext + 4) * fine), BF),
            jax.ShapeDtypeStruct((side * side, side * mid), BF),
        ),
        [
            pltpu.VMEM((seen, 40, seen * fine), F32),
            pltpu.VMEM((3, seen * 32, seen * fine), BF),
            pltpu.VMEM((3, (seen - 2) * 16, seen * fine), BF),
            pltpu.VMEM((2, side * 16, LANES), F32),
            pltpu.VMEM((side * side, side * mid), F32),
        ],
        low,
        cells,
        high,
        *fine_tabs,
    )

    small, turned = lax.optimization_barrier((small, turned))
    swap = [(s, around(s, 1)) for s in range(cores)]
    swapped = lax.ppermute(turned, "gx", swap)
    reach = (side - 1) * side
    low, high = exchange(small[:reach], small[side:], "yz", along_y)
    small = jnp.concatenate([low, small, high], axis=0)
    low, high = exchange(small, small, "yz", along_z)
    own = jnp.concatenate([low, small, high], axis=1)
    other = lax.ppermute(own, "gx", swap)

    total = side * across
    half = total // 2
    layers, span = 3 * side - 2, 3 * side * mid
    window, sent = call(
        middle,
        (
            jax.ShapeDtypeStruct((layers - 4, 16, 14 * mid), BF),
            jax.ShapeDtypeStruct((devices * cores, 16, LANES), BF),
        ),
        [
            pltpu.VMEM((layers, 32, span), F32),
            pltpu.VMEM((3, layers * 16, span), BF),
            pltpu.VMEM((layers - 4, 16, 14 * mid), BF),
            pltpu.VMEM((2, side * 8, LANES), F32),
            pltpu.VMEM((32, LANES), F32),
        ],
        own,
        other,
        *middle_tabs,
    )
    sent, swapped = lax.optimization_barrier((sent, swapped))
    gathered = lax.all_to_all(sent, ("gx", "yz"), 0, 0)
    partial = call(
        bottom_start,
        jax.ShapeDtypeStruct((half * side, half * mid), BF),
        [
            pltpu.VMEM((half + 2, 32, half * mid + LANES), F32),
            pltpu.VMEM((3, (half + 2) * 16, half * mid + LANES), BF),
            pltpu.VMEM(table.shape, BF),
            flat,
            pltpu.VMEM((half * side, half * mid), F32),
        ],
        gathered,
        turned,
        swapped,
    )

    pieces = [partial] + [
        lax.ppermute(partial, "yz", [(s, s ^ turn) for s in range(devices)])
        for turn in range(1, across)
    ]
    sent = call(
        bottom,
        jax.ShapeDtypeStruct((devices, 88, LANES), BF),
        [
            pltpu.VMEM((half + 2, 32, half * mid + LANES), F32),
            pltpu.VMEM((3, (half + 2) * 16, half * mid + LANES), BF),
            pltpu.VMEM((half + 5, 8, half * mid + 2 * LANES), F32),
            pltpu.VMEM((88, LANES), F32),
        ],
        *pieces,
        bottom_tab,
    )
    near = lax.all_to_all(sent, "yz", 0, 0)
    far = lax.ppermute(near, "gx", swap)

    risen = call(
        decoder,
        jax.ShapeDtypeStruct((ext, 16, ext * fine), BF),
        [
            pltpu.VMEM((16, 32, 1024), F32),
            pltpu.VMEM((3, 256, 1024), BF),
            pltpu.VMEM((8, 16, 512), F32),
            pltpu.VMEM((8, 16, 32, LANES), F32),
        ],
        near,
        far,
        window,
        skip,
        *decoder_tabs,
    )
    risen = risen[:, :ext].reshape(ext, ext, ext, fine).transpose(3, 1, 0, 2)
    return risen.reshape(1, fine, ext, ext * ext)


def with_halo(cells, sides, width):
    for axis, dim in sides:
        count = lax.axis_size(axis)
        head = lax.slice_in_dim(cells, 0, width, axis=dim)
        tail = lax.slice_in_dim(cells, cells.shape[dim] - width, cells.shape[dim], axis=dim)
        cells = jnp.concatenate(
            [
                lax.ppermute(tail, axis, [(i, (i + 1) % count) for i in range(count)]),
                cells,
                lax.ppermute(head, axis, [((i + 1) % count, i) for i in range(count)]),
            ],
            axis=dim,
        )
    return cells


def shortened(x):
    return jax.tree.map(lambda a: a.astype(jnp.bfloat16) if a.dtype == jnp.float32 else a, x)


def from_behind(block, axis, distance):
    devices = range(lax.axis_size(axis))
    route = [((i - distance) % len(devices), i) for i in devices]
    return lax.ppermute(block, axis, route)


def conv_taps(padded, weight, width_in):
    kernel = weight.reshape(weight.shape[0], width_in, 3, 3, 3)
    return lax.conv_general_dilated(
        padded[None],
        kernel,
        (1, 1, 1),
        "VALID",
        dimension_numbers=("NCDHW", "OIDHW", "NCDHW"),
        preferred_element_type=jnp.float32,
    )[0]


def rectify(running):
    return jnp.maximum(running, 0.0).astype(jnp.bfloat16)


def shrink(region, weight):
    kernel = weight.reshape(weight.shape[0], region.shape[0], 2, 2, 2)
    result = lax.conv_general_dilated(
        region[None],
        kernel,
        (2, 2, 2),
        "VALID",
        dimension_numbers=("NCDHW", "OIDHW", "NCDHW"),
        preferred_element_type=jnp.float32,
    )[0]
    return result.astype(jnp.bfloat16)


def expand(region, weight, skipped):
    width_in, extent_x, extent_y, extent_z = region.shape
    width_out = weight.shape[1] // 8
    columns = lax.dot_general(
        weight,
        region.reshape(width_in, -1),
        (((0,), (0,)), ((), ())),
        preferred_element_type=jnp.float32,
    )
    spread = columns.reshape(width_out, 2, 2, 2, extent_x, extent_y, extent_z).transpose(
        0, 4, 1, 5, 2, 6, 3
    )
    spread = spread.reshape(width_out, 2 * extent_x, 2 * extent_y, 2 * extent_z)
    return (spread + skipped.astype(jnp.float32)).astype(jnp.bfloat16)


def x_margins(region):
    return with_halo(region, (("gx", 1),), 1)


def from_peer(plane, offset):
    return from_behind(shortened(plane), "yz", offset).astype(plane.dtype)


def pad_block(region, across):
    extended = x_margins(region)
    below_face = from_peer(extended[:, :, -1:, :], across)
    above_face = from_peer(extended[:, :, :1, :], -across)
    extended = jnp.concatenate([below_face, extended, above_face], axis=2)
    column = lax.axis_index("yz") % across
    last_plane = extended[:, :, :, -1:]
    first_plane = extended[:, :, :, :1]
    behind = jnp.where(column == 0, from_peer(last_plane, 1 - across), from_peer(last_plane, 1))
    ahead = jnp.where(
        column == across - 1, from_peer(first_plane, across - 1), from_peer(first_plane, -1)
    )
    return jnp.concatenate([behind, extended, ahead], axis=3)


def conv_layer(region, weight, across):
    return rectify(conv_taps(pad_block(region, across), weight, region.shape[0]))


def assemble(stored):
    width_out = stored.shape[0] // 4
    return (
        stored.reshape(4, width_out, stored.shape[1])
        .transpose(1, 0, 2)
        .reshape(width_out, 4 * stored.shape[1])
    )


def bottom_layer(region, weight, across):
    width_in = region.shape[0]
    padded = pad_block(region, across)
    gathered = lax.all_gather(weight, "yz", axis=0, tiled=True)
    return rectify(conv_taps(padded, assemble(gathered), width_in))


def body(
    features_in,
    encode_fine_first,
    encode_fine_second,
    reduce_fine,
    encode_middle_first,
    encode_middle_second,
    reduce_middle,
    bottom_first,
    bottom_second,
    expand_middle,
    decode_middle_first,
    decode_middle_second,
    expand_fine,
    decode_fine_first,
    decode_fine_second,
):
    across = math.isqrt(lax.axis_size("yz"))
    width_fine, extent = (features_in.shape[1], features_in.shape[2])
    region = features_in.reshape(width_fine, extent, extent, extent)
    fine_skip = conv_layer(
        conv_layer(region, encode_fine_first, across), encode_fine_second, across
    )
    middle = shrink(fine_skip, reduce_fine)
    middle_skip = conv_layer(
        conv_layer(middle, encode_middle_first, across), encode_middle_second, across
    )
    bottom = shrink(middle_skip, reduce_middle)
    bottom = bottom_layer(bottom_layer(bottom, bottom_first, across), bottom_second, across)
    rising = expand(bottom, expand_middle, middle_skip)
    rising = conv_layer(
        conv_layer(rising, decode_middle_first, across), decode_middle_second, across
    )
    rising = expand(rising, expand_fine, fine_skip)
    rising = conv_layer(conv_layer(rising, decode_fine_first, across), decode_fine_second, across)
    return rising.reshape(1, width_fine, extent, extent * extent)


def solution(mesh):
    placed = (
        P("yz", None, "gx", None),
        P(),
        P(),
        P(),
        P(),
        P(),
        P(),
        P("yz", None),
        P("yz", None),
        P(),
        P(),
        P(),
        P(),
        P(),
        P(),
    )

    def chosen(*args):
        across = math.isqrt(lax.axis_size("yz"))
        stored, channels = args[7].shape[0], args[4].shape[0]
        gathered = lax.axis_size("gx") == 2 and stored == channels
        gathered = gathered and across == 4 and across * channels == args[6].shape[0]
        return (gathered_body if gathered else body)(*args)

    return jax.shard_map(
        chosen, mesh=mesh, in_specs=placed, out_specs=P("yz", None, "gx", None), check_vma=False
    )
```

```python
import math

import jax
import jax.numpy as jnp
from jax import lax
from jax.experimental import pallas as pl
from jax.experimental.pallas import tpu as pltpu
from jax.sharding import PartitionSpec as P

BF = jnp.bfloat16
F32 = jnp.float32
LANES = 128
DEPTH = 256
GRANT = 24 << 20


def dot(a, b):
    return lax.dot_general(a, b, (((1,), (0,)), ((), ())), preferred_element_type=F32)


def lane_group(rows, width):
    return lax.broadcasted_iota(jnp.int32, (rows, LANES), 1) // width


def transposed(flat, weight):
    columns = weight.shape[1]
    copies = jnp.concatenate([weight.astype(F32)] * (LANES // weight.shape[0]), axis=0)
    for start in range(0, columns, LANES):
        stop = min(start + LANES, columns)
        flat[start:stop, :] = copies[:, start:stop].T


def blocks(taps, cells, wide_in, wide_out, target):
    group = lane_group(wide_in, wide_out)
    for cell in range(cells):
        value = jnp.zeros((wide_in, LANES), F32)
        for k, tap in enumerate(taps):
            out = target(cell, k)
            if out is not None and 0 <= out < LANES // wide_out:
                value = jnp.where(group == out, tap, value)
        yield cell * wide_in, value.astype(BF)


def conv_table(table, flat, weight, channels):
    transposed(flat, weight)
    for dy in range(3):
        for dx in range(3):
            taps = [flat[pl.ds(9 * dx + 3 * dy + dz, channels, 27), :] for dz in range(3)]
            for row, block in blocks(
                taps, DEPTH // channels, channels, channels, lambda z, k: z - k
            ):
                row += DEPTH * dx
                table[row : row + channels, span_of(dy)] = block


def shrink_table(table, flat, weight, channels, offset):
    transposed(flat, weight)

    def target(z, k):
        return (z - offset - k) // 2 if (z - offset - k) % 2 == 0 else None

    for dx in range(2):
        for dy in range(2):
            taps = [flat[pl.ds(4 * dx + 2 * dy + dz, channels, 8), :] for dz in range(2)]
            for row, block in blocks(
                taps, DEPTH // channels, channels, weight.shape[0], target
            ):
                row += DEPTH * dy
                table[row : row + channels, LANES * dx : LANES * (dx + 1)] = block


def picked(weight, dx, dy, channels):
    rows = weight.shape[1]
    lane = lax.broadcasted_iota(jnp.int32, (rows, LANES), 1) % (2 * channels)
    row = lax.broadcasted_iota(jnp.int32, (rows, LANES), 0)
    wanted = 8 * (lane % channels) + 4 * dx + 2 * dy + lane // channels
    return dot(weight, (row == wanted).astype(BF))


def stage(wide, shifted, layers, rows, first, width, base=0):
    for y in range(layers):
        for d in range(3):
            shifted[d, y * rows : (y + 1) * rows, :width] = wide[
                base + y, first + d : first + d + rows, :width
            ].astype(BF)


def convolve(shifted, table, layers, rows, tile, depth=DEPTH):
    height = layers * rows
    start = tile * LANES
    left = jnp.concatenate(
        [shifted[dx, 0 : height + 2 * rows, start : start + depth] for dx in range(3)], axis=1
    )
    right = jnp.concatenate([table[DEPTH * dx : DEPTH * dx + depth, :] for dx in range(3)], axis=0)
    pair = dot(left[: height + rows], right[:, : 2 * LANES])
    last = dot(left[2 * rows :], right[:, 2 * LANES :])
    return pair[:height, :LANES] + pair[rows:, LANES:] + last


def rounded_relu(value):
    return jnp.maximum(value, 0.0).astype(BF)


def span_of(tile):
    return slice(tile * LANES, (tile + 1) * LANES)


def fine_tables(first, second, reduce, first_table, second_table, down, flat):
    conv_table(first_table, flat, first[...], 32)
    conv_table(second_table, flat, second[...], 32)
    shrink_table(down, flat, reduce[...], 32, 2)


def middle_tables(first, second, reduce, first_table, second_table, down, flat):
    conv_table(first_table, flat, first[...], 64)
    conv_table(second_table, flat, second[...], 64)
    across = reduce.shape[0] // 64
    column = lax.axis_index("yz") % across
    rows = reduce[pl.ds(pl.multiple_of(column * 64, 64), 64), :]
    shrink_table(down, flat, rows, 64, 0)


def decoder_tables(bottom, up, m1, m2, up_fine, f1, f2, *refs):
    bottom_table, lift, m1_table, m2_table, lift_fine, f1_table, f2_table, flat = refs
    conv_table(bottom_table, flat, bottom[...], 64)
    conv_table(m1_table, flat, m1[...], 64)
    conv_table(m2_table, flat, m2[...], 64)
    conv_table(f1_table, flat, f1[...], 32)
    conv_table(f2_table, flat, f2[...], 32)
    across = lift.shape[1] // DEPTH
    odd = lax.axis_index("yz") % across % 2
    blank = jnp.zeros((64, LANES), BF)
    second_half = lane_group(64, 64) == 1
    for dx in range(2):
        for dy in range(2):
            pair = picked(up[...], dx, dy, 64)
            for group in range(across):
                value = pair[64 * group : 64 * (group + 1)]
                for cell in range(4):
                    for half in range(2):
                        block = blank
                        if cell - half in (0, 1):
                            block = jnp.where(odd == cell - half, value, 0.0).astype(BF)
                        row = DEPTH * group + 64 * cell
                        lift[2 * dx + dy, row : row + 64, span_of(half)] = block
            value = picked(up_fine[...], dx, dy, 32)
            for cell, block in enumerate(
                (
                    blank,
                    jnp.where(second_half, 0.0, value).astype(BF),
                    jnp.where(second_half, value, 0.0).astype(BF),
                    blank,
                )
            ):
                lift_fine[2 * dx + dy, 64 * cell : 64 * (cell + 1), :] = block


def fine_encoder(
    low, mid, high, first_table, second_table, down, skip, small, wide, s1, s2, halves, flats
):
    layers, width = mid.shape[0], mid.shape[2]
    start = 0
    for piece in (low, mid, high):
        wide[:, start : start + piece.shape[1], :] = piece[...].astype(F32)
        start += piece.shape[1]
    stage(wide, s1, layers, 32, 0, width)
    inner = layers - 2
    tiles = width // LANES
    for tile in range(tiles):
        depth = DEPTH if tile + 1 < tiles else LANES
        value = rounded_relu(convolve(s1, first_table, inner, 32, tile, depth))
        wide[:inner, :32, span_of(tile)] = value.astype(F32).reshape(inner, 32, LANES)
    stage(wide, s2, inner, 16, 0, width)
    kept = inner - 2
    for tile in range(tiles - 1):
        value = rounded_relu(convolve(s2, second_table, kept, 16, tile))
        skip[:, :, span_of(tile)] = value.reshape(kept, 16, LANES)
    count = (kept - 4) // 2
    for tile in range(count // 2):
        left = jnp.concatenate(
            [
                jnp.concatenate(
                    [
                        skip[2 + 2 * y + dy, :, tile * LANES : tile * LANES + DEPTH]
                        for y in range(count)
                    ],
                    axis=0,
                )
                for dy in range(2)
            ],
            axis=1,
        )
        total = dot(left, down[...])
        halves[0] = total[:, :LANES]
        halves[1] = total[:, LANES:]
        for y in range(count):
            value = halves[0, pl.ds(16 * y + 2, count, 2), :]
            value = value + halves[1, pl.ds(16 * y + 3, count, 2), :]
            row = count * (count * tile + y)
            flats[row : row + count, :] = value
    result = flats[...].astype(BF)
    for copy in range(small.shape[0]):
        small[copy] = result


def wrap_rows(wide, layers, count):
    wide[1 : layers + 1, 7:8, :] = wide[1 : layers + 1, 7 + count : 8 + count, :]
    wide[1 : layers + 1, 8 + count : 9 + count, :] = wide[1 : layers + 1, 8:9, :]
    wide[0:1] = wide[layers : layers + 1]
    wide[layers + 1 : layers + 2] = wide[1:2]


def wrap_x(wide, layers, count):
    wide[:layers, 7:8, :] = wide[:layers, 7 + count : 8 + count, :]
    wide[:layers, 8 + count : 9 + count, :] = wide[:layers, 8:9, :]


def middle(
    own, other, first_table, second_table, down, window, shrunk, wide, s, whole, halves, flats
):
    across = math.isqrt(own.shape[0])
    side = window.shape[0] // 2
    lanes = side * 64
    span = across * lanes
    place, core = lax.axis_index("yz"), lax.axis_index("gx")
    row, column = place // across, place % across
    layers = 3 * side
    for k in range(3):
        i = (row + across // 2 * core + k + across - 1) % across
        for spot, j in enumerate([across - 1] + list(range(across))):
            start = spot * lanes
            size = min(lanes, span + LANES - start)
            for part, gathered in enumerate((own, other)):
                block = gathered[i * across + j].astype(F32)
                for y in range(side):
                    for tile in range(size // LANES):
                        first = side * (side * tile + y)
                        wide[
                            side * k + y,
                            8 + side * part : 8 + side * (part + 1),
                            start + LANES * tile : start + LANES * (tile + 1),
                        ] = block[first : first + side]
    wrap_x(wide, layers, 2 * side)
    stage(wide, s, layers, 16, 7, span + LANES)
    layers -= 2
    for tile in range(span // LANES):
        value = rounded_relu(convolve(s, first_table, layers, 16, tile))
        wide[:layers, 8:24, span_of(tile)] = value.astype(F32).reshape(layers, 16, LANES)
    wide[:layers, :, span : span + LANES] = wide[:layers, :, 0:LANES]
    wrap_x(wide, layers, 2 * side)
    stage(wide, s, layers, 16, 7, span + LANES)
    layers -= 2
    for tile in range(span // LANES):
        value = rounded_relu(convolve(s, second_table, layers, 16, tile))
        whole[:, :, span_of(tile)] = value.reshape(layers, 16, LANES)
    whole[:, :, span : span + 512] = whole[:, :, 0:512]
    window[...] = whole[
        1 : 1 + window.shape[0],
        :,
        pl.ds(pl.multiple_of(column * lanes, LANES), window.shape[2]),
    ]
    for tile in range(shrunk.shape[1] // LANES):
        left = jnp.concatenate(
            [
                jnp.concatenate(
                    [
                        whole[2 * y + dy, :, tile * DEPTH : (tile + 1) * DEPTH]
                        for y in range(side)
                    ],
                    axis=0,
                )
                for dy in range(2)
            ],
            axis=1,
        )
        total = dot(left, down[...])
        halves[0] = total[:, :LANES]
        halves[1] = total[:, LANES:]
        for y in range(side):
            value = halves[0, pl.ds(16 * y, side, 2), :]
            value = value + halves[1, pl.ds(16 * y + 1, side, 2), :]
            flats[side * y : side * (y + 1), span_of(tile)] = value
    shrunk[...] = flats[...].astype(BF)


def bottom_start(near, far, turned, swapped, partial, wide, s, table, flat, flats):
    span = partial.shape[1]
    cells = span // 64
    side = cells // 2
    core = lax.axis_index("gx")
    across = cells * 2 // side
    block = side // 2
    row = lax.axis_index("yz") // across
    for part, given in enumerate((near, far)):
        values = given[...].astype(F32)
        half = core if part == 0 else 1 - core
        for y in range(side):
            layer = (block * row + side * half + y + cells - 2) % cells + 1
            value = values[side * y : side * (y + 1)]
            if part == 1:
                value = jnp.concatenate([value[block:], value[:block]], axis=0)
            wide[pl.ds(layer, 1), 8 : 8 + side, :span] = value[None]
    wide[1 : cells + 1, 8 : 8 + side, span : span + LANES] = wide[
        1 : cells + 1, 8 : 8 + side, 0:LANES
    ]
    wrap_rows(wide, cells, side)
    stage(wide, s, cells + 2, 16, 7, span + LANES)
    mine, theirs = turned[...].astype(F32), swapped[...].astype(F32)
    is_first = core == 0
    stored = jnp.concatenate(
        [jnp.where(is_first, mine, theirs), jnp.where(is_first, theirs, mine)], axis=0
    )
    conv_table(table, flat, stored, 64)
    for tile in range(span // LANES):
        value = convolve(s, table, cells, 16, tile)
        for y in range(cells):
            flats[side * y : side * (y + 1), span_of(tile)] = value[16 * y : 16 * y + side]
    partial[...] = flats[...].astype(BF)


def bottom(*refs):
    *pieces, table, out, wide, s, whole, flats = refs
    span = pieces[0].shape[1]
    cells = span // 64
    side = cells // 2
    across = math.isqrt(out.shape[0])
    total = 0.0
    for piece in pieces:
        total = total + piece[...].astype(F32)
    total = jnp.maximum(total, 0.0).astype(BF).astype(F32)
    for y in range(cells):
        wide[1 + y, 8 : 8 + side, :span] = total[side * y : side * (y + 1)]
    wide[1 : cells + 1, 8 : 8 + side, span : span + LANES] = wide[
        1 : cells + 1, 8 : 8 + side, 0:LANES
    ]
    wrap_rows(wide, cells, side)
    stage(wide, s, cells + 2, 16, 7, span + LANES)
    for tile in range(span // LANES):
        value = convolve(s, table, cells, 16, tile).reshape(cells, 16, LANES)
        whole[2 : cells + 2, :, span_of(tile + 1)] = value[:, :8]
    whole[0:2] = whole[cells : cells + 2]
    whole[cells + 2 : cells + 5] = whole[2:5]
    whole[:, :, 0:LANES] = whole[:, :, span : span + LANES]
    whole[:, :, span + LANES : span + 512] = whole[:, :, LANES:512]
    block = cells // across
    kept = side // 2
    layers = block + 4
    for i in range(across):
        for j in range(across):
            start = (block * j - block * j % 2) * 64
            for tile in range(4):
                for y in range(layers):
                    row = kept * (layers * tile + y)
                    flats[row : row + kept, :] = whole[
                        block * i + y,
                        0:kept,
                        start + tile * LANES : start + (tile + 1) * LANES,
                    ]
            out[i * across + j] = flats[...].astype(BF)


def decoder(
    near,
    far,
    window,
    far_window,
    skip,
    lift,
    m1_table,
    m2_table,
    lift_fine,
    f1_table,
    f2_table,
    out,
    wide,
    s,
    columns,
    spread,
):
    across = math.isqrt(near.shape[0])
    kept = window.shape[0] // 4
    layers = kept + 4
    groups = []
    for group in range(across):
        for part, parts in enumerate((near, far)):
            total = 0.0
            for k in range(across):
                total = total + parts[k * across + group].astype(F32)
            total = jnp.maximum(total, 0.0)
            for tile in range(4):
                for y in range(layers):
                    row = kept * (layers * tile + y)
                    columns[y, kept * part : kept * (part + 1), span_of(tile)] = total[
                        row : row + kept
                    ]
        groups.append(
            jnp.concatenate(
                [
                    columns[:layers, :, :512].astype(BF).reshape(layers * 16, 512),
                    jnp.zeros((layers * 16, LANES), BF),
                ],
                axis=1,
            )
        )
    for tile in range(4):
        left = jnp.concatenate(
            [g[:, tile * LANES : tile * LANES + DEPTH] for g in groups], axis=1
        )
        for dx in range(2):
            for dy in range(2):
                value = dot(left, lift[2 * dx + dy])
                for y in range(layers):
                    for half in range(2):
                        spread[2 * tile + half, 2 * y + dy, pl.ds(8 + dx, 2 * kept, 2), :] = value[
                            16 * y : 16 * y + 2 * kept, span_of(half)
                        ]
    count = window.shape[0]
    is_first = lax.axis_index("gx") == 0
    for tile in range(window.shape[2] // LANES):
        theirs = far_window[:, :, span_of(tile)].astype(F32)
        wide[:count, 8 : 8 + count // 2, span_of(tile)] = theirs[:, count // 2 : count]
        wide[:count, 8 + count // 2 : 8 + count, span_of(tile)] = theirs[:, : count // 2]
        kept_here = jnp.where(
            is_first, window[:, :, span_of(tile)].astype(F32), wide[:count, 8:24, span_of(tile)]
        )
        total = spread[tile, 1 : count + 1, 8:24, :] + kept_here
        wide[:count, 8:24, span_of(tile)] = total.astype(BF).astype(F32)
    ends = 8 + count
    wide[:, 7:8, :] = wide[:, ends - 1 : ends, :]
    wide[:, ends : ends + 1, :] = wide[:, 8:9, :]
    stage(wide, s, count, 16, 7, window.shape[2])
    count = count - 2
    for tile in range(6):
        value = rounded_relu(convolve(s, m1_table, count, 16, tile))
        wide[:count, 8:24, span_of(tile)] = value.astype(F32).reshape(count, 16, LANES)
    wide[:, 7:8, :] = wide[:, ends - 1 : ends, :]
    wide[:, ends : ends + 1, :] = wide[:, 8:9, :]
    stage(wide, s, count, 16, 7, 6 * LANES)
    count = count - 2
    risen = jnp.concatenate(
        [rounded_relu(convolve(s, m2_table, count, 16, tile)) for tile in range(5)], axis=1
    )
    for dx in range(2):
        for dy in range(2):
            for tile in range(4):
                left = risen[:, tile * LANES : tile * LANES + DEPTH]
                rise = dot(left, lift_fine[2 * dx + dy])
                for y in range(count):
                    part = rise[16 * y : 16 * (y + 1)]
                    spread[tile, 2 * y + dy, pl.ds(2 + dx, 7, 2), :] = part[0:7]
                    spread[tile, 2 * y + dy, dx : dx + 1, :] = part[ends - 9 : ends - 8]
    count = 2 * count
    for tile in range(skip.shape[2] // LANES):
        total = spread[tile, :count, 0:16, :] + skip[:, :, span_of(tile)].astype(F32)
        wide[:count, 0:16, span_of(tile)] = total.astype(BF).astype(F32)
    stage(wide, s, count, 16, 0, 4 * LANES)
    count = count - 2
    for tile in range(4):
        value = rounded_relu(convolve(s, f1_table, count, 16, tile, DEPTH if tile < 3 else LANES))
        wide[:count, 0:16, span_of(tile)] = value.astype(F32).reshape(count, 16, LANES)
    stage(wide, s, count, 16, 0, 4 * LANES)
    count = count - 2
    for tile in range(3):
        value = rounded_relu(convolve(s, f2_table, count, 16, tile))
        out[:, :, span_of(tile)] = value.reshape(count, 16, LANES)


def call(kernel, outs, scratch, *args):
    return pl.pallas_call(
        kernel,
        out_shape=jax.tree.map(lambda out: pltpu.VMEM(out.shape, out.dtype), outs),
        in_specs=[pl.BlockSpec(memory_space=pltpu.VMEM)] * len(args),
        out_specs=jax.tree.map(lambda _: pl.BlockSpec(memory_space=pltpu.VMEM), outs),
        scratch_shapes=scratch,
        compiler_params=pltpu.CompilerParams(vmem_limit_bytes=GRANT),
        name=kernel.__name__,
    )(*[near_by(arg) for arg in args])


def near_by(arg):
    return pltpu.with_memory_space_constraint(arg, pltpu.MemorySpace.VMEM)


def exchange(head, tail, axis, route):
    ahead = [(source, route(source, 1)) for source in range(lax.axis_size(axis))]
    back = [(source, route(source, -1)) for source in range(lax.axis_size(axis))]
    return lax.ppermute(tail, axis, ahead), lax.ppermute(head, axis, back)


def gathered_body(
    features_in,
    encode_fine_first,
    encode_fine_second,
    reduce_fine,
    encode_middle_first,
    encode_middle_second,
    reduce_middle,
    bottom_first,
    bottom_second,
    expand_middle,
    decode_middle_first,
    decode_middle_second,
    expand_fine,
    decode_fine_first,
    decode_fine_second,
):
    devices = lax.axis_size("yz")
    across = math.isqrt(devices)
    fine, ext = features_in.shape[1], features_in.shape[2]
    mid = encode_middle_first.shape[0]
    halo = 4

    def around(source, step):
        return (source + step) % lax.axis_size("gx")

    def along_y(source, step):
        return (source + step * across) % devices

    def along_z(source, step):
        return source // across * across + (source % across + step) % across

    seen = ext + 2 * halo
    side = ext // 2
    flat = pltpu.VMEM((27 * mid, LANES), F32)
    table = jax.ShapeDtypeStruct((3 * DEPTH, 3 * LANES), BF)
    down = jax.ShapeDtypeStruct((2 * DEPTH, 2 * LANES), BF)
    fine_tabs = call(
        fine_tables,
        (table, table, down),
        [flat],
        encode_fine_first,
        encode_fine_second,
        reduce_fine,
    )
    middle_tabs = call(
        middle_tables,
        (table, table, down),
        [flat],
        encode_middle_first,
        encode_middle_second,
        reduce_middle,
    )
    bottom_tab, *decoder_tabs = call(
        decoder_tables,
        (
            table,
            jax.ShapeDtypeStruct((4, across * DEPTH, 2 * LANES), BF),
            table,
            table,
            jax.ShapeDtypeStruct((4, DEPTH, LANES), BF),
            table,
            table,
        ),
        [flat],
        bottom_second,
        expand_middle,
        decode_middle_first,
        decode_middle_second,
        expand_fine,
        decode_fine_first,
        decode_fine_second,
    )

    cores = lax.axis_size("gx")
    size = bottom_first.shape[0] // cores
    mine = lax.dynamic_slice_in_dim(bottom_first, lax.axis_index("gx") * size, size, 0)
    turned = lax.ppermute(
        mine, "yz", [(s, s % across * across + s // across) for s in range(devices)]
    )

    cells = features_in.reshape(fine, ext, ext, ext).transpose(2, 1, 3, 0)
    cells = cells.reshape(ext, ext, ext * fine)
    low, high = exchange(cells[:halo], cells[ext - halo :], "yz", along_y)
    cells = jnp.concatenate([low, cells, high], axis=0)
    edge = halo * fine
    low, high = exchange(cells[:, :, :edge], cells[:, :, -edge:], "yz", along_z)
    cells = jnp.concatenate([low, cells, high], axis=2)
    low, high = exchange(cells[:, :halo], cells[:, ext - halo :], "gx", around)

    skip, small = call(
        fine_encoder,
        (
            jax.ShapeDtypeStruct((ext + 4, ext + 4, (ext + 4) * fine), BF),
            jax.ShapeDtypeStruct((devices, 112, LANES), BF),
        ),
        [
            pltpu.VMEM((seen, 40, seen * fine), F32),
            pltpu.VMEM((3, seen * 32, seen * fine), BF),
            pltpu.VMEM((3, (seen - 2) * 16, seen * fine), BF),
            pltpu.VMEM((2, side * 16, LANES), F32),
            pltpu.VMEM((112, LANES), F32),
        ],
        low,
        cells,
        high,
        *fine_tabs,
    )

    small, turned = lax.optimization_barrier((small, turned))
    swap = [(s, around(s, 1)) for s in range(cores)]
    swapped = lax.ppermute(turned, "gx", swap)
    own = lax.all_to_all(small, "yz", 0, 0)
    other = lax.ppermute(own, "gx", swap)

    total = side * across
    half = total // 2
    span = total * mid
    window, shrunk = call(
        middle,
        (
            jax.ShapeDtypeStruct((2 * side, 16, 14 * mid), BF),
            jax.ShapeDtypeStruct((side * side, half * mid), BF),
        ),
        [
            pltpu.VMEM((3 * side, 32, span + LANES), F32),
            pltpu.VMEM((3, 3 * side * 16, span + LANES), BF),
            pltpu.VMEM((3 * side - 4, 16, span + 512), BF),
            pltpu.VMEM((2, side * 16, LANES), F32),
            pltpu.VMEM((side * side, half * mid), F32),
        ],
        own,
        other,
        *middle_tabs,
    )
    far_shrunk = lax.ppermute(shrunk, "gx", swap)
    partial = call(
        bottom_start,
        jax.ShapeDtypeStruct((half * side, half * mid), BF),
        [
            pltpu.VMEM((half + 2, 32, half * mid + LANES), F32),
            pltpu.VMEM((3, (half + 2) * 16, half * mid + LANES), BF),
            pltpu.VMEM(table.shape, BF),
            flat,
            pltpu.VMEM((half * side, half * mid), F32),
        ],
        shrunk,
        far_shrunk,
        turned,
        swapped,
    )
    partial, window = lax.optimization_barrier((partial, window))
    far_window = lax.ppermute(window, "gx", swap)

    pieces = [partial] + [
        lax.ppermute(partial, "yz", [(s, s ^ turn) for s in range(devices)])
        for turn in range(1, across)
    ]
    sent = call(
        bottom,
        jax.ShapeDtypeStruct((devices, 88, LANES), BF),
        [
            pltpu.VMEM((half + 2, 32, half * mid + LANES), F32),
            pltpu.VMEM((3, (half + 2) * 16, half * mid + LANES), BF),
            pltpu.VMEM((half + 5, 8, half * mid + 512), F32),
            pltpu.VMEM((88, LANES), F32),
        ],
        *pieces,
        bottom_tab,
    )
    sent, far_window = lax.optimization_barrier((sent, far_window))
    near = lax.all_to_all(sent, "yz", 0, 0)
    far = lax.ppermute(near, "gx", swap)

    risen = call(
        decoder,
        jax.ShapeDtypeStruct((ext, 16, ext * fine), BF),
        [
            pltpu.VMEM((16, 32, 1024), F32),
            pltpu.VMEM((3, 256, 1024), BF),
            pltpu.VMEM((8, 16, 512), F32),
            pltpu.VMEM((8, 16, 32, LANES), F32),
        ],
        near,
        far,
        window,
        far_window,
        skip,
        *decoder_tabs,
    )
    risen = risen[:, :ext].reshape(ext, ext, ext, fine).transpose(3, 1, 0, 2)
    return risen.reshape(1, fine, ext, ext * ext)


def with_halo(cells, sides, width):
    for axis, dim in sides:
        count = lax.axis_size(axis)
        head = lax.slice_in_dim(cells, 0, width, axis=dim)
        tail = lax.slice_in_dim(cells, cells.shape[dim] - width, cells.shape[dim], axis=dim)
        cells = jnp.concatenate(
            [
                lax.ppermute(tail, axis, [(i, (i + 1) % count) for i in range(count)]),
                cells,
                lax.ppermute(head, axis, [((i + 1) % count, i) for i in range(count)]),
            ],
            axis=dim,
        )
    return cells


def shortened(x):
    return jax.tree.map(lambda a: a.astype(jnp.bfloat16) if a.dtype == jnp.float32 else a, x)


def from_behind(block, axis, distance):
    devices = range(lax.axis_size(axis))
    route = [((i - distance) % len(devices), i) for i in devices]
    return lax.ppermute(block, axis, route)


def conv_taps(padded, weight, width_in):
    kernel = weight.reshape(weight.shape[0], width_in, 3, 3, 3)
    return lax.conv_general_dilated(
        padded[None],
        kernel,
        (1, 1, 1),
        "VALID",
        dimension_numbers=("NCDHW", "OIDHW", "NCDHW"),
        preferred_element_type=jnp.float32,
    )[0]


def rectify(running):
    return jnp.maximum(running, 0.0).astype(jnp.bfloat16)


def shrink(region, weight):
    kernel = weight.reshape(weight.shape[0], region.shape[0], 2, 2, 2)
    result = lax.conv_general_dilated(
        region[None],
        kernel,
        (2, 2, 2),
        "VALID",
        dimension_numbers=("NCDHW", "OIDHW", "NCDHW"),
        preferred_element_type=jnp.float32,
    )[0]
    return result.astype(jnp.bfloat16)


def expand(region, weight, skipped):
    width_in, extent_x, extent_y, extent_z = region.shape
    width_out = weight.shape[1] // 8
    columns = lax.dot_general(
        weight,
        region.reshape(width_in, -1),
        (((0,), (0,)), ((), ())),
        preferred_element_type=jnp.float32,
    )
    spread = columns.reshape(width_out, 2, 2, 2, extent_x, extent_y, extent_z).transpose(
        0, 4, 1, 5, 2, 6, 3
    )
    spread = spread.reshape(width_out, 2 * extent_x, 2 * extent_y, 2 * extent_z)
    return (spread + skipped.astype(jnp.float32)).astype(jnp.bfloat16)


def x_margins(region):
    return with_halo(region, (("gx", 1),), 1)


def from_peer(plane, offset):
    return from_behind(shortened(plane), "yz", offset).astype(plane.dtype)


def pad_block(region, across):
    extended = x_margins(region)
    below_face = from_peer(extended[:, :, -1:, :], across)
    above_face = from_peer(extended[:, :, :1, :], -across)
    extended = jnp.concatenate([below_face, extended, above_face], axis=2)
    column = lax.axis_index("yz") % across
    last_plane = extended[:, :, :, -1:]
    first_plane = extended[:, :, :, :1]
    behind = jnp.where(column == 0, from_peer(last_plane, 1 - across), from_peer(last_plane, 1))
    ahead = jnp.where(
        column == across - 1, from_peer(first_plane, across - 1), from_peer(first_plane, -1)
    )
    return jnp.concatenate([behind, extended, ahead], axis=3)


def conv_layer(region, weight, across):
    return rectify(conv_taps(pad_block(region, across), weight, region.shape[0]))


def assemble(stored):
    width_out = stored.shape[0] // 4
    return (
        stored.reshape(4, width_out, stored.shape[1])
        .transpose(1, 0, 2)
        .reshape(width_out, 4 * stored.shape[1])
    )


def bottom_layer(region, weight, across):
    width_in = region.shape[0]
    padded = pad_block(region, across)
    gathered = lax.all_gather(weight, "yz", axis=0, tiled=True)
    return rectify(conv_taps(padded, assemble(gathered), width_in))


def body(
    features_in,
    encode_fine_first,
    encode_fine_second,
    reduce_fine,
    encode_middle_first,
    encode_middle_second,
    reduce_middle,
    bottom_first,
    bottom_second,
    expand_middle,
    decode_middle_first,
    decode_middle_second,
    expand_fine,
    decode_fine_first,
    decode_fine_second,
):
    across = math.isqrt(lax.axis_size("yz"))
    width_fine, extent = (features_in.shape[1], features_in.shape[2])
    region = features_in.reshape(width_fine, extent, extent, extent)
    fine_skip = conv_layer(
        conv_layer(region, encode_fine_first, across), encode_fine_second, across
    )
    middle = shrink(fine_skip, reduce_fine)
    middle_skip = conv_layer(
        conv_layer(middle, encode_middle_first, across), encode_middle_second, across
    )
    bottom = shrink(middle_skip, reduce_middle)
    bottom = bottom_layer(bottom_layer(bottom, bottom_first, across), bottom_second, across)
    rising = expand(bottom, expand_middle, middle_skip)
    rising = conv_layer(
        conv_layer(rising, decode_middle_first, across), decode_middle_second, across
    )
    rising = expand(rising, expand_fine, fine_skip)
    rising = conv_layer(conv_layer(rising, decode_fine_first, across), decode_fine_second, across)
    return rising.reshape(1, width_fine, extent, extent * extent)


def solution(mesh):
    placed = (
        P("yz", None, "gx", None),
        P(),
        P(),
        P(),
        P(),
        P(),
        P(),
        P("yz", None),
        P("yz", None),
        P(),
        P(),
        P(),
        P(),
        P(),
        P(),
    )

    def chosen(*args):
        across = math.isqrt(lax.axis_size("yz"))
        stored, channels = args[7].shape[0], args[4].shape[0]
        gathered = lax.axis_size("gx") == 2 and stored == channels
        gathered = gathered and across == 4 and across * channels == args[6].shape[0]
        return (gathered_body if gathered else body)(*args)

    return jax.shard_map(
        chosen, mesh=mesh, in_specs=placed, out_specs=P("yz", None, "gx", None), check_vma=False
    )
```

```python
import math

import jax
import jax.numpy as jnp
from jax import lax
from jax.experimental import pallas as pl
from jax.experimental.pallas import tpu as pltpu
from jax.sharding import PartitionSpec as P

BF = jnp.bfloat16
F32 = jnp.float32
LANES = 128
DEPTH = 256
GRANT = 24 << 20


def dot(a, b):
    return lax.dot_general(a, b, (((1,), (0,)), ((), ())), preferred_element_type=F32)


def lane_group(rows, width):
    return lax.broadcasted_iota(jnp.int32, (rows, LANES), 1) // width


def transposed(flat, weight):
    columns = weight.shape[1]
    copies = jnp.concatenate([weight.astype(F32)] * (LANES // weight.shape[0]), axis=0)
    for start in range(0, columns, LANES):
        stop = min(start + LANES, columns)
        flat[start:stop, :] = copies[:, start:stop].T


def blocks(taps, cells, wide_in, wide_out, target):
    group = lane_group(wide_in, wide_out)
    for cell in range(cells):
        value = jnp.zeros((wide_in, LANES), F32)
        for k, tap in enumerate(taps):
            out = target(cell, k)
            if out is not None and 0 <= out < LANES // wide_out:
                value = jnp.where(group == out, tap, value)
        yield cell * wide_in, value.astype(BF)


def conv_table(table, flat, weight, channels):
    transposed(flat, weight)
    for dy in range(3):
        for dx in range(3):
            taps = [flat[pl.ds(9 * dx + 3 * dy + dz, channels, 27), :] for dz in range(3)]
            for row, block in blocks(
                taps, DEPTH // channels, channels, channels, lambda z, k: z - k
            ):
                row += DEPTH * dx
                table[row : row + channels, span_of(dy)] = block


def shrink_table(table, flat, weight, channels, offset):
    transposed(flat, weight)

    def target(z, k):
        return (z - offset - k) // 2 if (z - offset - k) % 2 == 0 else None

    for dx in range(2):
        for dy in range(2):
            taps = [flat[pl.ds(4 * dx + 2 * dy + dz, channels, 8), :] for dz in range(2)]
            for row, block in blocks(
                taps, DEPTH // channels, channels, weight.shape[0], target
            ):
                row += DEPTH * dy
                table[row : row + channels, LANES * dx : LANES * (dx + 1)] = block


def picked(weight, dx, dy, channels):
    rows = weight.shape[1]
    lane = lax.broadcasted_iota(jnp.int32, (rows, LANES), 1) % (2 * channels)
    row = lax.broadcasted_iota(jnp.int32, (rows, LANES), 0)
    wanted = 8 * (lane % channels) + 4 * dx + 2 * dy + lane // channels
    return dot(weight, (row == wanted).astype(BF))


def stage(wide, shifted, layers, rows, first, width, base=0):
    for y in range(layers):
        for d in range(3):
            shifted[d, y * rows : (y + 1) * rows, :width] = wide[
                base + y, first + d : first + d + rows, :width
            ].astype(BF)


def convolve(shifted, table, layers, rows, tile, depth=DEPTH):
    height = layers * rows
    start = tile * LANES
    left = jnp.concatenate(
        [shifted[dx, 0 : height + 2 * rows, start : start + depth] for dx in range(3)], axis=1
    )
    right = jnp.concatenate([table[DEPTH * dx : DEPTH * dx + depth, :] for dx in range(3)], axis=0)
    pair = dot(left[: height + rows], right[:, : 2 * LANES])
    last = dot(left[2 * rows :], right[:, 2 * LANES :])
    return pair[:height, :LANES] + pair[rows:, LANES:] + last


def relu(value):
    return jnp.maximum(value, 0.0)


def rounded_relu(value):
    return jnp.maximum(value, 0.0).astype(BF)


def span_of(tile):
    return slice(tile * LANES, (tile + 1) * LANES)


def fine_tables(first, second, reduce, first_table, second_table, down, flat):
    conv_table(first_table, flat, first[...], 32)
    conv_table(second_table, flat, second[...], 32)
    shrink_table(down, flat, reduce[...], 32, 2)


def middle_tables(first, second, reduce, first_table, second_table, down, flat):
    conv_table(first_table, flat, first[...], 64)
    conv_table(second_table, flat, second[...], 64)
    across = reduce.shape[0] // 64
    column = lax.axis_index("yz") % across
    rows = reduce[pl.ds(pl.multiple_of(column * 64, 64), 64), :]
    shrink_table(down, flat, rows, 64, 0)


def decoder_tables(bottom, up, m1, m2, up_fine, f1, f2, *refs):
    bottom_table, lift, m1_table, m2_table, lift_fine, f1_table, f2_table, flat = refs
    conv_table(bottom_table, flat, bottom[...], 64)
    conv_table(m1_table, flat, m1[...], 64)
    conv_table(m2_table, flat, m2[...], 64)
    conv_table(f1_table, flat, f1[...], 32)
    conv_table(f2_table, flat, f2[...], 32)
    across = lift.shape[1] // DEPTH
    odd = lax.axis_index("yz") % across % 2
    blank = jnp.zeros((64, LANES), BF)
    second_half = lane_group(64, 64) == 1
    for dx in range(2):
        for dy in range(2):
            pair = picked(up[...], dx, dy, 64)
            for group in range(across):
                value = pair[64 * group : 64 * (group + 1)]
                for cell in range(4):
                    for half in range(2):
                        block = blank
                        if cell - half in (0, 1):
                            block = jnp.where(odd == cell - half, value, 0.0).astype(BF)
                        row = DEPTH * group + 64 * cell
                        lift[2 * dx + dy, row : row + 64, span_of(half)] = block
            value = picked(up_fine[...], dx, dy, 32)
            for cell, block in enumerate(
                (
                    blank,
                    jnp.where(second_half, 0.0, value).astype(BF),
                    jnp.where(second_half, value, 0.0).astype(BF),
                    blank,
                )
            ):
                lift_fine[2 * dx + dy, 64 * cell : 64 * (cell + 1), :] = block


def fine_encoder(
    low, mid, high, first_table, second_table, down, skip, small, wide, s1, s2, halves, flats
):
    layers, width = mid.shape[0], mid.shape[2]
    start = 0
    for piece in (low, mid, high):
        wide[:, start : start + piece.shape[1], :] = piece[...].astype(F32)
        start += piece.shape[1]
    stage(wide, s1, layers, 32, 0, width)
    inner = layers - 2
    tiles = width // LANES
    for tile in range(tiles):
        depth = DEPTH if tile + 1 < tiles else LANES
        value = relu(convolve(s1, first_table, inner, 32, tile, depth))
        wide[:inner, :32, span_of(tile)] = value.reshape(inner, 32, LANES)
    stage(wide, s2, inner, 16, 0, width)
    kept = inner - 2
    for tile in range(tiles - 1):
        value = rounded_relu(convolve(s2, second_table, kept, 16, tile))
        skip[:, :, span_of(tile)] = value.reshape(kept, 16, LANES)
    count = (kept - 4) // 2
    for tile in range(count // 2):
        left = jnp.concatenate(
            [
                jnp.concatenate(
                    [
                        skip[2 + 2 * y + dy, :, tile * LANES : tile * LANES + DEPTH]
                        for y in range(count)
                    ],
                    axis=0,
                )
                for dy in range(2)
            ],
            axis=1,
        )
        total = dot(left, down[...])
        halves[0] = total[:, :LANES]
        halves[1] = total[:, LANES:]
        for y in range(count):
            value = halves[0, pl.ds(16 * y + 2, count, 2), :]
            value = value + halves[1, pl.ds(16 * y + 3, count, 2), :]
            row = count * (count * tile + y)
            flats[row : row + count, :] = value
    result = flats[...].astype(BF)
    for copy in range(small.shape[0]):
        small[copy] = result


def wrap_rows(wide, layers, count):
    wide[1 : layers + 1, 7:8, :] = wide[1 : layers + 1, 7 + count : 8 + count, :]
    wide[1 : layers + 1, 8 + count : 9 + count, :] = wide[1 : layers + 1, 8:9, :]
    wide[0:1] = wide[layers : layers + 1]
    wide[layers + 1 : layers + 2] = wide[1:2]


def wrap_x(wide, layers, count):
    wide[:layers, 7:8, :] = wide[:layers, 7 + count : 8 + count, :]
    wide[:layers, 8 + count : 9 + count, :] = wide[:layers, 8:9, :]


def middle(
    own, other, first_table, second_table, down, window, shrunk, wide, s, whole, halves, flats
):
    across = math.isqrt(own.shape[0])
    side = window.shape[0] // 2
    lanes = side * 64
    span = across * lanes
    place, core = lax.axis_index("yz"), lax.axis_index("gx")
    row, column = place // across, place % across
    layers = 3 * side - 1
    for k in range(3):
        i = (row + across // 2 * core + k + across - 1) % across
        for spot, j in enumerate([across - 1] + list(range(across))):
            start = spot * lanes
            size = min(lanes, span + LANES - start)
            for part, gathered in enumerate((own, other)):
                block = gathered[i * across + j].astype(F32)
                for y in range(min(side, layers - side * k)):
                    for tile in range(size // LANES):
                        first = side * (side * tile + y)
                        wide[
                            side * k + y,
                            8 + side * part : 8 + side * (part + 1),
                            start + LANES * tile : start + LANES * (tile + 1),
                        ] = block[first : first + side]
    wrap_x(wide, layers, 2 * side)
    stage(wide, s, layers, 16, 7, span + LANES)
    layers -= 2
    for tile in range(span // LANES):
        value = relu(convolve(s, first_table, layers, 16, tile))
        wide[:layers, 8:24, span_of(tile)] = value.reshape(layers, 16, LANES)
    wide[:layers, :, span : span + LANES] = wide[:layers, :, 0:LANES]
    wrap_x(wide, layers, 2 * side)
    stage(wide, s, layers, 16, 7, span + LANES)
    layers -= 2
    for tile in range(span // LANES):
        value = rounded_relu(convolve(s, second_table, layers, 16, tile))
        whole[:, :, span_of(tile)] = value.reshape(layers, 16, LANES)
    whole[:, :, span : span + 512] = whole[:, :, 0:512]
    window[...] = whole[
        1 : 1 + window.shape[0],
        :,
        pl.ds(pl.multiple_of(column * lanes, LANES), window.shape[2]),
    ]
    for tile in range(shrunk.shape[1] // LANES):
        left = jnp.concatenate(
            [
                jnp.concatenate(
                    [
                        whole[2 * y + dy, :, tile * DEPTH : (tile + 1) * DEPTH]
                        for y in range(side)
                    ],
                    axis=0,
                )
                for dy in range(2)
            ],
            axis=1,
        )
        total = dot(left, down[...])
        halves[0] = total[:, :LANES]
        halves[1] = total[:, LANES:]
        for y in range(side):
            value = halves[0, pl.ds(16 * y, side, 2), :]
            value = value + halves[1, pl.ds(16 * y + 1, side, 2), :]
            flats[side * y : side * (y + 1), span_of(tile)] = value
    shrunk[...] = flats[...].astype(BF)


def bottom_start(near, far, turned, swapped, partial, wide, s, table, flat, flats):
    span = partial.shape[1]
    cells = span // 64
    side = cells // 2
    core = lax.axis_index("gx")
    across = cells * 2 // side
    block = side // 2
    row = lax.axis_index("yz") // across
    for part, given in enumerate((near, far)):
        values = given[...].astype(F32)
        half = core if part == 0 else 1 - core
        for y in range(side):
            layer = (block * row + side * half + y + cells - 2) % cells + 1
            value = values[side * y : side * (y + 1)]
            if part == 1:
                value = jnp.concatenate([value[block:], value[:block]], axis=0)
            wide[pl.ds(layer, 1), 8 : 8 + side, :span] = value[None]
    wide[1 : cells + 1, 8 : 8 + side, span : span + LANES] = wide[
        1 : cells + 1, 8 : 8 + side, 0:LANES
    ]
    wrap_rows(wide, cells, side)
    stage(wide, s, cells + 2, 16, 7, span + LANES)
    mine, theirs = turned[...].astype(F32), swapped[...].astype(F32)
    is_first = core == 0
    stored = jnp.concatenate(
        [jnp.where(is_first, mine, theirs), jnp.where(is_first, theirs, mine)], axis=0
    )
    conv_table(table, flat, stored, 64)
    for tile in range(span // LANES):
        value = convolve(s, table, cells, 16, tile)
        for y in range(cells):
            flats[side * y : side * (y + 1), span_of(tile)] = value[16 * y : 16 * y + side]
    partial[...] = flats[...].astype(BF)


def bottom(*refs):
    *pieces, table, out, wide, s, whole, flats = refs
    span = pieces[0].shape[1]
    cells = span // 64
    side = cells // 2
    across = math.isqrt(out.shape[0])
    total = 0.0
    for piece in pieces:
        total = total + piece[...].astype(F32)
    total = relu(total)
    for y in range(cells):
        wide[1 + y, 8 : 8 + side, :span] = total[side * y : side * (y + 1)]
    wide[1 : cells + 1, 8 : 8 + side, span : span + LANES] = wide[
        1 : cells + 1, 8 : 8 + side, 0:LANES
    ]
    wrap_rows(wide, cells, side)
    stage(wide, s, cells + 2, 16, 7, span + LANES)
    for tile in range(span // LANES):
        value = convolve(s, table, cells, 16, tile).reshape(cells, 16, LANES)
        whole[2 : cells + 2, :, span_of(tile + 1)] = value[:, :8]
    whole[0:2] = whole[cells : cells + 2]
    whole[cells + 2 : cells + 5] = whole[2:5]
    whole[:, :, 0:LANES] = whole[:, :, span : span + LANES]
    whole[:, :, span + LANES : span + 512] = whole[:, :, LANES:512]
    block = cells // across
    kept = side // 2
    layers = block + 4
    for i in range(across):
        for j in range(across):
            start = (block * j - block * j % 2) * 64
            for tile in range(4):
                for y in range(layers):
                    row = kept * (layers * tile + y)
                    flats[row : row + kept, :] = whole[
                        block * i + y,
                        0:kept,
                        start + tile * LANES : start + (tile + 1) * LANES,
                    ]
            out[i * across + j] = flats[...].astype(BF)


def decoder(
    near,
    far,
    window,
    far_window,
    skip,
    lift,
    m1_table,
    m2_table,
    lift_fine,
    f1_table,
    f2_table,
    out,
    wide,
    s,
    columns,
    spread,
):
    across = math.isqrt(near.shape[0])
    kept = window.shape[0] // 4
    layers = kept + 4
    groups = []
    for group in range(across):
        for part, parts in enumerate((near, far)):
            total = 0.0
            for k in range(across):
                total = total + parts[k * across + group].astype(F32)
            total = jnp.maximum(total, 0.0)
            for tile in range(4):
                for y in range(layers):
                    row = kept * (layers * tile + y)
                    columns[y, kept * part : kept * (part + 1), span_of(tile)] = total[
                        row : row + kept
                    ]
        groups.append(
            jnp.concatenate(
                [
                    columns[:layers, :, :512].astype(BF).reshape(layers * 16, 512),
                    jnp.zeros((layers * 16, LANES), BF),
                ],
                axis=1,
            )
        )
    for tile in range(4):
        left = jnp.concatenate(
            [g[:, tile * LANES : tile * LANES + DEPTH] for g in groups], axis=1
        )
        for dx in range(2):
            for dy in range(2):
                value = dot(left, lift[2 * dx + dy])
                for y in range(layers):
                    for half in range(2):
                        spread[2 * tile + half, 2 * y + dy, pl.ds(8 + dx, 2 * kept, 2), :] = value[
                            16 * y : 16 * y + 2 * kept, span_of(half)
                        ]
    count = window.shape[0]
    is_first = lax.axis_index("gx") == 0
    for tile in range(window.shape[2] // LANES):
        theirs = far_window[:, :, span_of(tile)].astype(F32)
        wide[:count, 8 : 8 + count // 2, span_of(tile)] = theirs[:, count // 2 : count]
        wide[:count, 8 + count // 2 : 8 + count, span_of(tile)] = theirs[:, : count // 2]
        kept_here = jnp.where(
            is_first, window[:, :, span_of(tile)].astype(F32), wide[:count, 8:24, span_of(tile)]
        )
        total = spread[tile, 1 : count + 1, 8:24, :] + kept_here
        wide[:count, 8:24, span_of(tile)] = total
    ends = 8 + count
    wide[:, 7:8, :] = wide[:, ends - 1 : ends, :]
    wide[:, ends : ends + 1, :] = wide[:, 8:9, :]
    stage(wide, s, count, 16, 7, window.shape[2])
    count = count - 2
    for tile in range(6):
        value = relu(convolve(s, m1_table, count, 16, tile))
        wide[:count, 8:24, span_of(tile)] = value.reshape(count, 16, LANES)
    wide[:, 7:8, :] = wide[:, ends - 1 : ends, :]
    wide[:, ends : ends + 1, :] = wide[:, 8:9, :]
    stage(wide, s, count, 16, 7, 6 * LANES)
    count = count - 2
    risen = jnp.concatenate(
        [rounded_relu(convolve(s, m2_table, count, 16, tile)) for tile in range(5)], axis=1
    )
    for dx in range(2):
        for dy in range(2):
            for tile in range(4):
                left = risen[:, tile * LANES : tile * LANES + DEPTH]
                rise = dot(left, lift_fine[2 * dx + dy])
                for y in range(count):
                    part = rise[16 * y : 16 * (y + 1)]
                    spread[tile, 2 * y + dy, pl.ds(2 + dx, 7, 2), :] = part[0:7]
                    spread[tile, 2 * y + dy, dx : dx + 1, :] = part[ends - 9 : ends - 8]
    count = 2 * count
    for tile in range(skip.shape[2] // LANES):
        total = spread[tile, :count, 0:16, :] + skip[:, :, span_of(tile)].astype(F32)
        wide[:count, 0:16, span_of(tile)] = total
    stage(wide, s, count, 16, 0, 4 * LANES)
    count = count - 2
    for tile in range(4):
        value = relu(convolve(s, f1_table, count, 16, tile, DEPTH if tile < 3 else LANES))
        wide[:count, 0:16, span_of(tile)] = value.reshape(count, 16, LANES)
    stage(wide, s, count, 16, 0, 4 * LANES)
    count = count - 2
    for tile in range(3):
        value = rounded_relu(convolve(s, f2_table, count, 16, tile))
        out[:, :, span_of(tile)] = value.reshape(count, 16, LANES)


def call(kernel, outs, scratch, *args):
    return pl.pallas_call(
        kernel,
        out_shape=jax.tree.map(lambda out: pltpu.VMEM(out.shape, out.dtype), outs),
        in_specs=[pl.BlockSpec(memory_space=pltpu.VMEM)] * len(args),
        out_specs=jax.tree.map(lambda _: pl.BlockSpec(memory_space=pltpu.VMEM), outs),
        scratch_shapes=scratch,
        compiler_params=pltpu.CompilerParams(vmem_limit_bytes=GRANT),
        name=kernel.__name__,
    )(*[near_by(arg) for arg in args])


def near_by(arg):
    return pltpu.with_memory_space_constraint(arg, pltpu.MemorySpace.VMEM)


def exchange(head, tail, axis, route):
    ahead = [(source, route(source, 1)) for source in range(lax.axis_size(axis))]
    back = [(source, route(source, -1)) for source in range(lax.axis_size(axis))]
    return lax.ppermute(tail, axis, ahead), lax.ppermute(head, axis, back)


def gathered_body(
    features_in,
    encode_fine_first,
    encode_fine_second,
    reduce_fine,
    encode_middle_first,
    encode_middle_second,
    reduce_middle,
    bottom_first,
    bottom_second,
    expand_middle,
    decode_middle_first,
    decode_middle_second,
    expand_fine,
    decode_fine_first,
    decode_fine_second,
):
    devices = lax.axis_size("yz")
    across = math.isqrt(devices)
    fine, ext = features_in.shape[1], features_in.shape[2]
    mid = encode_middle_first.shape[0]
    halo = 4

    def around(source, step):
        return (source + step) % lax.axis_size("gx")

    def along_y(source, step):
        return (source + step * across) % devices

    def along_z(source, step):
        return source // across * across + (source % across + step) % across

    seen = ext + 2 * halo
    side = ext // 2
    flat = pltpu.VMEM((27 * mid, LANES), F32)
    table = jax.ShapeDtypeStruct((3 * DEPTH, 3 * LANES), BF)
    down = jax.ShapeDtypeStruct((2 * DEPTH, 2 * LANES), BF)
    fine_tabs = call(
        fine_tables,
        (table, table, down),
        [flat],
        encode_fine_first,
        encode_fine_second,
        reduce_fine,
    )
    middle_tabs = call(
        middle_tables,
        (table, table, down),
        [flat],
        encode_middle_first,
        encode_middle_second,
        reduce_middle,
    )
    bottom_tab, *decoder_tabs = call(
        decoder_tables,
        (
            table,
            jax.ShapeDtypeStruct((4, across * DEPTH, 2 * LANES), BF),
            table,
            table,
            jax.ShapeDtypeStruct((4, DEPTH, LANES), BF),
            table,
            table,
        ),
        [flat],
        bottom_second,
        expand_middle,
        decode_middle_first,
        decode_middle_second,
        expand_fine,
        decode_fine_first,
        decode_fine_second,
    )

    cores = lax.axis_size("gx")
    size = bottom_first.shape[0] // cores
    mine = lax.dynamic_slice_in_dim(bottom_first, lax.axis_index("gx") * size, size, 0)
    turned = lax.ppermute(
        mine, "yz", [(s, s % across * across + s // across) for s in range(devices)]
    )

    cells = features_in.reshape(fine, ext, ext, ext).transpose(2, 1, 3, 0)
    cells = cells.reshape(ext, ext, ext * fine)
    low, high = exchange(cells[:halo], cells[ext - halo :], "yz", along_y)
    cells = jnp.concatenate([low, cells, high], axis=0)
    edge = halo * fine
    low, high = exchange(cells[:, :, :edge], cells[:, :, -edge:], "yz", along_z)
    cells = jnp.concatenate([low, cells, high], axis=2)
    low, high = exchange(cells[:, :halo], cells[:, ext - halo :], "gx", around)

    skip, small = call(
        fine_encoder,
        (
            jax.ShapeDtypeStruct((ext + 4, ext + 4, (ext + 4) * fine), BF),
            jax.ShapeDtypeStruct((devices, 112, LANES), BF),
        ),
        [
            pltpu.VMEM((seen, 40, seen * fine), F32),
            pltpu.VMEM((3, seen * 32, seen * fine), BF),
            pltpu.VMEM((3, (seen - 2) * 16, seen * fine), BF),
            pltpu.VMEM((2, side * 16, LANES), F32),
            pltpu.VMEM((112, LANES), F32),
        ],
        low,
        cells,
        high,
        *fine_tabs,
    )

    small, turned = lax.optimization_barrier((small, turned))
    swap = [(s, around(s, 1)) for s in range(cores)]
    swapped = lax.ppermute(turned, "gx", swap)
    own = lax.all_to_all(small, "yz", 0, 0)
    other = lax.ppermute(own, "gx", swap)

    total = side * across
    half = total // 2
    span = total * mid
    window, shrunk = call(
        middle,
        (
            jax.ShapeDtypeStruct((2 * side, 16, 14 * mid), BF),
            jax.ShapeDtypeStruct((side * side, half * mid), BF),
        ),
        [
            pltpu.VMEM((3 * side, 32, span + LANES), F32),
            pltpu.VMEM((3, 3 * side * 16, span + LANES), BF),
            pltpu.VMEM((3 * side - 5, 16, span + 512), BF),
            pltpu.VMEM((2, side * 16, LANES), F32),
            pltpu.VMEM((side * side, half * mid), F32),
        ],
        own,
        other,
        *middle_tabs,
    )
    far_shrunk = lax.ppermute(shrunk, "gx", swap)
    partial = call(
        bottom_start,
        jax.ShapeDtypeStruct((half * side, half * mid), BF),
        [
            pltpu.VMEM((half + 2, 32, half * mid + LANES), F32),
            pltpu.VMEM((3, (half + 2) * 16, half * mid + LANES), BF),
            pltpu.VMEM(table.shape, BF),
            flat,
            pltpu.VMEM((half * side, half * mid), F32),
        ],
        shrunk,
        far_shrunk,
        turned,
        swapped,
    )
    partial, window = lax.optimization_barrier((partial, window))
    far_window = lax.ppermute(window, "gx", swap)

    pieces = [partial] + [
        lax.ppermute(partial, "yz", [(s, s ^ turn) for s in range(devices)])
        for turn in range(1, across)
    ]
    sent = call(
        bottom,
        jax.ShapeDtypeStruct((devices, 88, LANES), BF),
        [
            pltpu.VMEM((half + 2, 32, half * mid + LANES), F32),
            pltpu.VMEM((3, (half + 2) * 16, half * mid + LANES), BF),
            pltpu.VMEM((half + 5, 8, half * mid + 512), F32),
            pltpu.VMEM((88, LANES), F32),
        ],
        *pieces,
        bottom_tab,
    )
    sent, far_window = lax.optimization_barrier((sent, far_window))
    near = lax.all_to_all(sent, "yz", 0, 0)
    far = lax.ppermute(near, "gx", swap)

    risen = call(
        decoder,
        jax.ShapeDtypeStruct((ext, 16, ext * fine), BF),
        [
            pltpu.VMEM((16, 32, 1024), F32),
            pltpu.VMEM((3, 256, 1024), BF),
            pltpu.VMEM((8, 16, 512), F32),
            pltpu.VMEM((8, 16, 32, LANES), F32),
        ],
        near,
        far,
        window,
        far_window,
        skip,
        *decoder_tabs,
    )
    risen = risen[:, :ext].reshape(ext, ext, ext, fine).transpose(3, 1, 0, 2)
    return risen.reshape(1, fine, ext, ext * ext)


def with_halo(cells, sides, width):
    for axis, dim in sides:
        count = lax.axis_size(axis)
        head = lax.slice_in_dim(cells, 0, width, axis=dim)
        tail = lax.slice_in_dim(cells, cells.shape[dim] - width, cells.shape[dim], axis=dim)
        cells = jnp.concatenate(
            [
                lax.ppermute(tail, axis, [(i, (i + 1) % count) for i in range(count)]),
                cells,
                lax.ppermute(head, axis, [((i + 1) % count, i) for i in range(count)]),
            ],
            axis=dim,
        )
    return cells


def shortened(x):
    return jax.tree.map(lambda a: a.astype(jnp.bfloat16) if a.dtype == jnp.float32 else a, x)


def from_behind(block, axis, distance):
    devices = range(lax.axis_size(axis))
    route = [((i - distance) % len(devices), i) for i in devices]
    return lax.ppermute(block, axis, route)


def conv_taps(padded, weight, width_in):
    kernel = weight.reshape(weight.shape[0], width_in, 3, 3, 3)
    return lax.conv_general_dilated(
        padded[None],
        kernel,
        (1, 1, 1),
        "VALID",
        dimension_numbers=("NCDHW", "OIDHW", "NCDHW"),
        preferred_element_type=jnp.float32,
    )[0]


def rectify(running):
    return jnp.maximum(running, 0.0).astype(jnp.bfloat16)


def shrink(region, weight):
    kernel = weight.reshape(weight.shape[0], region.shape[0], 2, 2, 2)
    result = lax.conv_general_dilated(
        region[None],
        kernel,
        (2, 2, 2),
        "VALID",
        dimension_numbers=("NCDHW", "OIDHW", "NCDHW"),
        preferred_element_type=jnp.float32,
    )[0]
    return result.astype(jnp.bfloat16)


def expand(region, weight, skipped):
    width_in, extent_x, extent_y, extent_z = region.shape
    width_out = weight.shape[1] // 8
    columns = lax.dot_general(
        weight,
        region.reshape(width_in, -1),
        (((0,), (0,)), ((), ())),
        preferred_element_type=jnp.float32,
    )
    spread = columns.reshape(width_out, 2, 2, 2, extent_x, extent_y, extent_z).transpose(
        0, 4, 1, 5, 2, 6, 3
    )
    spread = spread.reshape(width_out, 2 * extent_x, 2 * extent_y, 2 * extent_z)
    return (spread + skipped.astype(jnp.float32)).astype(jnp.bfloat16)


def x_margins(region):
    return with_halo(region, (("gx", 1),), 1)


def from_peer(plane, offset):
    return from_behind(shortened(plane), "yz", offset).astype(plane.dtype)


def pad_block(region, across):
    extended = x_margins(region)
    below_face = from_peer(extended[:, :, -1:, :], across)
    above_face = from_peer(extended[:, :, :1, :], -across)
    extended = jnp.concatenate([below_face, extended, above_face], axis=2)
    column = lax.axis_index("yz") % across
    last_plane = extended[:, :, :, -1:]
    first_plane = extended[:, :, :, :1]
    behind = jnp.where(column == 0, from_peer(last_plane, 1 - across), from_peer(last_plane, 1))
    ahead = jnp.where(
        column == across - 1, from_peer(first_plane, across - 1), from_peer(first_plane, -1)
    )
    return jnp.concatenate([behind, extended, ahead], axis=3)


def conv_layer(region, weight, across):
    return rectify(conv_taps(pad_block(region, across), weight, region.shape[0]))


def assemble(stored):
    width_out = stored.shape[0] // 4
    return (
        stored.reshape(4, width_out, stored.shape[1])
        .transpose(1, 0, 2)
        .reshape(width_out, 4 * stored.shape[1])
    )


def bottom_layer(region, weight, across):
    width_in = region.shape[0]
    padded = pad_block(region, across)
    gathered = lax.all_gather(weight, "yz", axis=0, tiled=True)
    return rectify(conv_taps(padded, assemble(gathered), width_in))


def body(
    features_in,
    encode_fine_first,
    encode_fine_second,
    reduce_fine,
    encode_middle_first,
    encode_middle_second,
    reduce_middle,
    bottom_first,
    bottom_second,
    expand_middle,
    decode_middle_first,
    decode_middle_second,
    expand_fine,
    decode_fine_first,
    decode_fine_second,
):
    across = math.isqrt(lax.axis_size("yz"))
    width_fine, extent = (features_in.shape[1], features_in.shape[2])
    region = features_in.reshape(width_fine, extent, extent, extent)
    fine_skip = conv_layer(
        conv_layer(region, encode_fine_first, across), encode_fine_second, across
    )
    middle = shrink(fine_skip, reduce_fine)
    middle_skip = conv_layer(
        conv_layer(middle, encode_middle_first, across), encode_middle_second, across
    )
    bottom = shrink(middle_skip, reduce_middle)
    bottom = bottom_layer(bottom_layer(bottom, bottom_first, across), bottom_second, across)
    rising = expand(bottom, expand_middle, middle_skip)
    rising = conv_layer(
        conv_layer(rising, decode_middle_first, across), decode_middle_second, across
    )
    rising = expand(rising, expand_fine, fine_skip)
    rising = conv_layer(conv_layer(rising, decode_fine_first, across), decode_fine_second, across)
    return rising.reshape(1, width_fine, extent, extent * extent)


def solution(mesh):
    placed = (
        P("yz", None, "gx", None),
        P(),
        P(),
        P(),
        P(),
        P(),
        P(),
        P("yz", None),
        P("yz", None),
        P(),
        P(),
        P(),
        P(),
        P(),
        P(),
    )

    def chosen(*args):
        across = math.isqrt(lax.axis_size("yz"))
        stored, channels = args[7].shape[0], args[4].shape[0]
        gathered = lax.axis_size("gx") == 2 and stored == channels
        gathered = gathered and across == 4 and across * channels == args[6].shape[0]
        return (gathered_body if gathered else body)(*args)

    return jax.shard_map(
        chosen, mesh=mesh, in_specs=placed, out_specs=P("yz", None, "gx", None), check_vma=False
    )
```
